32 devices in a mesh: role: 2 (over core), dev: 16 (over z, y, x).
Axes of the slice: x: 2, y: 2, z: 4, core: 2. Of those that a mesh axis runs over, the one named last changes fastest.
Arguments:
- positions: float32 [256, 3, 512], P(('role', 'dev')), may hold values from -1 to 1
- normals: float32 [256, 3, 512], P(('role', 'dev')), may hold values from -3.6 to 3.6
- panel_areas: float32 [256, 512], P(('role', 'dev')), may hold values from 0.005 to 0.05
- panel_counts: int32 [256], P(('role', 'dev')), may hold values from 128 to 512, as said below
- near_lists: int32 [256, 6], P(('role', 'dev')), may hold values from 0 to 255, as said below
- near_counts: int32 [256], P(('role', 'dev')), may hold values from 1 to 6
- leaf_lists: int32 [256, 16], P(('role', 'dev')), may hold values from 0 to 255, as said below
- leaf_kinds: int32 [256, 16], P(('role', 'dev')), may hold values from 0 to 7
- group_lists: int32 [32, 16], P(('role', 'dev')), may hold values from 0 to 31
- group_kinds: int32 [32, 16], P(('role', 'dev')), may hold values from 0 to 7
- block_inverse: bfloat16 [256, 512, 512], P(('role', 'dev')), may hold values from -1 to 3
- moment_maps: bfloat16 [256, 256, 512], P(('role', 'dev')), may hold values from -0.25 to 0.25
- up_operators: bfloat16 [8, 256, 256], replicated, may hold values from -0.125 to 0.125
- far_operators: bfloat16 [2, 8, 256, 256], replicated, may hold values from -0.09375 to 0.09375
- krylov_basis: float32 [8, 256, 512], P(None, ('role', 'dev')), may hold values from -64 to 64, as said below
Outputs:
- next_vector: float32 [256, 512], P(('role', 'dev'))
- hessenberg_column: float32 [9], replicated
The draws below stay inside these ranges and needn't reach their ends.
Inputs may be any that keep to these rules, and one draw needn't show every extreme that they name: `panel_counts`: some cluster has all 512 panels live. `near_lists`: ids of clusters held by the devices at most 3 places from the cluster's own device along role+dev; entries may repeat. `leaf_lists`: ids of clusters held by the devices at most 3 places from the cluster's own device along role+dev; entries may repeat. `krylov_basis`: the vectors are orthonormal under the mean over all 131072 entries, and zero on panels that are not live.
All inputs are finite; a program needn't handle non-finite values.
Results may differ from the reference program's by a relative error of at most 0.0044.
Values may be sent and summed in bfloat16 or wider, within the bound.
A program may use at most 64 MiB of HBM per device.

```python
import math
import jax
import jax.numpy as jnp
from jax import lax

P_SIZE = 512
C = 256
CL_DEV = 8
NNB = 6
NIL = 16
NOP = 8
KRY = 8
RADIUS = 3
CLUSTERS = 256
GROUPS = 32


def live_counts(key):
    counts = jax.random.randint(jax.random.fold_in(key, 101), (CLUSTERS,), P_SIZE // 4, P_SIZE + 1)
    chosen = jax.random.randint(jax.random.fold_in(key, 102), (), 0, CLUSTERS)
    return jnp.where(jnp.arange(CLUSTERS) == chosen, P_SIZE, counts).astype(jnp.int32)


def draw_panel_counts(key, part):
    return live_counts(key)


def window_lists(key, width):
    owners = jnp.arange(CLUSTERS, dtype=jnp.int32) // CL_DEV
    offsets = jax.random.randint(key, (CLUSTERS, width), 0, (2 * RADIUS + 1) * CL_DEV)
    listed = (owners[:, None] - RADIUS) * CL_DEV + offsets
    return jnp.clip(listed, 0, CLUSTERS - 1).astype(jnp.int32)


def draw_near_lists(key, part):
    return window_lists(jax.random.fold_in(key, 201), NNB)


def draw_leaf_lists(key, part):
    return window_lists(jax.random.fold_in(key, 202), NIL)


def draw_block_inverse(key, part):
    spread_key = jax.random.fold_in(key, 301)
    scale_key = jax.random.fold_in(key, 302)
    spread_part = jnp.clip(0.5 * jax.random.normal(spread_key, (CLUSTERS, P_SIZE, P_SIZE), jnp.float32), -3.0, 3.0)
    spread_part = spread_part * P_SIZE ** (-0.5)
    diagonal = jax.random.uniform(scale_key, (CLUSTERS, P_SIZE), jnp.float32, 1.0, 2.0)
    return (spread_part + diagonal[:, :, None] * jnp.eye(P_SIZE, dtype=jnp.float32)).astype(jnp.bfloat16)


def draw_krylov_basis(key, part):
    counts = live_counts(key)
    live = (jnp.arange(P_SIZE)[None, :] < counts[:, None]).astype(jnp.float32)
    drawn = jax.random.normal(jax.random.fold_in(key, 401), (KRY, CLUSTERS, P_SIZE), jnp.float32)
    drawn = drawn * live[None]
    entries = CLUSTERS * P_SIZE
    vectors = []
    for index_k in range(KRY):
        vector = drawn[index_k]
        for sweep in range(2):
            for earlier in vectors:
                vector = vector - jnp.sum(vector * earlier) / entries * earlier
        vector = vector * jnp.sqrt(entries / jnp.sum(vector * vector))
        vectors.append(vector)
    return jnp.stack(vectors)


def with_ends(values, stream_key, least, top_value):
    place = [jax.random.randint(jax.random.fold_in(stream_key, axis), (), 0, length) for axis, length in enumerate(values.shape)]
    widest = values.shape.index(max(values.shape))
    neighbour = place[:widest] + [(place[widest] + 1) % values.shape[widest]] + place[widest + 1:]
    return values.at[tuple(place)].set(least).at[tuple(neighbour)].set(top_value)


def shard_levels(key, shape, split, least, top_value):
    def one(axis_at, blocks):
        heights = jax.random.uniform(jax.random.fold_in(jax.random.fold_in(key, 6), axis_at), (blocks,), jnp.float32, least / len(split), top_value / len(split))
        return jnp.repeat(jnp.exp(heights), shape[axis_at] // blocks).reshape((-1,) + (1,) * (len(shape) - axis_at - 1))

    level = one(*split[0])
    for cut in split[1:]:
        level = level * one(*cut)
    return level


def noise(own_key, extent, scale, limit, cuts=(), held_as=jnp.bfloat16):
    result = jax.random.normal(own_key, extent, jnp.float32) * scale
    if len(cuts) > 0:
        result = shard_levels(own_key, extent, cuts, -0.22, 0.18) * result
    return jnp.clip(result, min=-limit, max=limit).astype(held_as)


def setup_inputs(seed: int = 0) -> dict:
    seeds = jax.random.split(jax.random.key(seed), 16)
    return {
        "positions": jnp.clip(jax.random.uniform(seeds[0], (CLUSTERS, 3, P_SIZE), jnp.float32, -1.0, 1.0) * shard_levels(seeds[0], (CLUSTERS, 3, P_SIZE), ((0, 32),), -0.4, 0.0), -1.0, 1.0),
        "normals": noise(seeds[1], (CLUSTERS, 3, P_SIZE), 0.6, 3.6, ((0, 32),), jnp.float32),
        "panel_areas": jnp.clip(jnp.exp(math.log(0.05) - 2.3025851 * jax.random.uniform(seeds[2], (CLUSTERS, P_SIZE), jnp.float32) ** shard_levels(seeds[2], (CLUSTERS, P_SIZE), ((0, 32),), -0.2, 0.2)), 0.005, 0.05),
        "panel_counts": draw_panel_counts(jax.random.fold_in(seeds[15], 71), 0),
        "near_lists": draw_near_lists(jax.random.fold_in(seeds[15], 71), 0),
        "near_counts": with_ends(jax.random.randint(seeds[5], (CLUSTERS,), 1, NNB + 1), jax.random.fold_in(seeds[5], 1), 1, NNB).astype(jnp.int32),
        "leaf_lists": draw_leaf_lists(jax.random.fold_in(seeds[15], 71), 0),
        "leaf_kinds": with_ends(jax.random.randint(seeds[7], (CLUSTERS, NIL), 0, NOP), jax.random.fold_in(seeds[7], 1), 0, NOP - 1).astype(jnp.int32),
        "group_lists": with_ends(jax.random.randint(seeds[8], (GROUPS, NIL), 0, GROUPS), jax.random.fold_in(seeds[8], 1), 0, GROUPS - 1).astype(jnp.int32),
        "group_kinds": with_ends(jax.random.randint(seeds[9], (GROUPS, NIL), 0, NOP), jax.random.fold_in(seeds[9], 1), 0, NOP - 1).astype(jnp.int32),
        "block_inverse": draw_block_inverse(jax.random.fold_in(seeds[15], 71), 0),
        "moment_maps": noise(seeds[11], (CLUSTERS, C, P_SIZE), P_SIZE ** -0.5, 0.25, ((0, 32),)),
        "up_operators": noise(seeds[12], (8, C, C), (8 * C) ** -0.5, 0.125),
        "far_operators": noise(seeds[13], (2, NOP, C, C), (C * NIL) ** -0.5, 0.09375),
        "krylov_basis": draw_krylov_basis(jax.random.fold_in(seeds[15], 71), 0),
    }


SOFTEN = 0.01
EPSILON = 1e-06
HIGH = lax.Precision.HIGHEST

def near_cluster(operands):
    target, sources = operands
    square = jnp.full((sources.shape[0], target.shape[1], sources.shape[2]), SOFTEN, jnp.float32)
    projected = jnp.zeros((sources.shape[0], target.shape[1], sources.shape[2]), jnp.float32)
    for component in range(3):
        offsets = target[component][None, :, None] - sources[:, component][:, None, :]
        square = square + offsets * offsets
        projected = projected + offsets * sources[:, 3 + component][:, None, :]
    inverse = lax.rsqrt(square)
    return lax.optimization_barrier(jnp.sum(projected * inverse * inverse * inverse, axis=(0, 2)))

def translate(chosen, kind_ids, operators):
    onehot = (kind_ids[:, :, None] == jnp.arange(operators.shape[0], dtype=jnp.int32)[None, None, :]).astype(jnp.float32)
    summed = jnp.einsum('gno,gnc->goc', onehot, chosen, precision=HIGH)
    return jnp.einsum('goc,oqc->gq', summed, operators, precision=HIGH)

def precond_one(operands):
    matrix, vector = operands
    return jnp.dot(matrix, vector, preferred_element_type=jnp.float32)

def back_one(operands):
    matrix, vector = operands
    return jnp.dot(vector, matrix, preferred_element_type=jnp.float32)

def reference(positions, normals, panel_areas, panel_counts, near_lists, near_counts, leaf_lists, leaf_kinds, group_lists, group_kinds, block_inverse, moment_maps, up_operators, far_operators, krylov_basis):
    live = (jnp.arange(P_SIZE, dtype=jnp.int32)[None, :] < panel_counts[:, None]).astype(jnp.float32)
    current = krylov_basis[KRY - 1].astype(jnp.bfloat16)
    density = (live * lax.map(precond_one, (block_inverse, current))).astype(jnp.bfloat16)
    density_wide = density.astype(jnp.float32)
    weighted = (panel_areas * density_wide)[:, None, :] * normals
    sources = jnp.concatenate([positions, weighted], axis=1)
    slot_ids = jnp.concatenate([jnp.arange(CLUSTERS, dtype=jnp.int32)[:, None], near_lists.astype(jnp.int32)], axis=1)
    slot_live = (jnp.arange(NNB + 1, dtype=jnp.int32)[None, :] <= near_counts[:, None]).astype(jnp.float32)

    def near_one(operands):
        target, slots, alive = operands
        return near_cluster((target, sources[slots] * alive[:, None, None]))
    near_field = lax.map(near_one, (positions, slot_ids, slot_live))
    moments = lax.map(precond_one, (moment_maps, density)).astype(jnp.bfloat16)
    up_wide = up_operators.astype(jnp.float32)
    far_wide = far_operators.astype(jnp.float32)
    children = moments.astype(jnp.float32).reshape(GROUPS, 8, C)
    group_moments = jnp.einsum('gkc,kqc->gq', children, up_wide, precision=HIGH)
    group_local = translate(group_moments[group_lists], group_kinds, far_wide[1]).astype(jnp.bfloat16)
    downward = jnp.einsum('gq,kqc->gkc', group_local.astype(jnp.float32), up_wide, precision=HIGH).reshape(CLUSTERS, C)
    leaf_local = (translate(moments[leaf_lists].astype(jnp.float32), leaf_kinds, far_wide[0]) + downward).astype(jnp.bfloat16)
    far_field = lax.map(back_one, (moment_maps, leaf_local))
    image = live * (0.5 * density_wide + near_field + far_field)
    entries = CLUSTERS * P_SIZE
    coeffs = jnp.einsum('kcp,cp->k', krylov_basis, image, precision=HIGH) / entries
    remainder = image - jnp.einsum('k,kcp->cp', coeffs, krylov_basis, precision=HIGH)
    height = jnp.sqrt(jnp.sum(remainder * remainder) / entries + EPSILON)
    return (remainder / height, jnp.concatenate([coeffs, height[None]]))
```

```python
import functools

import jax
import jax.numpy as jnp
from jax import lax
from jax.experimental import pallas as pl
from jax.experimental.pallas import tpu as pltpu
from jax.sharding import PartitionSpec as P

RADIUS = 3
SIDES = 2 * RADIUS + 1
SOFTEN = 0.01
EPSILON = 1e-06
UNITS = 24
MESH = pl.DeviceIdType.MESH
NT = (((1,), (1,)), ((), ()))
NN = (((1,), (0,)), ((), ()))
TN = (((0,), (0,)), ((), ()))
F32 = jnp.float32
BF16 = jnp.bfloat16
AXES = ("role", "dev")


def mm(a, b, dims):
    return lax.dot_general(a, b, dims, preferred_element_type=F32)


def row_is(shape, k):
    return lax.broadcasted_iota(jnp.int32, shape, 0) == k


def place(roles, devs):
    me = lax.axis_index("role") * devs + lax.axis_index("dev")
    return me, roles * devs


def coords(linear, devs):
    return (linear // devs, lax.rem(linear, devs))


def greet(me, total, devs):
    barrier = pltpu.get_barrier_semaphore()

    def body(i, carry):
        pl.semaphore_signal(
            barrier,
            inc=1,
            device_id=coords(lax.rem(me + i, total), devs),
            device_id_type=MESH,
        )
        return carry

    lax.fori_loop(1, total, body, 0)
    return barrier


def live_mask(cnt_ref, shape):
    rows = lax.broadcasted_iota(jnp.int32, shape, 0)
    limit = jnp.zeros(shape, jnp.int32)
    for c in range(shape[0]):
        limit = jnp.where(rows == c, cnt_ref[c], limit)
    return lax.broadcasted_iota(jnp.int32, shape, 1) < limit


def halves(x):
    hi = x.astype(BF16).astype(F32)
    return jnp.concatenate([hi, x - hi], axis=0).astype(BF16)


def source_kernel(
    roles,
    devs,
    cnt,
    pos,
    nrm,
    area,
    kry,
    binv,
    maps,
    ups,
    posw,
    anw,
    cntw,
    momw,
    gmall,
    nrm_v,
    area_v,
    kry_v,
    binv_v,
    maps_v,
    ups_v,
    local_sem,
    big_sem,
    send_sem,
    recv_sem,
    gsend,
    grecv,
):
    me, total = place(roles, devs)
    local, panels = area.shape
    coeffs = maps_v.shape[1]
    copies = []
    for c in range(local):
        copies.append(pltpu.make_async_copy(binv.at[c], binv_v.at[c], big_sem.at[c]))
    map_copy = pltpu.make_async_copy(maps, maps_v, local_sem.at[0])
    up_copy = pltpu.make_async_copy(ups, ups_v, local_sem.at[1])
    small = [
        pltpu.make_async_copy(pos, posw.at[RADIUS], local_sem.at[2]),
        pltpu.make_async_copy(nrm, nrm_v, local_sem.at[3]),
        pltpu.make_async_copy(area, area_v, local_sem.at[4]),
        pltpu.make_async_copy(kry.at[kry.shape[0] - 1], kry_v, local_sem.at[5]),
    ]
    for copy in small + copies:
        copy.start()
    map_copy.start()
    up_copy.start()
    barrier = greet(me, total, devs)
    for copy in small:
        copy.wait()
    parts = [nrm_v[a] * area_v[...] for a in range(3)]
    anw[RADIUS, : 3 * local] = jnp.concatenate(parts, axis=0).astype(BF16)
    lane = lax.broadcasted_iota(jnp.int32, (1, 128), 1)
    counts = jnp.zeros((1, 128), jnp.int32)
    for c in range(local):
        counts = jnp.where(lane == c, cnt[c], counts)
    cntw[RADIUS] = counts
    pl.semaphore_wait(barrier, total - 1)

    def to_neighbours(ref, kind, rows=None):
        made = []

        def slot(side):
            return ref.at[side] if rows is None else ref.at[side, rows]

        for n, d in enumerate([1, -1, 2, -2, 3, -3]):
            made.append(
                pltpu.make_async_remote_copy(
                    src_ref=slot(RADIUS),
                    dst_ref=slot(RADIUS - d),
                    send_sem=send_sem.at[kind, n],
                    recv_sem=recv_sem.at[kind, n],
                    device_id=coords(lax.rem(me + d + total, total), devs),
                    device_id_type=MESH,
                )
            )
        for copy in made:
            copy.start()
        return made

    sent = to_neighbours(posw, 0) + to_neighbours(anw, 4, pl.ds(0, 3 * local)) + to_neighbours(cntw, 1)
    live = live_mask(cnt, (local, panels))
    current = kry_v[...].astype(BF16)
    density = jnp.zeros((local, panels), F32)
    for c in range(local):
        copies[c].wait()
        found = mm(current, binv_v[c], NT)
        density = jnp.where(row_is(found.shape, c), found, density)
    rounded = jnp.where(live, density, 0.0).astype(BF16)
    anw[RADIUS, 3 * local :] = rounded
    sent += to_neighbours(anw, 2, pl.ds(3 * local, local))
    map_copy.wait()
    moments = jnp.zeros((local, coeffs), F32)
    for c in range(local):
        found = mm(rounded, maps_v[c], NT)
        moments = jnp.where(row_is(found.shape, c), found, moments)
    moments = moments.astype(BF16)
    momw[RADIUS] = moments
    sent += to_neighbours(momw, 3)
    up_copy.wait()
    merged = jnp.zeros((local, coeffs), F32)
    for k in range(local):
        found = mm(moments, ups_v[k], NT)
        merged = jnp.where(row_is(found.shape, k), found, merged)
    gmall[me] = jnp.sum(merged, axis=0, keepdims=True)

    def group_copy(i):
        return pltpu.make_async_remote_copy(
            src_ref=gmall.at[me],
            dst_ref=gmall.at[me],
            send_sem=gsend.at[i],
            recv_sem=grecv.at[i],
            device_id=coords(lax.rem(me + i, total), devs),
            device_id_type=MESH,
        )

    def start_one(i, carry):
        group_copy(i).start()
        return carry

    def wait_one(i, carry):
        source = lax.rem(me - i + total, total)
        pltpu.make_async_remote_copy(
            src_ref=gmall.at[me],
            dst_ref=gmall.at[source],
            send_sem=gsend.at[i],
            recv_sem=grecv.at[i],
            device_id=coords(lax.rem(me + i, total), devs),
            device_id_type=MESH,
        ).wait()
        return carry

    lax.fori_loop(1, total, start_one, 0)
    for copy in sent:
        copy.wait()
    lax.fori_loop(1, total, wait_one, 0)


def splits(x):
    hi = x.astype(BF16).astype(F32)
    rest = x - hi
    mid = rest.astype(BF16).astype(F32)
    return hi, mid, rest - mid


def near_kernel(
    first,
    near,
    used,
    cnt,
    cntw,
    posw,
    anw,
    out,
    feat,
    goal,
    src,
    wgt,
    sq0,
    sq1,
    g0,
    g1,
    acc,
    begin,
    spans,
):
    local, panels = out.shape
    wide = goal.shape[2]
    shape = (8, panels)
    rows = lax.broadcasted_iota(jnp.int32, shape, 0)
    chunks = panels // 128

    def spread(side, k, value):
        for b in range(chunks):
            feat[side, b, pl.ds(k, local, stride=8), :] = value[:, b * 128 : (b + 1) * 128]

    for side in range(SIDES):
        products_an = anw[side].astype(F32)
        dens = products_an[3 * local :]
        norm = jnp.zeros((local, panels), F32)
        inside = jnp.zeros((local, panels), F32)
        for a in range(3):
            y = posw[side, a]
            w = products_an[a * local : (a + 1) * local] * dens
            norm = norm + y * y
            inside = inside - y * w
            spread(side, a, y)
            spread(side, 4 + a, w)
        spread(side, 3, norm)
        spread(side, 7, inside)

    def features(side, inner):
        at = pl.ds(pl.multiple_of(inner * 8, 8), 8)
        return jnp.concatenate([feat[side, b, at, :] for b in range(chunks)], axis=1)

    def pack(parts):
        return jnp.concatenate(parts, axis=0).astype(BF16)

    zero = jnp.zeros(shape, F32)
    halves_of = panels // wide

    def cluster_body(c, start):
        own = features(RADIUS, c)
        x = jnp.where(rows < 3, -2.0 * own, jnp.where(rows == 3, own + SOFTEN, 0.0))
        hi, mid, low = splits(x)
        norms = [jnp.broadcast_to(part[3:4], shape) for part in (hi, mid, low)]
        firm = jnp.where(rows < 3, hi, jnp.where(rows == 3, 1.0, 0.0))
        soft = jnp.where(rows < 3, mid, 0.0)
        last = jnp.where(rows < 3, low, 0.0)
        tail = soft
        for k in range(3):
            tail = jnp.where(rows == 4 + k, norms[k], tail)
        made = pack([firm, firm, firm, soft, last, tail])
        for h in range(halves_of):
            goal[halves_of * c + h] = made[:, h * wide : (h + 1) * wide]

        def slot_body(s, offset):
            listed = near[c, jnp.maximum(s - 1, 0)] - first[0]
            w = jnp.where(s == 0, RADIUS * local + c, listed)
            side = w // local
            inner = lax.rem(w, local)
            hi, mid, low = splits(features(side, inner))
            ones = jnp.where(rows < 4, mid, 1.0)
            made = pack([hi, mid, low, hi, hi, ones])
            pulled = pack([jnp.where(rows < 4, pltpu.roll(mid, 4, 0), hi), low])
            for b in range(panels // 128):
                src[offset + b] = made[:, b * 128 : (b + 1) * 128]
                wgt[offset + b] = pulled[:, b * 128 : (b + 1) * 128]
            return offset + (cntw[side, 0, inner] + 127) // 128

        end = lax.fori_loop(0, used[c] + 1, slot_body, start)
        pad_rows = lax.broadcasted_iota(jnp.int32, (48, 128), 0)
        src[end] = jnp.where(pad_rows >= 44, 1.0, 0.0).astype(BF16)
        wgt[end] = jnp.zeros((16, 128), BF16)
        stop = (end + 1) // 2 * 2
        begin[c] = start // 2
        spans[c] = (cnt[c] + wide - 1) // wide
        return stop

    end = lax.fori_loop(0, local, cluster_body, 0)
    begin[local] = end // 2
    begin[local + 1] = end // 2
    spans[local] = 1
    acc[...] = jnp.zeros(acc.shape, F32)

    def advance(state):
        c, h, b = state
        over = b + 1 >= begin[jnp.minimum(c + 1, local)]
        h = jnp.where(over, h + 1, h)
        done = h >= spans[c]
        b = jnp.where(over, begin[c], b + 1)
        c_next = jnp.where(done, jnp.minimum(c + 1, local), c)
        b = jnp.where(done, begin[c_next], b)
        return c_next, jnp.where(done, 0, h), b

    def products(state, ref):
        c, h, b = state
        target = goal[halves_of * c + h]
        for k in range(2):
            ref[k * 128 : (k + 1) * 128, :] = mm(src[2 * b + k], target, TN)

    def consume(state, ref):
        c, h, b = state
        cube = ref[...]
        both = jnp.concatenate([wgt[2 * b], wgt[2 * b + 1]], axis=1)
        acc[halves_of * c + h] += mm(both, cube, NN)

    def count_body(c, total):
        return total + spans[c] * (begin[c + 1] - begin[c])

    units = lax.fori_loop(0, local, count_body, 0)
    origin = (jnp.int32(0), jnp.int32(0), jnp.int32(0))
    products(origin, sq0)

    def middle(a, b):
        inverse = lax.rsqrt(a[...])
        b[...] = (inverse * inverse * inverse).astype(BF16)

    def body(t, states):
        old, state = states
        for u in range(UNITS):
            later = advance(state)
            products(later, (sq0, sq1)[u % 2])
            middle((sq1, sq0)[u % 2], (g1, g0)[u % 2])
            consume(old, (g0, g1)[u % 2])
            old, state = state, later
        return old, state

    middle(sq0, g0)
    second = advance(origin)
    products(second, sq1)
    lax.fori_loop(0, (units + UNITS - 1) // UNITS, body, (origin, second))
    for c in range(local):
        own = features(RADIUS, c)
        for h in range(halves_of):
            got = acc[halves_of * c + h]
            total = got[:8] + pltpu.roll(got[:8], 4, 0) + got[8:]
            part = own[:, h * wide : (h + 1) * wide]
            x = pltpu.roll(part, 4, 0)
            keep = rows[:, :wide]
            value = jnp.where(keep < 4, 0.0, jnp.where(keep == 7, total, total * x))
            out[c : c + 1, h * wide : (h + 1) * wide] = jnp.sum(value, axis=0, keepdims=True)


def finish_kernel(
    roles,
    devs,
    cnt,
    glist,
    gkind,
    llist,
    lkind,
    momw,
    gmall,
    near,
    anw,
    kry,
    maps_v,
    ups_v,
    fars_v,
    nxt,
    hess,
    red,
    send_sem,
    recv_sem,
):
    me, total = place(roles, devs)
    local, panels = near.shape
    coeffs = maps_v.shape[1]
    kinds = fars_v.shape[1]
    window = SIDES * local
    barrier = greet(me, total, devs)

    groups = gmall[...].reshape(total, coeffs)
    g_rows = lax.broadcasted_iota(jnp.int32, (kinds, total), 0)
    g_lanes = lax.broadcasted_iota(jnp.int32, (kinds, total), 1)
    g_hot = jnp.zeros((kinds, total), F32)
    for n in range(glist.shape[1]):
        g_hot += jnp.where((g_rows == gkind[0, n]) & (g_lanes == glist[0, n]), 1.0, 0.0)
    g_hot = g_hot.astype(BF16)
    hi, mid, low = splits(groups)
    g_sum = mm(g_hot, hi.astype(BF16), NN) + mm(g_hot, mid.astype(BF16), NN)
    g_sum += mm(g_hot, low.astype(BF16), NN)
    g_both = halves(g_sum)

    lanes = lax.broadcasted_iota(jnp.int32, (local, window), 1)
    base = (me - RADIUS) * local
    hots = [jnp.zeros((local, window), F32) for _ in range(kinds)]
    for n in range(llist.shape[1]):
        hit = lanes == (llist[:, n : n + 1] - base)
        kind = jnp.broadcast_to(lkind[:, n : n + 1], (local, window))
        for o in range(kinds):
            hots[o] = hots[o] + jnp.where(hit & (kind == o), 1.0, 0.0)
    hot = jnp.concatenate(hots, axis=0).astype(BF16)
    held = jnp.concatenate([momw[side].astype(F32) for side in range(SIDES)], axis=0)
    summed = mm(hot, held.astype(BF16), NN)

    g_parts = jnp.zeros((kinds, coeffs), F32)
    for o in range(kinds):
        found = mm(g_both, fars_v[1, o], NT)
        found = found[:kinds] + found[kinds:]
        g_parts = jnp.where(row_is(found.shape, o), found, g_parts)
    g_local = jnp.sum(g_parts, axis=0, keepdims=True).astype(BF16)
    leaf = jnp.zeros((local, coeffs), F32)
    for o in range(kinds):
        found = mm(halves(summed[o * local : (o + 1) * local]), fars_v[0, o], NT)
        leaf = leaf + found[:local] + found[local:]
    g_wide = jnp.broadcast_to(g_local.astype(F32), (local, coeffs)).astype(BF16)
    down = jnp.zeros((local, coeffs), F32)
    for k in range(local):
        found = mm(g_wide, ups_v[k], NN)
        down = jnp.where(row_is(found.shape, k), found, down)
    leaf = (leaf + down).astype(BF16)
    far = jnp.zeros((local, panels), F32)
    for c in range(local):
        found = mm(leaf, maps_v[c], NN)
        far = jnp.where(row_is(found.shape, c), found, far)
    live = live_mask(cnt, (local, panels))
    image = jnp.where(live, 0.5 * anw[RADIUS].astype(F32)[3 * local :] + near[...] + far, 0.0)

    lane = lax.broadcasted_iota(jnp.int32, (1, 128), 1)
    count = kry.shape[0]
    row = jnp.zeros((1, 128), F32)
    for k in range(count + 1):
        part = image * (kry[k] if k < count else image)
        value = jnp.sum(jnp.sum(part, axis=0, keepdims=True), axis=1, keepdims=True)
        row = jnp.where(lane == k, value, row)
    red[me] = row
    pl.semaphore_wait(barrier, total - 1)

    def one(i):
        source = lax.rem(me - i + total, total)
        target = coords(lax.rem(me + i, total), devs)

        def copy(dst):
            return pltpu.make_async_remote_copy(
                src_ref=red.at[me],
                dst_ref=red.at[dst],
                send_sem=send_sem.at[i],
                recv_sem=recv_sem.at[i],
                device_id=target,
                device_id_type=MESH,
            )

        return copy, source

    def start_one(i, carry):
        one(i)[0](me).start()
        return carry

    def wait_one(i, carry):
        copy, source = one(i)
        copy(source).wait()
        return carry

    lax.fori_loop(1, total, start_one, 0)
    lax.fori_loop(1, total, wait_one, 0)
    scale = 1.0 / (total * local * panels)
    sums = jnp.sum(red[...], axis=0) * scale
    rest = image
    energy = sums[:, count : count + 1]
    for k in range(count):
        c_k = sums[:, k : k + 1]
        rest = rest - c_k * kry[k]
        energy = energy - c_k * c_k
    height = jnp.sqrt(energy + EPSILON)
    nxt[...] = rest / height
    hess[...] = jnp.where(lane == count, height, sums)[:, : count + 1]


def shards(
    roles,
    devs,
    positions,
    normals,
    panel_areas,
    panel_counts,
    near_lists,
    near_counts,
    leaf_lists,
    leaf_kinds,
    group_lists,
    group_kinds,
    block_inverse,
    moment_maps,
    up_operators,
    far_operators,
    krylov_basis,
):
    local, _, panels = positions.shape
    coeffs = moment_maps.shape[1]
    total = roles * devs
    vmem = pl.BlockSpec(memory_space=pltpu.VMEM)
    smem = pl.BlockSpec(memory_space=pltpu.SMEM)
    hbm = pl.BlockSpec(memory_space=pltpu.HBM)
    dma = pltpu.SemaphoreType.DMA
    posw, anw, cntw, momw, gmall = pl.pallas_call(
        functools.partial(source_kernel, roles, devs),
        name="sources",
        out_shape=(
            jax.ShapeDtypeStruct((SIDES, 3, local, panels), F32),
            jax.ShapeDtypeStruct((SIDES, 4 * local, panels), BF16),
            jax.ShapeDtypeStruct((SIDES, 1, 128), jnp.int32),
            jax.ShapeDtypeStruct((SIDES, local, coeffs), BF16),
            jax.ShapeDtypeStruct((total, 1, coeffs), F32),
        ),
        in_specs=[smem] + [hbm] * 7,
        out_specs=(vmem,) * 5,
        scratch_shapes=[
            pltpu.VMEM((3, local, panels), F32),
            pltpu.VMEM((local, panels), F32),
            pltpu.VMEM((local, panels), F32),
            pltpu.VMEM(block_inverse.shape, BF16),
            pltpu.VMEM(moment_maps.shape, BF16),
            pltpu.VMEM(up_operators.shape, BF16),
            dma((6,)),
            dma((local,)),
            dma((5, 6)),
            dma((5, 6)),
            dma((total,)),
            dma((total,)),
        ],
        compiler_params=pltpu.CompilerParams(
            collective_id=0, has_side_effects=True, vmem_limit_bytes=62 << 20
        ),
    )(
        panel_counts,
        jnp.transpose(positions, (1, 0, 2)),
        jnp.transpose(normals, (1, 0, 2)),
        panel_areas,
        krylov_basis,
        block_inverse,
        moment_maps,
        up_operators,
    )
    own = lax.axis_index(AXES)
    first = jnp.reshape((own - RADIUS) * local, (1,)).astype(jnp.int32)
    wide = 256
    room = local * ((near_lists.shape[1] + 1) * (panels // 128) + 1) + 8
    goals = (local + 1) * (panels // wide)
    near = pl.pallas_call(
        near_kernel,
        name="near",
        cost_estimate=pl.CostEstimate(
            flops=40 * local * panels * panels * (near_lists.shape[1] + 1),
            bytes_accessed=48 * local * panels * SIDES,
            transcendentals=local * panels * panels * (near_lists.shape[1] + 1),
        ),
        out_shape=jax.ShapeDtypeStruct((local, panels), F32),
        in_specs=[smem, smem, smem, smem, smem, vmem, vmem],
        out_specs=vmem,
        scratch_shapes=[
            pltpu.VMEM((SIDES, panels // 128, 8 * local, 128), F32),
            pltpu.VMEM((goals, 48, wide), BF16),
            pltpu.VMEM((room, 48, 128), BF16),
            pltpu.VMEM((room, 16, 128), BF16),
            pltpu.VMEM((256, wide), F32),
            pltpu.VMEM((256, wide), F32),
            pltpu.VMEM((256, wide), BF16),
            pltpu.VMEM((256, wide), BF16),
            pltpu.VMEM((goals, 16, wide), F32),
            pltpu.SMEM((local + 2,), jnp.int32),
            pltpu.SMEM((local + 2,), jnp.int32),
        ],
        compiler_params=pltpu.CompilerParams(vmem_limit_bytes=14 << 20),
    )(first, near_lists, near_counts, panel_counts, cntw, posw, anw)
    nxt, hess = pl.pallas_call(
        functools.partial(finish_kernel, roles, devs),
        name="finish",
        out_shape=(
            jax.ShapeDtypeStruct((local, panels), F32),
            jax.ShapeDtypeStruct((1, krylov_basis.shape[0] + 1), F32),
        ),
        in_specs=[smem, smem, smem] + [vmem] * 10,
        out_specs=(vmem, vmem),
        scratch_shapes=[
            pltpu.VMEM((total, 1, 128), F32),
            dma((total,)),
            dma((total,)),
        ],
        compiler_params=pltpu.CompilerParams(
            collective_id=1, has_side_effects=True, vmem_limit_bytes=14 << 20
        ),
    )(
        panel_counts,
        group_lists,
        group_kinds,
        leaf_lists,
        leaf_kinds,
        momw,
        gmall,
        near,
        anw,
        krylov_basis,
        moment_maps,
        up_operators,
        far_operators,
    )
    return nxt, jnp.reshape(hess, (krylov_basis.shape[0] + 1,))


def solution(mesh):
    roles, devs = mesh.shape["role"], mesh.shape["dev"]
    return jax.shard_map(
        functools.partial(shards, roles, devs),
        mesh=mesh,
        in_specs=(
            P(AXES, None, None),
            P(AXES, None, None),
            P(AXES, None),
            P(AXES),
            P(AXES, None),
            P(AXES),
            P(AXES, None),
            P(AXES, None),
            P(AXES, None),
            P(AXES, None),
            P(AXES, None, None),
            P(AXES, None, None),
            P(),
            P(),
            P(None, AXES, None),
        ),
        out_specs=(P(AXES, None), P()),
        check_vma=False,
    )
```

```python
import functools

import jax
import jax.numpy as jnp
from jax import lax
from jax.experimental import pallas as pl
from jax.experimental.pallas import tpu as pltpu
from jax.sharding import PartitionSpec as P

RADIUS = 3
SIDES = 2 * RADIUS + 1
SOFTEN = 0.01
EPSILON = 1e-06
UNITS = 24
SPARE = 12 << 20
MESH = pl.DeviceIdType.MESH
NT = (((1,), (1,)), ((), ()))
NN = (((1,), (0,)), ((), ()))
TN = (((0,), (0,)), ((), ()))
F32 = jnp.float32
BF16 = jnp.bfloat16
AXES = ("role", "dev")


def mm(a, b, dims):
    return lax.dot_general(a, b, dims, preferred_element_type=F32)


def row_is(shape, k):
    return lax.broadcasted_iota(jnp.int32, shape, 0) == k


def place(roles, devs):
    me = lax.axis_index("role") * devs + lax.axis_index("dev")
    return me, roles * devs


def coords(linear, devs):
    return (linear // devs, lax.rem(linear, devs))


def greet(me, total, devs):
    barrier = pltpu.get_barrier_semaphore()

    def body(i, carry):
        pl.semaphore_signal(
            barrier,
            inc=1,
            device_id=coords(lax.rem(me + i, total), devs),
            device_id_type=MESH,
        )
        return carry

    lax.fori_loop(1, total, body, 0)
    return barrier


def live_mask(cnt_ref, shape):
    rows = lax.broadcasted_iota(jnp.int32, shape, 0)
    limit = jnp.zeros(shape, jnp.int32)
    for c in range(shape[0]):
        limit = jnp.where(rows == c, cnt_ref[c], limit)
    return lax.broadcasted_iota(jnp.int32, shape, 1) < limit


def halves(x):
    hi = x.astype(BF16).astype(F32)
    return jnp.concatenate([hi, x - hi], axis=0).astype(BF16)


def splits(x):
    hi = x.astype(BF16).astype(F32)
    rest = x - hi
    mid = rest.astype(BF16).astype(F32)
    return hi, mid, rest - mid


def pack(parts):
    return jnp.concatenate(parts, axis=0).astype(BF16)


def spread_all(feat, positions, weights):
    local, panels = positions[0].shape
    norm = jnp.zeros((local, panels), F32)
    inside = jnp.zeros((local, panels), F32)
    for y, w in zip(positions, weights):
        norm = norm + y * y
        inside = inside - y * w
    rows = list(positions) + [norm] + list(weights) + [inside]
    for k, value in enumerate(rows):
        for b in range(panels // 128):
            feat[b, pl.ds(k, local, stride=8), :] = value[:, b * 128 : (b + 1) * 128]


def read_features(feat, inner):
    at = pl.ds(pl.multiple_of(inner * 8, 8), 8)
    return jnp.concatenate([feat[b, at, :] for b in range(feat.shape[0])], axis=1)


def goal_rows(own):
    shape = own.shape
    rows = lax.broadcasted_iota(jnp.int32, shape, 0)
    x = jnp.where(rows < 3, -2.0 * own, jnp.where(rows == 3, own + SOFTEN, 0.0))
    hi, mid, low = splits(x)
    norms = [jnp.broadcast_to(part[3:4], shape) for part in (hi, mid, low)]
    firm = jnp.where(rows < 3, hi, jnp.where(rows == 3, 1.0, 0.0))
    soft = jnp.where(rows < 3, mid, 0.0)
    last = jnp.where(rows < 3, low, 0.0)
    tail = soft
    for k in range(3):
        tail = jnp.where(rows == 4 + k, norms[k], tail)
    return pack([firm, firm, firm, soft, last, tail])


def source_rows(own):
    rows = lax.broadcasted_iota(jnp.int32, own.shape, 0)
    hi, mid, low = splits(own)
    made = pack([hi, mid, low, hi, hi, jnp.where(rows < 4, mid, 1.0)])
    return made, pack([jnp.where(rows < 4, pltpu.roll(mid, 4, 0), hi), low])


def squares(src, block, target, ref):
    for k in range(2):
        ref[k * 128 : (k + 1) * 128, :] = mm(src[2 * block + k], target, TN)


def cubes(a, b):
    inverse = lax.rsqrt(a[...])
    b[...] = (inverse * inverse * inverse).astype(BF16)


def gathered(wgt, block, ref):
    both = jnp.concatenate([wgt[2 * block], wgt[2 * block + 1]], axis=1)
    return mm(both, ref[...], NN)


def combine(own, got):
    total = got[:8] + pltpu.roll(got[:8], 4, 0) + got[8:]
    rows = lax.broadcasted_iota(jnp.int32, total.shape, 0)
    part = total * pltpu.roll(own, 4, 0)
    value = jnp.where(rows < 4, 0.0, jnp.where(rows == 7, total, part))
    return jnp.sum(value, axis=0, keepdims=True)


def own_near(pos_v, nrm_parts, density, feat, goal, src, wgt, sqs, gs, acc, out):
    local, panels = density.shape
    wide = goal.shape[2]
    per_h = panels // wide
    blocks = panels // 256
    positions = [pos_v[a] for a in range(3)]
    spread_all(feat, positions, [part * density for part in nrm_parts])
    for c in range(local):
        own = read_features(feat, c)
        made = goal_rows(own)
        for h in range(per_h):
            goal[per_h * c + h] = made[:, h * wide : (h + 1) * wide]
        made, pulled = source_rows(own)
        for b in range(panels // 128):
            src[2 * blocks * c + b] = made[:, b * 128 : (b + 1) * 128]
            wgt[2 * blocks * c + b] = pulled[:, b * 128 : (b + 1) * 128]
    acc[...] = jnp.zeros(acc.shape, F32)
    units = local * per_h * blocks

    def place_of(n):
        n = lax.rem(n, units)
        c = n // (per_h * blocks)
        return n // blocks, c * blocks + lax.rem(n, blocks)

    def start(n, ref):
        g, b = place_of(n)
        squares(src, b, goal[g], ref)

    start(0, sqs[0])
    cubes(sqs[0], gs[0])
    start(1, sqs[1])
    steps = 16

    def body(t, carry):
        for u in range(steps):
            n = t * steps + u
            start(n + 2, sqs[u % 2])
            cubes(sqs[(u + 1) % 2], gs[(u + 1) % 2])
            g, b = place_of(n)
            acc[g] += gathered(wgt, b, gs[u % 2])
        return carry

    lax.fori_loop(0, units // steps, body, 0)
    for c in range(local):
        own = read_features(feat, c)
        for h in range(per_h):
            part = slice(h * wide, (h + 1) * wide)
            out[c : c + 1, part] = out[c : c + 1, part] + combine(own[:, part], acc[per_h * c + h])


def source_kernel(
    roles,
    devs,
    cnt,
    near,
    used,
    pos,
    nrm,
    area,
    kry,
    binv,
    maps,
    ups,
    posw,
    anw,
    cntw,
    momw,
    gmall,
    base,
    pos_v,
    an_v,
    cnt_v,
    info_v,
    nrm_v,
    area_v,
    kry_v,
    binv_v,
    maps_v,
    ups_v,
    local_sem,
    big_sem,
    send_sem,
    recv_sem,
    gsend,
    grecv,
    feat,
    goal,
    src,
    wgt,
    sq0,
    sq1,
    g0,
    g1,
    acc,
):
    me, total = place(roles, devs)
    local, panels = area.shape
    coeffs = maps_v.shape[1]
    barrier = greet(me, total, devs)
    copies = []
    for c in range(local):
        copies.append(pltpu.make_async_copy(binv.at[c], binv_v.at[c], big_sem.at[c]))
    map_copy = pltpu.make_async_copy(maps, maps_v, local_sem.at[0])
    up_copy = pltpu.make_async_copy(ups, ups_v, local_sem.at[1])
    small = [
        pltpu.make_async_copy(pos, pos_v, local_sem.at[2]),
        pltpu.make_async_copy(nrm, nrm_v, local_sem.at[3]),
        pltpu.make_async_copy(area, area_v, local_sem.at[4]),
        pltpu.make_async_copy(kry.at[kry.shape[0] - 1], kry_v, local_sem.at[5]),
    ]
    for copy in small + copies:
        copy.start()
    home = [
        pltpu.make_async_copy(pos_v, posw.at[RADIUS], local_sem.at[6]),
        pltpu.make_async_copy(an_v, anw.at[RADIUS], local_sem.at[7]),
        pltpu.make_async_copy(cnt_v, cntw.at[RADIUS], local_sem.at[8]),
        pltpu.make_async_copy(info_v, cntw.at[pl.ds(SIDES, local)], local_sem.at[9]),
    ]
    map_copy.start()
    up_copy.start()
    for copy in small:
        copy.wait()
    home[0].start()
    parts = [(nrm_v[a] * area_v[...]).astype(BF16).astype(F32) for a in range(3)]
    an_v[: 3 * local] = jnp.concatenate(parts, axis=0).astype(BF16)
    lane = lax.broadcasted_iota(jnp.int32, (1, 128), 1)
    counts = jnp.zeros((1, 128), jnp.int32)
    for c in range(local):
        counts = jnp.where(lane == c, cnt[c], counts)
    cnt_v[...] = counts
    home[2].start()
    for c in range(local):
        row = jnp.where(lane == 6, used[c], (me - RADIUS) * local)
        for n in range(near.shape[1]):
            row = jnp.where(lane == 8 + n, near[c, n], row)
        info_v[c] = row
    home[3].start()
    pl.semaphore_wait(barrier, total - 1)

    def to_neighbours(own, ref, kind, rows=None):
        made = []

        def slot(side):
            return ref.at[side] if rows is None else ref.at[side, rows]

        for n, d in enumerate([1, -1, 2, -2, 3, -3]):
            made.append(
                pltpu.make_async_remote_copy(
                    src_ref=own if rows is None else own.at[rows],
                    dst_ref=slot(RADIUS - d),
                    send_sem=send_sem.at[kind, n],
                    recv_sem=recv_sem.at[kind, n],
                    device_id=coords(lax.rem(me + d + total, total), devs),
                    device_id_type=MESH,
                )
            )
        for copy in made:
            copy.start()
        return made

    sent = to_neighbours(pos_v, posw, 0)
    sent += to_neighbours(an_v, anw, 4, pl.ds(0, 3 * local))
    sent += to_neighbours(cnt_v, cntw, 1)
    live = live_mask(cnt, (local, panels))
    current = kry_v[...].astype(BF16)
    density = jnp.zeros((local, panels), F32)
    for c in range(local):
        copies[c].wait()
        found = mm(current, binv_v[c], NT)
        density = jnp.where(row_is(found.shape, c), found, density)
    rounded = jnp.where(live, density, 0.0).astype(BF16)
    an_v[3 * local :] = rounded
    base[...] = 0.5 * rounded.astype(F32)
    home[1].start()
    sent += to_neighbours(an_v, anw, 2, pl.ds(3 * local, local))
    map_copy.wait()
    moments = jnp.zeros((local, coeffs), F32)
    for c in range(local):
        found = mm(rounded, maps_v[c], NT)
        moments = jnp.where(row_is(found.shape, c), found, moments)
    moments = moments.astype(BF16)
    momw[RADIUS] = moments
    sent += to_neighbours(momw.at[RADIUS], momw, 3)
    up_copy.wait()
    merged = jnp.zeros((local, coeffs), F32)
    for k in range(local):
        found = mm(moments, ups_v[k], NT)
        merged = jnp.where(row_is(found.shape, k), found, merged)
    gmall[me] = jnp.sum(merged, axis=0, keepdims=True)

    def group_copy(i):
        return pltpu.make_async_remote_copy(
            src_ref=gmall.at[me],
            dst_ref=gmall.at[me],
            send_sem=gsend.at[i],
            recv_sem=grecv.at[i],
            device_id=coords(lax.rem(me + i, total), devs),
            device_id_type=MESH,
        )

    def start_one(i, carry):
        group_copy(i).start()
        return carry

    def wait_one(i, carry):
        source = lax.rem(me - i + total, total)
        pltpu.make_async_remote_copy(
            src_ref=gmall.at[me],
            dst_ref=gmall.at[source],
            send_sem=gsend.at[i],
            recv_sem=grecv.at[i],
            device_id=coords(lax.rem(me + i, total), devs),
            device_id_type=MESH,
        ).wait()
        return carry

    lax.fori_loop(1, total, start_one, 0)
    own_near(
        pos_v, parts, rounded.astype(F32), feat, goal, src, wgt, (sq0, sq1), (g0, g1), acc, base
    )
    for copy in home + sent:
        copy.wait()
    lax.fori_loop(1, total, wait_one, 0)


def near_kernel(
    infoh,
    posh,
    anh,
    out,
    info,
    posw,
    anw,
    sems,
    feat,
    goal,
    src,
    wgt,
    sq0,
    sq1,
    g0,
    g1,
    acc,
    begin,
    spans,
):
    local, panels = out.shape
    wide = goal.shape[2]
    per_h = panels // wide
    tally = pltpu.make_async_copy(infoh.at[pl.ds(0, SIDES + local)], info, sems.at[2, 0])
    tally.start()
    order = [RADIUS] + [k for k in range(SIDES) if k != RADIUS]
    loads = []
    for k in order:
        loads.append(pltpu.make_async_copy(posh.at[k], posw.at[k], sems.at[0, k]))
        loads.append(pltpu.make_async_copy(anh.at[k], anw.at[k], sems.at[1, k]))
    for copy in loads:
        copy.start()
    for n, side in enumerate(order):
        loads[2 * n].wait()
        loads[2 * n + 1].wait()
        fields = anw[side].astype(F32)
        dens = fields[3 * local :]
        weights = [fields[a * local : (a + 1) * local] * dens for a in range(3)]
        spread_all(feat.at[side], [posw[side, a] for a in range(3)], weights)
    tally.wait()
    first = info[SIDES, 0, 7]

    def cluster_body(c, start):
        made = goal_rows(read_features(feat.at[RADIUS], c))
        for h in range(per_h):
            goal[per_h * c + h] = made[:, h * wide : (h + 1) * wide]

        def slot_body(s, offset):
            w = info[SIDES + c, 0, 8 + s] - first
            side = w // local
            inner = lax.rem(w, local)
            made, pulled = source_rows(read_features(feat.at[side], inner))
            for b in range(panels // 128):
                src[offset + b] = made[:, b * 128 : (b + 1) * 128]
                wgt[offset + b] = pulled[:, b * 128 : (b + 1) * 128]
            return offset + (info[side, 0, inner] + 127) // 128

        end = lax.fori_loop(0, info[SIDES + c, 0, 6], slot_body, start)
        pad_rows = lax.broadcasted_iota(jnp.int32, (48, 128), 0)
        src[end] = jnp.where(pad_rows >= 44, 1.0, 0.0).astype(BF16)
        wgt[end] = jnp.zeros((16, 128), BF16)
        stop = (end + 1) // 2 * 2
        begin[c] = start // 2
        spans[c] = (info[RADIUS, 0, c] + wide - 1) // wide
        return stop

    end = lax.fori_loop(0, local, cluster_body, 0)
    begin[local] = end // 2
    begin[local + 1] = end // 2
    spans[local] = 1
    acc[...] = jnp.zeros(acc.shape, F32)

    def advance(state):
        c, h, b = state
        over = b + 1 >= begin[jnp.minimum(c + 1, local)]
        h = jnp.where(over, h + 1, h)
        done = h >= spans[c]
        b = jnp.where(over, begin[c], b + 1)
        c_next = jnp.where(done, jnp.minimum(c + 1, local), c)
        b = jnp.where(done, begin[c_next], b)
        return c_next, jnp.where(done, 0, h), b

    def products(state, ref):
        c, h, b = state
        squares(src, b, goal[per_h * c + h], ref)

    def count_body(c, total):
        return total + spans[c] * (begin[c + 1] - begin[c])

    units = lax.fori_loop(0, local, count_body, 0)
    origin = (jnp.int32(0), jnp.int32(0), jnp.int32(0))
    products(origin, sq0)
    cubes(sq0, g0)
    second = advance(origin)
    products(second, sq1)

    def body(t, states):
        old, state = states
        for u in range(UNITS):
            later = advance(state)
            products(later, (sq0, sq1)[u % 2])
            cubes((sq1, sq0)[u % 2], (g1, g0)[u % 2])
            c, h, b = old
            acc[per_h * c + h] += gathered(wgt, b, (g0, g1)[u % 2])
            old, state = state, later
        return old, state

    lax.fori_loop(0, (units + UNITS - 1) // UNITS, body, (origin, second))
    for c in range(local):
        own = read_features(feat.at[RADIUS], c)
        for h in range(per_h):
            part = slice(h * wide, (h + 1) * wide)
            out[c : c + 1, part] = combine(own[:, part], acc[per_h * c + h])


def finish_kernel(
    roles,
    devs,
    cnt,
    glist,
    gkind,
    llist,
    lkind,
    momw,
    gmall,
    near,
    base,
    kry,
    maps_v,
    ups_v,
    fars_v,
    nxt,
    hess,
    red,
    send_sem,
    recv_sem,
):
    me, total = place(roles, devs)
    local, panels = near.shape
    coeffs = maps_v.shape[1]
    kinds = fars_v.shape[1]
    window = SIDES * local
    barrier = greet(me, total, devs)

    groups = gmall[...].reshape(total, coeffs)
    g_rows = lax.broadcasted_iota(jnp.int32, (kinds, total), 0)
    g_lanes = lax.broadcasted_iota(jnp.int32, (kinds, total), 1)
    g_hot = jnp.zeros((kinds, total), F32)
    for n in range(glist.shape[1]):
        g_hot += jnp.where((g_rows == gkind[0, n]) & (g_lanes == glist[0, n]), 1.0, 0.0)
    g_hot = g_hot.astype(BF16)
    hi, mid, low = splits(groups)
    g_sum = mm(g_hot, hi.astype(BF16), NN) + mm(g_hot, mid.astype(BF16), NN)
    g_sum += mm(g_hot, low.astype(BF16), NN)
    g_both = halves(g_sum)

    lanes = lax.broadcasted_iota(jnp.int32, (local, window), 1)
    shift = (me - RADIUS) * local
    hots = [jnp.zeros((local, window), F32) for _ in range(kinds)]
    for n in range(llist.shape[1]):
        hit = lanes == (llist[:, n : n + 1] - shift)
        kind = jnp.broadcast_to(lkind[:, n : n + 1], (local, window))
        for o in range(kinds):
            hots[o] = hots[o] + jnp.where(hit & (kind == o), 1.0, 0.0)
    hot = jnp.concatenate(hots, axis=0).astype(BF16)
    held = jnp.concatenate([momw[side].astype(F32) for side in range(SIDES)], axis=0)
    summed = mm(hot, held.astype(BF16), NN)

    g_parts = jnp.zeros((kinds, coeffs), F32)
    for o in range(kinds):
        found = mm(g_both, fars_v[1, o], NT)
        found = found[:kinds] + found[kinds:]
        g_parts = jnp.where(row_is(found.shape, o), found, g_parts)
    g_local = jnp.sum(g_parts, axis=0, keepdims=True).astype(BF16)
    leaf = jnp.zeros((local, coeffs), F32)
    for o in range(kinds):
        found = mm(halves(summed[o * local : (o + 1) * local]), fars_v[0, o], NT)
        leaf = leaf + found[:local] + found[local:]
    g_wide = jnp.broadcast_to(g_local.astype(F32), (local, coeffs)).astype(BF16)
    down = jnp.zeros((local, coeffs), F32)
    for k in range(local):
        found = mm(g_wide, ups_v[k], NN)
        down = jnp.where(row_is(found.shape, k), found, down)
    leaf = (leaf + down).astype(BF16)
    far = jnp.zeros((local, panels), F32)
    for c in range(local):
        found = mm(leaf, maps_v[c], NN)
        far = jnp.where(row_is(found.shape, c), found, far)
    live = live_mask(cnt, (local, panels))
    image = jnp.where(live, base[...] + near[...] + far, 0.0)

    lane = lax.broadcasted_iota(jnp.int32, (1, 128), 1)
    count = kry.shape[0]
    row = jnp.zeros((1, 128), F32)
    for k in range(count + 1):
        part = image * (kry[k] if k < count else image)
        value = jnp.sum(jnp.sum(part, axis=0, keepdims=True), axis=1, keepdims=True)
        row = jnp.where(lane == k, value, row)
    red[me] = row
    pl.semaphore_wait(barrier, total - 1)

    def one(i):
        source = lax.rem(me - i + total, total)
        target = coords(lax.rem(me + i, total), devs)

        def copy(dst):
            return pltpu.make_async_remote_copy(
                src_ref=red.at[me],
                dst_ref=red.at[dst],
                send_sem=send_sem.at[i],
                recv_sem=recv_sem.at[i],
                device_id=target,
                device_id_type=MESH,
            )

        return copy, source

    def start_one(i, carry):
        one(i)[0](me).start()
        return carry

    def wait_one(i, carry):
        copy, source = one(i)
        copy(source).wait()
        return carry

    lax.fori_loop(1, total, start_one, 0)
    lax.fori_loop(1, total, wait_one, 0)
    scale = 1.0 / (total * local * panels)
    sums = jnp.sum(red[...], axis=0) * scale
    rest = image
    energy = sums[:, count : count + 1]
    for k in range(count):
        c_k = sums[:, k : k + 1]
        rest = rest - c_k * kry[k]
        energy = energy - c_k * c_k
    height = jnp.sqrt(energy + EPSILON)
    nxt[...] = rest / height
    hess[...] = jnp.where(lane == count, height, sums)[:, : count + 1]


def shards(
    roles,
    devs,
    positions,
    normals,
    panel_areas,
    panel_counts,
    near_lists,
    near_counts,
    leaf_lists,
    leaf_kinds,
    group_lists,
    group_kinds,
    block_inverse,
    moment_maps,
    up_operators,
    far_operators,
    krylov_basis,
):
    local, _, panels = positions.shape
    coeffs = moment_maps.shape[1]
    total = roles * devs
    wide = 256
    vmem = pl.BlockSpec(memory_space=pltpu.VMEM)
    smem = pl.BlockSpec(memory_space=pltpu.SMEM)
    hbm = pl.BlockSpec(memory_space=pltpu.HBM)
    dma = pltpu.SemaphoreType.DMA
    posw, anw, cntw, momw, gmall, base = pl.pallas_call(
        functools.partial(source_kernel, roles, devs),
        name="sources",
        out_shape=(
            jax.ShapeDtypeStruct((SPARE // (12 * local * panels), 3, local, panels), F32),
            jax.ShapeDtypeStruct((SPARE // (8 * local * panels), 4 * local, panels), BF16),
            jax.ShapeDtypeStruct((SPARE // 512, 1, 128), jnp.int32),
            jax.ShapeDtypeStruct((SIDES, local, coeffs), BF16),
            jax.ShapeDtypeStruct((total, 1, coeffs), F32),
            jax.ShapeDtypeStruct((local, panels), F32),
        ),
        in_specs=[smem] * 3 + [hbm] * 7,
        out_specs=(hbm, hbm, hbm, vmem, vmem, vmem),
        scratch_shapes=[
            pltpu.VMEM((3, local, panels), F32),
            pltpu.VMEM((4 * local, panels), BF16),
            pltpu.VMEM((1, 128), jnp.int32),
            pltpu.VMEM((local, 1, 128), jnp.int32),
            pltpu.VMEM((3, local, panels), F32),
            pltpu.VMEM((local, panels), F32),
            pltpu.VMEM((local, panels), F32),
            pltpu.VMEM(block_inverse.shape, BF16),
            pltpu.VMEM(moment_maps.shape, BF16),
            pltpu.VMEM(up_operators.shape, BF16),
            dma((10,)),
            dma((local,)),
            dma((5, 6)),
            dma((5, 6)),
            dma((total,)),
            dma((total,)),
            pltpu.VMEM((panels // 128, 8 * local, 128), F32),
            pltpu.VMEM((local * (panels // wide), 48, wide), BF16),
            pltpu.VMEM((local * (panels // 128), 48, 128), BF16),
            pltpu.VMEM((local * (panels // 128), 16, 128), BF16),
            pltpu.VMEM((256, wide), F32),
            pltpu.VMEM((256, wide), F32),
            pltpu.VMEM((256, wide), BF16),
            pltpu.VMEM((256, wide), BF16),
            pltpu.VMEM((local * (panels // wide), 16, wide), F32),
        ],
        compiler_params=pltpu.CompilerParams(
            collective_id=0, has_side_effects=True, vmem_limit_bytes=62 << 20
        ),
    )(
        panel_counts,
        near_lists,
        near_counts,
        jnp.transpose(positions, (1, 0, 2)),
        jnp.transpose(normals, (1, 0, 2)),
        panel_areas,
        krylov_basis,
        block_inverse,
        moment_maps,
        up_operators,
    )
    room = local * (near_lists.shape[1] * (panels // 128) + 1) + 8
    goals = (local + 1) * (panels // wide)
    near = pl.pallas_call(
        near_kernel,
        name="near",
        cost_estimate=pl.CostEstimate(
            flops=40 * local * panels * panels * (near_lists.shape[1] + 1),
            bytes_accessed=48 * local * panels * SIDES,
            transcendentals=local * panels * panels * (near_lists.shape[1] + 1),
        ),
        out_shape=jax.ShapeDtypeStruct((local, panels), F32),
        in_specs=[hbm, hbm, hbm],
        out_specs=vmem,
        scratch_shapes=[
            pltpu.SMEM((SIDES + local, 1, 128), jnp.int32),
            pltpu.VMEM((SIDES, 3, local, panels), F32),
            pltpu.VMEM((SIDES, 4 * local, panels), BF16),
            dma((3, SIDES)),
            pltpu.VMEM((SIDES, panels // 128, 8 * local, 128), F32),
            pltpu.VMEM((goals, 48, wide), BF16),
            pltpu.VMEM((room, 48, 128), BF16),
            pltpu.VMEM((room, 16, 128), BF16),
            pltpu.VMEM((256, wide), F32),
            pltpu.VMEM((256, wide), F32),
            pltpu.VMEM((256, wide), BF16),
            pltpu.VMEM((256, wide), BF16),
            pltpu.VMEM((goals, 16, wide), F32),
            pltpu.SMEM((local + 2,), jnp.int32),
            pltpu.SMEM((local + 2,), jnp.int32),
        ],
        compiler_params=pltpu.CompilerParams(vmem_limit_bytes=52 << 20),
    )(cntw, posw, anw)
    nxt, hess = pl.pallas_call(
        functools.partial(finish_kernel, roles, devs),
        name="finish",
        out_shape=(
            jax.ShapeDtypeStruct((local, panels), F32),
            jax.ShapeDtypeStruct((1, krylov_basis.shape[0] + 1), F32),
        ),
        in_specs=[smem, smem, smem] + [vmem] * 10,
        out_specs=(vmem, vmem),
        scratch_shapes=[
            pltpu.VMEM((total, 1, 128), F32),
            dma((total,)),
            dma((total,)),
        ],
        compiler_params=pltpu.CompilerParams(
            collective_id=1, has_side_effects=True, vmem_limit_bytes=14 << 20
        ),
    )(
        panel_counts,
        group_lists,
        group_kinds,
        leaf_lists,
        leaf_kinds,
        momw,
        gmall,
        near,
        base,
        krylov_basis,
        moment_maps,
        up_operators,
        far_operators,
    )
    return nxt, jnp.reshape(hess, (krylov_basis.shape[0] + 1,))


def solution(mesh):
    roles, devs = mesh.shape["role"], mesh.shape["dev"]
    return jax.shard_map(
        functools.partial(shards, roles, devs),
        mesh=mesh,
        in_specs=(
            P(AXES, None, None),
            P(AXES, None, None),
            P(AXES, None),
            P(AXES),
            P(AXES, None),
            P(AXES),
            P(AXES, None),
            P(AXES, None),
            P(AXES, None),
            P(AXES, None),
            P(AXES, None, None),
            P(AXES, None, None),
            P(),
            P(),
            P(None, AXES, None),
        ),
        out_specs=(P(AXES, None), P()),
        check_vma=False,
    )
```

```python
import functools

import jax
import jax.numpy as jnp
from jax import lax
from jax.experimental import pallas as pl
from jax.experimental.pallas import tpu as pltpu
from jax.sharding import PartitionSpec as P

RADIUS = 3
SIDES = 2 * RADIUS + 1
SOFTEN = 0.01
EPSILON = 1e-06
UNITS = 24
SPARE = 12 << 20
FIXED = 32767.0
MESH = pl.DeviceIdType.MESH
NT = (((1,), (1,)), ((), ()))
NN = (((1,), (0,)), ((), ()))
TN = (((0,), (0,)), ((), ()))
F32 = jnp.float32
BF16 = jnp.bfloat16
AXES = ("role", "dev")


def mm(a, b, dims):
    return lax.dot_general(a, b, dims, preferred_element_type=F32)


def row_is(shape, k):
    return lax.broadcasted_iota(jnp.int32, shape, 0) == k


def place(roles, devs):
    me = lax.axis_index("role") * devs + lax.axis_index("dev")
    return me, roles * devs


def coords(linear, devs):
    return (linear // devs, lax.rem(linear, devs))


def far_first(me, roles, devs, visit):
    own = lax.rem(me, devs)

    def body(t, ends):
        low, high = ends
        left = own - low >= high - own
        other = jnp.where(left, low, high)
        for r in range(roles):
            visit(r * devs + other)
        return jnp.where(left, low + 1, low), jnp.where(left, high, high - 1)

    lax.fori_loop(0, devs - 1, body, (jnp.int32(0), jnp.int32(devs - 1)))
    for r in range(1, roles):
        visit(lax.rem(me + r * devs, roles * devs))


def greet(me, roles, devs):
    barrier = pltpu.get_barrier_semaphore()

    def visit(other):
        pl.semaphore_signal(barrier, inc=1, device_id=coords(other, devs), device_id_type=MESH)

    far_first(me, roles, devs, visit)
    return barrier


def live_mask(cnt_ref, shape):
    rows = lax.broadcasted_iota(jnp.int32, shape, 0)
    limit = jnp.zeros(shape, jnp.int32)
    for c in range(shape[0]):
        limit = jnp.where(rows == c, cnt_ref[c], limit)
    return lax.broadcasted_iota(jnp.int32, shape, 1) < limit


def halves(x):
    hi = x.astype(BF16).astype(F32)
    return jnp.concatenate([hi, x - hi], axis=0).astype(BF16)


def splits(x):
    hi = x.astype(BF16).astype(F32)
    rest = x - hi
    mid = rest.astype(BF16).astype(F32)
    return hi, mid, rest - mid


def pack(parts):
    return jnp.concatenate(parts, axis=0).astype(BF16)


def spread_all(feat, positions, weights):
    local, panels = positions[0].shape
    norm = jnp.zeros((local, panels), F32)
    inside = jnp.zeros((local, panels), F32)
    for y, w in zip(positions, weights):
        norm = norm + y * y
        inside = inside - y * w
    rows = list(positions) + [norm] + list(weights) + [inside]
    for k, value in enumerate(rows):
        for b in range(panels // 128):
            feat[b, pl.ds(k, local, stride=8), :] = value[:, b * 128 : (b + 1) * 128]


def read_features(feat, inner):
    at = pl.ds(pl.multiple_of(inner * 8, 8), 8)
    return jnp.concatenate([feat[b, at, :] for b in range(feat.shape[0])], axis=1)


def goal_rows(own):
    shape = own.shape
    rows = lax.broadcasted_iota(jnp.int32, shape, 0)
    x = jnp.where(rows < 3, -2.0 * own, jnp.where(rows == 3, own + SOFTEN, 0.0))
    hi, mid, low = splits(x)
    norms = [jnp.broadcast_to(part[3:4], shape) for part in (hi, mid, low)]
    firm = jnp.where(rows < 3, hi, jnp.where(rows == 3, 1.0, 0.0))
    soft = jnp.where(rows < 3, mid, 0.0)
    last = jnp.where(rows < 3, low, 0.0)
    tail = soft
    for k in range(3):
        tail = jnp.where(rows == 4 + k, norms[k], tail)
    return pack([firm, firm, firm, soft, last, tail])


def source_rows(own):
    rows = lax.broadcasted_iota(jnp.int32, own.shape, 0)
    hi, mid, low = splits(own)
    made = pack([hi, mid, low, hi, hi, jnp.where(rows < 4, mid, 1.0)])
    return made, pack([jnp.where(rows < 4, pltpu.roll(mid, 4, 0), hi), low])


def squares(src, block, target, ref):
    for k in range(2):
        ref[k * 128 : (k + 1) * 128, :] = mm(src[2 * block + k], target, TN)


def cubes(a, b):
    inverse = lax.rsqrt(a[...])
    b[...] = (inverse * inverse * inverse).astype(BF16)


def gathered(wgt, block, ref):
    both = jnp.concatenate([wgt[2 * block], wgt[2 * block + 1]], axis=1)
    return mm(both, ref[...], NN)


def combine(own, got):
    total = got[:8] + pltpu.roll(got[:8], 4, 0) + got[8:]
    rows = lax.broadcasted_iota(jnp.int32, total.shape, 0)
    part = total * pltpu.roll(own, 4, 0)
    value = jnp.where(rows < 4, 0.0, jnp.where(rows == 7, total, part))
    return jnp.sum(value, axis=0, keepdims=True)


def own_near(pos_v, nrm_parts, density, feat, goal, src, wgt, sqs, gs, acc, out):
    local, panels = density.shape
    wide = goal.shape[2]
    per_h = panels // wide
    blocks = panels // 256
    positions = [pos_v[a] for a in range(3)]
    spread_all(feat, positions, [part * density for part in nrm_parts])
    for c in range(local):
        own = read_features(feat, c)
        made = goal_rows(own)
        for h in range(per_h):
            goal[per_h * c + h] = made[:, h * wide : (h + 1) * wide]
        made, pulled = source_rows(own)
        for b in range(panels // 128):
            src[2 * blocks * c + b] = made[:, b * 128 : (b + 1) * 128]
            wgt[2 * blocks * c + b] = pulled[:, b * 128 : (b + 1) * 128]
    acc[...] = jnp.zeros(acc.shape, F32)
    units = local * per_h * blocks

    def place_of(n):
        n = lax.rem(n, units)
        c = n // (per_h * blocks)
        return n // blocks, c * blocks + lax.rem(n, blocks)

    def start(n, ref):
        g, b = place_of(n)
        squares(src, b, goal[g], ref)

    start(0, sqs[0])
    cubes(sqs[0], gs[0])
    start(1, sqs[1])
    steps = 16

    def body(t, carry):
        for u in range(steps):
            n = t * steps + u
            start(n + 2, sqs[u % 2])
            cubes(sqs[(u + 1) % 2], gs[(u + 1) % 2])
            g, b = place_of(n)
            acc[g] += gathered(wgt, b, gs[u % 2])
        return carry

    lax.fori_loop(0, units // steps, body, 0)
    for c in range(local):
        own = read_features(feat, c)
        for h in range(per_h):
            part = slice(h * wide, (h + 1) * wide)
            out[c : c + 1, part] = out[c : c + 1, part] + combine(own[:, part], acc[per_h * c + h])


def source_kernel(
    roles,
    devs,
    cnt,
    near,
    used,
    pos,
    nrm,
    area,
    kry,
    binv,
    maps,
    ups,
    posw,
    anw,
    cntw,
    momw,
    gmall,
    base,
    pos_v,
    fix_v,
    an_v,
    cnt_v,
    info_v,
    nrm_v,
    area_v,
    kry_v,
    binv_v,
    maps_v,
    ups_v,
    local_sem,
    big_sem,
    send_sem,
    recv_sem,
    gsend,
    grecv,
    feat,
    goal,
    src,
    wgt,
    sq0,
    sq1,
    g0,
    g1,
    acc,
):
    me, total = place(roles, devs)
    local, panels = area.shape
    coeffs = maps_v.shape[1]
    barrier = greet(me, roles, devs)
    copies = []
    for c in range(local):
        copies.append(pltpu.make_async_copy(binv.at[c], binv_v.at[c], big_sem.at[c]))
    map_copy = pltpu.make_async_copy(maps, maps_v, local_sem.at[0])
    up_copy = pltpu.make_async_copy(ups, ups_v, local_sem.at[1])
    small = [
        pltpu.make_async_copy(pos, pos_v, local_sem.at[2]),
        pltpu.make_async_copy(nrm, nrm_v, local_sem.at[3]),
        pltpu.make_async_copy(area, area_v, local_sem.at[4]),
        pltpu.make_async_copy(kry.at[kry.shape[0] - 1], kry_v, local_sem.at[5]),
    ]
    for copy in small + copies:
        copy.start()
    home = [
        pltpu.make_async_copy(fix_v, posw.at[RADIUS], local_sem.at[6]),
        pltpu.make_async_copy(an_v, anw.at[RADIUS], local_sem.at[7]),
        pltpu.make_async_copy(cnt_v, cntw.at[RADIUS], local_sem.at[8]),
        pltpu.make_async_copy(info_v, cntw.at[pl.ds(SIDES, local)], local_sem.at[9]),
    ]
    map_copy.start()
    up_copy.start()
    for copy in small:
        copy.wait()
    fix_v[...] = jnp.floor(pos_v[...] * FIXED + 0.5).astype(jnp.int32).astype(jnp.int16)
    home[0].start()
    parts = [(nrm_v[a] * area_v[...]).astype(BF16).astype(F32) for a in range(3)]
    an_v[: 3 * local] = jnp.concatenate(parts, axis=0).astype(BF16)
    lane = lax.broadcasted_iota(jnp.int32, (1, 128), 1)
    counts = jnp.zeros((1, 128), jnp.int32)
    for c in range(local):
        counts = jnp.where(lane == c, cnt[c], counts)
    cnt_v[...] = counts
    home[2].start()
    for c in range(local):
        row = jnp.where(lane == 6, used[c], (me - RADIUS) * local)
        for n in range(near.shape[1]):
            row = jnp.where(lane == 8 + n, near[c, n], row)
        info_v[c] = row
    home[3].start()
    pl.semaphore_wait(barrier, total - 1)

    def to_neighbours(own, ref, kind, rows=None):
        made = []

        def slot(side):
            return ref.at[side] if rows is None else ref.at[side, rows]

        for n, d in enumerate([1, -1, 2, -2, 3, -3]):
            made.append(
                pltpu.make_async_remote_copy(
                    src_ref=own if rows is None else own.at[rows],
                    dst_ref=slot(RADIUS - d),
                    send_sem=send_sem.at[kind, n],
                    recv_sem=recv_sem.at[kind, n],
                    device_id=coords(lax.rem(me + d + total, total), devs),
                    device_id_type=MESH,
                )
            )
        for copy in made:
            copy.start()
        return made

    sent = to_neighbours(fix_v, posw, 0)
    sent += to_neighbours(an_v, anw, 4, pl.ds(0, 3 * local))
    sent += to_neighbours(cnt_v, cntw, 1)
    live = live_mask(cnt, (local, panels))
    current = kry_v[...].astype(BF16)
    density = jnp.zeros((local, panels), F32)
    for c in range(local):
        copies[c].wait()
        found = mm(current, binv_v[c], NT)
        density = jnp.where(row_is(found.shape, c), found, density)
    rounded = jnp.where(live, density, 0.0).astype(BF16)
    an_v[3 * local :] = rounded
    base[...] = 0.5 * rounded.astype(F32)
    home[1].start()
    sent += to_neighbours(an_v, anw, 2, pl.ds(3 * local, local))
    map_copy.wait()
    moments = jnp.zeros((local, coeffs), F32)
    for c in range(local):
        found = mm(rounded, maps_v[c], NT)
        moments = jnp.where(row_is(found.shape, c), found, moments)
    moments = moments.astype(BF16)
    momw[RADIUS] = moments
    sent += to_neighbours(momw.at[RADIUS], momw, 3)
    up_copy.wait()
    merged = jnp.zeros((local, coeffs), F32)
    for k in range(local):
        found = mm(moments, ups_v[k], NT)
        merged = jnp.where(row_is(found.shape, k), found, merged)
    gmall[me] = jnp.sum(merged, axis=0, keepdims=True)

    def group_copy(slot, other):
        return pltpu.make_async_remote_copy(
            src_ref=gmall.at[me],
            dst_ref=gmall.at[slot],
            send_sem=gsend.at[other],
            recv_sem=grecv.at[slot],
            device_id=coords(other, devs),
            device_id_type=MESH,
        )

    far_first(me, roles, devs, lambda other: group_copy(me, other).start())
    own_near(
        pos_v, parts, rounded.astype(F32), feat, goal, src, wgt, (sq0, sq1), (g0, g1), acc, base
    )
    for copy in home + sent:
        copy.wait()
    far_first(me, roles, devs, lambda other: group_copy(other, other).wait())


def near_kernel(
    infoh,
    posh,
    anh,
    out,
    info,
    posw,
    anw,
    sems,
    feat,
    goal,
    src,
    wgt,
    sq0,
    sq1,
    g0,
    g1,
    acc,
    begin,
    spans,
):
    local, panels = out.shape
    wide = goal.shape[2]
    per_h = panels // wide
    tally = pltpu.make_async_copy(infoh.at[pl.ds(0, SIDES + local)], info, sems.at[2, 0])
    tally.start()
    order = [RADIUS] + [k for k in range(SIDES) if k != RADIUS]
    loads = []
    for k in order:
        loads.append(pltpu.make_async_copy(posh.at[k], posw.at[k], sems.at[0, k]))
        loads.append(pltpu.make_async_copy(anh.at[k], anw.at[k], sems.at[1, k]))
    for copy in loads:
        copy.start()
    for n, side in enumerate(order):
        loads[2 * n].wait()
        loads[2 * n + 1].wait()
        fields = anw[side].astype(F32)
        dens = fields[3 * local :]
        weights = [fields[a * local : (a + 1) * local] * dens for a in range(3)]
        centres = posw[side].astype(jnp.int32).astype(F32) * (1.0 / FIXED)
        spread_all(feat.at[side], [centres[a] for a in range(3)], weights)
    tally.wait()
    first = info[SIDES, 0, 7]

    def cluster_body(c, start):
        made = goal_rows(read_features(feat.at[RADIUS], c))
        for h in range(per_h):
            goal[per_h * c + h] = made[:, h * wide : (h + 1) * wide]

        def slot_body(s, offset):
            w = info[SIDES + c, 0, 8 + s] - first
            side = w // local
            inner = lax.rem(w, local)
            made, pulled = source_rows(read_features(feat.at[side], inner))
            for b in range(panels // 128):
                src[offset + b] = made[:, b * 128 : (b + 1) * 128]
                wgt[offset + b] = pulled[:, b * 128 : (b + 1) * 128]
            return offset + (info[side, 0, inner] + 127) // 128

        end = lax.fori_loop(0, info[SIDES + c, 0, 6], slot_body, start)
        pad_rows = lax.broadcasted_iota(jnp.int32, (48, 128), 0)
        src[end] = jnp.where(pad_rows >= 44, 1.0, 0.0).astype(BF16)
        wgt[end] = jnp.zeros((16, 128), BF16)
        stop = (end + 1) // 2 * 2
        begin[c] = start // 2
        spans[c] = (info[RADIUS, 0, c] + wide - 1) // wide
        return stop

    end = lax.fori_loop(0, local, cluster_body, 0)
    begin[local] = end // 2
    begin[local + 1] = end // 2
    spans[local] = 1
    acc[...] = jnp.zeros(acc.shape, F32)

    def advance(state):
        c, h, b = state
        over = b + 1 >= begin[jnp.minimum(c + 1, local)]
        h = jnp.where(over, h + 1, h)
        done = h >= spans[c]
        b = jnp.where(over, begin[c], b + 1)
        c_next = jnp.where(done, jnp.minimum(c + 1, local), c)
        b = jnp.where(done, begin[c_next], b)
        return c_next, jnp.where(done, 0, h), b

    def products(state, ref):
        c, h, b = state
        squares(src, b, goal[per_h * c + h], ref)

    def count_body(c, total):
        return total + spans[c] * (begin[c + 1] - begin[c])

    units = lax.fori_loop(0, local, count_body, 0)
    origin = (jnp.int32(0), jnp.int32(0), jnp.int32(0))
    products(origin, sq0)
    cubes(sq0, g0)
    second = advance(origin)
    products(second, sq1)

    def body(t, states):
        old, state = states
        for u in range(UNITS):
            later = advance(state)
            products(later, (sq0, sq1)[u % 2])
            cubes((sq1, sq0)[u % 2], (g1, g0)[u % 2])
            c, h, b = old
            acc[per_h * c + h] += gathered(wgt, b, (g0, g1)[u % 2])
            old, state = state, later
        return old, state

    lax.fori_loop(0, (units + UNITS - 1) // UNITS, body, (origin, second))
    for c in range(local):
        own = read_features(feat.at[RADIUS], c)
        for h in range(per_h):
            part = slice(h * wide, (h + 1) * wide)
            out[c : c + 1, part] = combine(own[:, part], acc[per_h * c + h])


def finish_kernel(
    roles,
    devs,
    cnt,
    glist,
    gkind,
    llist,
    lkind,
    momw,
    gmall,
    near,
    base,
    kry,
    maps_v,
    ups_v,
    fars_v,
    nxt,
    hess,
    red,
    send_sem,
    recv_sem,
):
    me, total = place(roles, devs)
    local, panels = near.shape
    coeffs = maps_v.shape[1]
    kinds = fars_v.shape[1]
    window = SIDES * local
    barrier = greet(me, roles, devs)

    groups = gmall[...].reshape(total, coeffs)
    g_rows = lax.broadcasted_iota(jnp.int32, (kinds, total), 0)
    g_lanes = lax.broadcasted_iota(jnp.int32, (kinds, total), 1)
    g_hot = jnp.zeros((kinds, total), F32)
    for n in range(glist.shape[1]):
        g_hot += jnp.where((g_rows == gkind[0, n]) & (g_lanes == glist[0, n]), 1.0, 0.0)
    g_hot = g_hot.astype(BF16)
    hi, mid, low = splits(groups)
    g_sum = mm(g_hot, hi.astype(BF16), NN) + mm(g_hot, mid.astype(BF16), NN)
    g_sum += mm(g_hot, low.astype(BF16), NN)
    g_both = halves(g_sum)

    lanes = lax.broadcasted_iota(jnp.int32, (local, window), 1)
    shift = (me - RADIUS) * local
    hots = [jnp.zeros((local, window), F32) for _ in range(kinds)]
    for n in range(llist.shape[1]):
        hit = lanes == (llist[:, n : n + 1] - shift)
        kind = jnp.broadcast_to(lkind[:, n : n + 1], (local, window))
        for o in range(kinds):
            hots[o] = hots[o] + jnp.where(hit & (kind == o), 1.0, 0.0)
    hot = jnp.concatenate(hots, axis=0).astype(BF16)
    held = jnp.concatenate([momw[side].astype(F32) for side in range(SIDES)], axis=0)
    summed = mm(hot, held.astype(BF16), NN)

    g_parts = jnp.zeros((kinds, coeffs), F32)
    for o in range(kinds):
        found = mm(g_both, fars_v[1, o], NT)
        found = found[:kinds] + found[kinds:]
        g_parts = jnp.where(row_is(found.shape, o), found, g_parts)
    g_local = jnp.sum(g_parts, axis=0, keepdims=True).astype(BF16)
    leaf = jnp.zeros((local, coeffs), F32)
    for o in range(kinds):
        found = mm(halves(summed[o * local : (o + 1) * local]), fars_v[0, o], NT)
        leaf = leaf + found[:local] + found[local:]
    g_wide = jnp.broadcast_to(g_local.astype(F32), (local, coeffs)).astype(BF16)
    down = jnp.zeros((local, coeffs), F32)
    for k in range(local):
        found = mm(g_wide, ups_v[k], NN)
        down = jnp.where(row_is(found.shape, k), found, down)
    leaf = (leaf + down).astype(BF16)
    far = jnp.zeros((local, panels), F32)
    for c in range(local):
        found = mm(leaf, maps_v[c], NN)
        far = jnp.where(row_is(found.shape, c), found, far)
    live = live_mask(cnt, (local, panels))
    image = jnp.where(live, base[...] + near[...] + far, 0.0)

    lane = lax.broadcasted_iota(jnp.int32, (1, 128), 1)
    count = kry.shape[0]
    row = jnp.zeros((1, 128), F32)
    for k in range(count + 1):
        part = image * (kry[k] if k < count else image)
        value = jnp.sum(jnp.sum(part, axis=0, keepdims=True), axis=1, keepdims=True)
        row = jnp.where(lane == k, value, row)
    red[me] = row
    pl.semaphore_wait(barrier, total - 1)

    def row_copy(slot, other):
        return pltpu.make_async_remote_copy(
            src_ref=red.at[me],
            dst_ref=red.at[slot],
            send_sem=send_sem.at[other],
            recv_sem=recv_sem.at[slot],
            device_id=coords(other, devs),
            device_id_type=MESH,
        )

    far_first(me, roles, devs, lambda other: row_copy(me, other).start())
    far_first(me, roles, devs, lambda other: row_copy(other, other).wait())
    scale = 1.0 / (total * local * panels)
    sums = jnp.sum(red[...], axis=0) * scale
    rest = image
    energy = sums[:, count : count + 1]
    for k in range(count):
        c_k = sums[:, k : k + 1]
        rest = rest - c_k * kry[k]
        energy = energy - c_k * c_k
    height = jnp.sqrt(energy + EPSILON)
    nxt[...] = rest / height
    hess[...] = jnp.where(lane == count, height, sums)[:, : count + 1]


def shards(
    roles,
    devs,
    positions,
    normals,
    panel_areas,
    panel_counts,
    near_lists,
    near_counts,
    leaf_lists,
    leaf_kinds,
    group_lists,
    group_kinds,
    block_inverse,
    moment_maps,
    up_operators,
    far_operators,
    krylov_basis,
):
    local, _, panels = positions.shape
    coeffs = moment_maps.shape[1]
    total = roles * devs
    wide = 256
    vmem = pl.BlockSpec(memory_space=pltpu.VMEM)
    smem = pl.BlockSpec(memory_space=pltpu.SMEM)
    hbm = pl.BlockSpec(memory_space=pltpu.HBM)
    dma = pltpu.SemaphoreType.DMA
    posw, anw, cntw, momw, gmall, base = pl.pallas_call(
        functools.partial(source_kernel, roles, devs),
        name="sources",
        out_shape=(
            jax.ShapeDtypeStruct((SPARE // (6 * local * panels), 3, local, panels), jnp.int16),
            jax.ShapeDtypeStruct((SPARE // (8 * local * panels), 4 * local, panels), BF16),
            jax.ShapeDtypeStruct((SPARE // 512, 1, 128), jnp.int32),
            jax.ShapeDtypeStruct((SIDES, local, coeffs), BF16),
            jax.ShapeDtypeStruct((total, 1, coeffs), F32),
            jax.ShapeDtypeStruct((local, panels), F32),
        ),
        in_specs=[smem] * 3 + [hbm] * 7,
        out_specs=(hbm, hbm, hbm, vmem, vmem, vmem),
        scratch_shapes=[
            pltpu.VMEM((3, local, panels), F32),
            pltpu.VMEM((3, local, panels), jnp.int16),
            pltpu.VMEM((4 * local, panels), BF16),
            pltpu.VMEM((1, 128), jnp.int32),
            pltpu.VMEM((local, 1, 128), jnp.int32),
            pltpu.VMEM((3, local, panels), F32),
            pltpu.VMEM((local, panels), F32),
            pltpu.VMEM((local, panels), F32),
            pltpu.VMEM(block_inverse.shape, BF16),
            pltpu.VMEM(moment_maps.shape, BF16),
            pltpu.VMEM(up_operators.shape, BF16),
            dma((10,)),
            dma((local,)),
            dma((5, 6)),
            dma((5, 6)),
            dma((total,)),
            dma((total,)),
            pltpu.VMEM((panels // 128, 8 * local, 128), F32),
            pltpu.VMEM((local * (panels // wide), 48, wide), BF16),
            pltpu.VMEM((local * (panels // 128), 48, 128), BF16),
            pltpu.VMEM((local * (panels // 128), 16, 128), BF16),
            pltpu.VMEM((256, wide), F32),
            pltpu.VMEM((256, wide), F32),
            pltpu.VMEM((256, wide), BF16),
            pltpu.VMEM((256, wide), BF16),
            pltpu.VMEM((local * (panels // wide), 16, wide), F32),
        ],
        compiler_params=pltpu.CompilerParams(
            collective_id=0, has_side_effects=True, vmem_limit_bytes=62 << 20
        ),
    )(
        panel_counts,
        near_lists,
        near_counts,
        jnp.transpose(positions, (1, 0, 2)),
        jnp.transpose(normals, (1, 0, 2)),
        panel_areas,
        krylov_basis,
        block_inverse,
        moment_maps,
        up_operators,
    )
    room = local * (near_lists.shape[1] * (panels // 128) + 1) + 8
    goals = (local + 1) * (panels // wide)
    near = pl.pallas_call(
        near_kernel,
        name="near",
        cost_estimate=pl.CostEstimate(
            flops=40 * local * panels * panels * (near_lists.shape[1] + 1),
            bytes_accessed=48 * local * panels * SIDES,
            transcendentals=local * panels * panels * (near_lists.shape[1] + 1),
        ),
        out_shape=jax.ShapeDtypeStruct((local, panels), F32),
        in_specs=[hbm, hbm, hbm],
        out_specs=vmem,
        scratch_shapes=[
            pltpu.SMEM((SIDES + local, 1, 128), jnp.int32),
            pltpu.VMEM((SIDES, 3, local, panels), jnp.int16),
            pltpu.VMEM((SIDES, 4 * local, panels), BF16),
            dma((3, SIDES)),
            pltpu.VMEM((SIDES, panels // 128, 8 * local, 128), F32),
            pltpu.VMEM((goals, 48, wide), BF16),
            pltpu.VMEM((room, 48, 128), BF16),
            pltpu.VMEM((room, 16, 128), BF16),
            pltpu.VMEM((256, wide), F32),
            pltpu.VMEM((256, wide), F32),
            pltpu.VMEM((256, wide), BF16),
            pltpu.VMEM((256, wide), BF16),
            pltpu.VMEM((goals, 16, wide), F32),
            pltpu.SMEM((local + 2,), jnp.int32),
            pltpu.SMEM((local + 2,), jnp.int32),
        ],
        compiler_params=pltpu.CompilerParams(vmem_limit_bytes=52 << 20),
    )(cntw, posw, anw)
    nxt, hess = pl.pallas_call(
        functools.partial(finish_kernel, roles, devs),
        name="finish",
        out_shape=(
            jax.ShapeDtypeStruct((local, panels), F32),
            jax.ShapeDtypeStruct((1, krylov_basis.shape[0] + 1), F32),
        ),
        in_specs=[smem, smem, smem] + [vmem] * 10,
        out_specs=(vmem, vmem),
        scratch_shapes=[
            pltpu.VMEM((total, 1, 128), F32),
            dma((total,)),
            dma((total,)),
        ],
        compiler_params=pltpu.CompilerParams(
            collective_id=1, has_side_effects=True, vmem_limit_bytes=14 << 20
        ),
    )(
        panel_counts,
        group_lists,
        group_kinds,
        leaf_lists,
        leaf_kinds,
        momw,
        gmall,
        near,
        base,
        krylov_basis,
        moment_maps,
        up_operators,
        far_operators,
    )
    return nxt, jnp.reshape(hess, (krylov_basis.shape[0] + 1,))


def solution(mesh):
    roles, devs = mesh.shape["role"], mesh.shape["dev"]
    return jax.shard_map(
        functools.partial(shards, roles, devs),
        mesh=mesh,
        in_specs=(
            P(AXES, None, None),
            P(AXES, None, None),
            P(AXES, None),
            P(AXES),
            P(AXES, None),
            P(AXES),
            P(AXES, None),
            P(AXES, None),
            P(AXES, None),
            P(AXES, None),
            P(AXES, None, None),
            P(AXES, None, None),
            P(),
            P(),
            P(None, AXES, None),
        ),
        out_specs=(P(AXES, None), P()),
        check_vma=False,
    )
```

```python
import functools

import jax
import jax.numpy as jnp
from jax import lax
from jax.experimental import pallas as pl
from jax.experimental.pallas import tpu as pltpu
from jax.sharding import PartitionSpec as P

RADIUS = 3
SIDES = 2 * RADIUS + 1
SOFTEN = 0.01
EPSILON = 1e-06
UNITS = 24
SPARE = 12 << 20
FIXED = 32767.0
MESH = pl.DeviceIdType.MESH
NT = (((1,), (1,)), ((), ()))
NN = (((1,), (0,)), ((), ()))
TN = (((0,), (0,)), ((), ()))
F32 = jnp.float32
BF16 = jnp.bfloat16
AXES = ("role", "dev")


def mm(a, b, dims):
    return lax.dot_general(a, b, dims, preferred_element_type=F32)


def row_is(shape, k):
    return lax.broadcasted_iota(jnp.int32, shape, 0) == k


def place(roles, devs):
    me = lax.axis_index("role") * devs + lax.axis_index("dev")
    return me, roles * devs


def coords(linear, devs):
    return (linear // devs, lax.rem(linear, devs))


def far_first(me, roles, devs, visit):
    own = lax.rem(me, devs)

    def body(t, ends):
        low, high = ends
        left = own - low >= high - own
        other = jnp.where(left, low, high)
        for r in range(roles):
            visit(r * devs + other)
        return jnp.where(left, low + 1, low), jnp.where(left, high, high - 1)

    lax.fori_loop(0, devs - 1, body, (jnp.int32(0), jnp.int32(devs - 1)))
    for r in range(1, roles):
        visit(lax.rem(me + r * devs, roles * devs))


def greet(me, roles, devs):
    barrier = pltpu.get_barrier_semaphore()

    def visit(other):
        pl.semaphore_signal(barrier, inc=1, device_id=coords(other, devs), device_id_type=MESH)

    far_first(me, roles, devs, visit)
    return barrier


def live_mask(cnt_ref, shape):
    rows = lax.broadcasted_iota(jnp.int32, shape, 0)
    limit = jnp.zeros(shape, jnp.int32)
    for c in range(shape[0]):
        limit = jnp.where(rows == c, cnt_ref[c], limit)
    return lax.broadcasted_iota(jnp.int32, shape, 1) < limit


def halves(x):
    hi = x.astype(BF16).astype(F32)
    return jnp.concatenate([hi, x - hi], axis=0).astype(BF16)


def splits(x):
    hi = x.astype(BF16).astype(F32)
    rest = x - hi
    mid = rest.astype(BF16).astype(F32)
    return hi, mid, rest - mid


def pack(parts):
    return jnp.concatenate(parts, axis=0).astype(BF16)


def spread_all(feat, positions, weights):
    local, panels = positions[0].shape
    norm = jnp.zeros((local, panels), F32)
    inside = jnp.zeros((local, panels), F32)
    for y, w in zip(positions, weights):
        norm = norm + y * y
        inside = inside - y * w
    rows = list(positions) + [norm] + list(weights) + [inside]
    for k, value in enumerate(rows):
        for b in range(panels // 128):
            feat[b, k * local : (k + 1) * local, :] = value[:, b * 128 : (b + 1) * 128]


def read_features(feat, inner):
    at = pl.ds(inner, 8, stride=feat.shape[1] // 8)
    return jnp.concatenate([feat[b, at, :] for b in range(feat.shape[0])], axis=1)


def goal_rows(own):
    shape = own.shape
    rows = lax.broadcasted_iota(jnp.int32, shape, 0)
    x = jnp.where(rows < 3, -2.0 * own, jnp.where(rows == 3, own + SOFTEN, 0.0))
    hi, mid, low = splits(x)
    norms = [jnp.broadcast_to(part[3:4], shape) for part in (hi, mid, low)]
    firm = jnp.where(rows < 3, hi, jnp.where(rows == 3, 1.0, 0.0))
    soft = jnp.where(rows < 3, mid, 0.0)
    last = jnp.where(rows < 3, low, 0.0)
    tail = soft
    for k in range(3):
        tail = jnp.where(rows == 4 + k, norms[k], tail)
    return pack([firm, firm, firm, soft, last, tail])


def source_rows(own):
    rows = lax.broadcasted_iota(jnp.int32, own.shape, 0)
    hi, mid, low = splits(own)
    made = pack([hi, mid, low, hi, hi, jnp.where(rows < 4, mid, 1.0)])
    return made, pack([jnp.where(rows < 4, pltpu.roll(mid, 4, 0), hi), low])


def squares(src, block, target, ref):
    for k in range(2):
        ref[k * 128 : (k + 1) * 128, :] = mm(src[2 * block + k], target, TN)


def cubes(a, b):
    inverse = lax.rsqrt(a[...])
    b[...] = (inverse * inverse * inverse).astype(BF16)


def gathered(wgt, block, ref):
    both = jnp.concatenate([wgt[2 * block], wgt[2 * block + 1]], axis=1)
    return mm(both, ref[...], NN)


def combine(own, got):
    total = got[:8] + pltpu.roll(got[:8], 4, 0) + got[8:]
    rows = lax.broadcasted_iota(jnp.int32, total.shape, 0)
    part = total * pltpu.roll(own, 4, 0)
    value = jnp.where(rows < 4, 0.0, jnp.where(rows == 7, total, part))
    return jnp.sum(value, axis=0, keepdims=True)


def own_near(pos_v, nrm_parts, density, feat, goal, src, wgt, sqs, gs, acc, out):
    local, panels = density.shape
    wide = goal.shape[2]
    per_h = panels // wide
    blocks = panels // 256
    positions = [pos_v[a] for a in range(3)]
    spread_all(feat, positions, [part * density for part in nrm_parts])
    for c in range(local):
        own = read_features(feat, c)
        made = goal_rows(own)
        for h in range(per_h):
            goal[per_h * c + h] = made[:, h * wide : (h + 1) * wide]
        made, pulled = source_rows(own)
        for b in range(panels // 128):
            src[2 * blocks * c + b] = made[:, b * 128 : (b + 1) * 128]
            wgt[2 * blocks * c + b] = pulled[:, b * 128 : (b + 1) * 128]
    acc[...] = jnp.zeros(acc.shape, F32)
    units = local * per_h * blocks

    def place_of(n):
        n = lax.rem(n, units)
        c = n // (per_h * blocks)
        return n // blocks, c * blocks + lax.rem(n, blocks)

    def start(n, ref):
        g, b = place_of(n)
        squares(src, b, goal[g], ref)

    start(0, sqs[0])
    cubes(sqs[0], gs[0])
    start(1, sqs[1])
    steps = 16

    def body(t, carry):
        for u in range(steps):
            n = t * steps + u
            start(n + 2, sqs[u % 2])
            cubes(sqs[(u + 1) % 2], gs[(u + 1) % 2])
            g, b = place_of(n)
            acc[g] += gathered(wgt, b, gs[u % 2])
        return carry

    lax.fori_loop(0, units // steps, body, 0)
    for c in range(local):
        own = read_features(feat, c)
        for h in range(per_h):
            part = slice(h * wide, (h + 1) * wide)
            out[c : c + 1, part] = out[c : c + 1, part] + combine(own[:, part], acc[per_h * c + h])


def source_kernel(
    roles,
    devs,
    cnt,
    near,
    used,
    pos,
    nrm,
    area,
    kry,
    binv,
    maps,
    ups,
    posw,
    anw,
    cntw,
    momw,
    gmall,
    base,
    mom_v,
    grp_v,
    base_v,
    pos_v,
    fix_v,
    an_v,
    cnt_v,
    info_v,
    nrm_v,
    area_v,
    kry_v,
    binv_v,
    maps_v,
    ups_v,
    local_sem,
    big_sem,
    send_sem,
    recv_sem,
    gsend,
    grecv,
    feat,
    goal,
    src,
    wgt,
    sq0,
    sq1,
    g0,
    g1,
    acc,
):
    me, total = place(roles, devs)
    local, panels = area.shape
    coeffs = maps_v.shape[1]
    barrier = greet(me, roles, devs)
    copies = []
    for c in range(local):
        copies.append(pltpu.make_async_copy(binv.at[c], binv_v.at[c], big_sem.at[c]))
    map_copy = pltpu.make_async_copy(maps, maps_v, local_sem.at[0])
    up_copy = pltpu.make_async_copy(ups, ups_v, local_sem.at[1])
    small = [
        pltpu.make_async_copy(pos, pos_v, local_sem.at[2]),
        pltpu.make_async_copy(nrm, nrm_v, local_sem.at[3]),
        pltpu.make_async_copy(area, area_v, local_sem.at[4]),
        pltpu.make_async_copy(kry.at[kry.shape[0] - 1], kry_v, local_sem.at[5]),
    ]
    for copy in small + copies:
        copy.start()
    home = [
        pltpu.make_async_copy(fix_v, posw.at[RADIUS], local_sem.at[6]),
        pltpu.make_async_copy(an_v, anw.at[RADIUS], local_sem.at[7]),
        pltpu.make_async_copy(cnt_v, cntw.at[RADIUS], local_sem.at[8]),
        pltpu.make_async_copy(info_v, cntw.at[pl.ds(SIDES, local)], local_sem.at[9]),
        pltpu.make_async_copy(mom_v, momw.at[RADIUS], local_sem.at[10]),
        pltpu.make_async_copy(grp_v, gmall.at[me], local_sem.at[11]),
        pltpu.make_async_copy(base_v, base, local_sem.at[12]),
    ]
    map_copy.start()
    up_copy.start()
    for copy in small:
        copy.wait()
    fix_v[...] = jnp.floor(pos_v[...] * FIXED + 0.5).astype(jnp.int32).astype(jnp.int16)
    home[0].start()
    parts = [(nrm_v[a] * area_v[...]).astype(BF16).astype(F32) for a in range(3)]
    an_v[: 3 * local] = jnp.concatenate(parts, axis=0).astype(BF16)
    lane = lax.broadcasted_iota(jnp.int32, (1, 128), 1)
    counts = jnp.zeros((1, 128), jnp.int32)
    for c in range(local):
        counts = jnp.where(lane == c, cnt[c], counts)
    cnt_v[...] = counts
    home[2].start()
    for c in range(local):
        row = jnp.where(lane == 6, used[c], (me - RADIUS) * local)
        for n in range(near.shape[1]):
            row = jnp.where(lane == 8 + n, near[c, n], row)
        info_v[c] = row
    home[3].start()
    pl.semaphore_wait(barrier, total - 1)

    def to_neighbours(own, ref, kind, rows=None):
        made = []

        def slot(side):
            return ref.at[side] if rows is None else ref.at[side, rows]

        for n, d in enumerate([1, -1, 2, -2, 3, -3]):
            made.append(
                pltpu.make_async_remote_copy(
                    src_ref=own if rows is None else own.at[rows],
                    dst_ref=slot(RADIUS - d),
                    send_sem=send_sem.at[kind, n],
                    recv_sem=recv_sem.at[kind, n],
                    device_id=coords(lax.rem(me + d + total, total), devs),
                    device_id_type=MESH,
                )
            )
        for copy in made:
            copy.start()
        return made

    sent = to_neighbours(fix_v, posw, 0)
    sent += to_neighbours(an_v, anw, 4, pl.ds(0, 3 * local))
    sent += to_neighbours(cnt_v, cntw, 1)
    live = live_mask(cnt, (local, panels))
    current = kry_v[...].astype(BF16)
    density = jnp.zeros((local, panels), F32)
    for c in range(local):
        copies[c].wait()
        found = mm(current, binv_v[c], NT)
        density = jnp.where(row_is(found.shape, c), found, density)
    rounded = jnp.where(live, density, 0.0).astype(BF16)
    an_v[3 * local :] = rounded
    base_v[...] = 0.5 * rounded.astype(F32)
    home[1].start()
    sent += to_neighbours(an_v, anw, 2, pl.ds(3 * local, local))
    map_copy.wait()
    moments = jnp.zeros((local, coeffs), F32)
    for c in range(local):
        found = mm(rounded, maps_v[c], NT)
        moments = jnp.where(row_is(found.shape, c), found, moments)
    moments = moments.astype(BF16)
    mom_v[...] = moments
    home[4].start()
    sent += to_neighbours(mom_v, momw, 3)
    up_copy.wait()
    merged = jnp.zeros((local, coeffs), F32)
    for k in range(local):
        found = mm(moments, ups_v[k], NT)
        merged = jnp.where(row_is(found.shape, k), found, merged)
    grp_v[...] = jnp.sum(merged, axis=0, keepdims=True)
    home[5].start()

    def group_copy(slot, other):
        return pltpu.make_async_remote_copy(
            src_ref=grp_v,
            dst_ref=gmall.at[slot],
            send_sem=gsend.at[other],
            recv_sem=grecv.at[slot],
            device_id=coords(other, devs),
            device_id_type=MESH,
        )

    far_first(me, roles, devs, lambda other: group_copy(me, other).start())
    own_near(
        pos_v, parts, rounded.astype(F32), feat, goal, src, wgt, (sq0, sq1), (g0, g1), acc, base_v
    )
    home[6].start()
    for copy in home + sent:
        copy.wait()
    far_first(me, roles, devs, lambda other: group_copy(other, other).wait())


def near_kernel(
    infoh,
    posh,
    anh,
    out,
    info,
    posw,
    anw,
    sems,
    feat,
    goal,
    src,
    wgt,
    sq0,
    sq1,
    g0,
    g1,
    acc,
    begin,
    spans,
):
    local, panels = out.shape
    wide = goal.shape[2]
    per_h = panels // wide
    tally = pltpu.make_async_copy(infoh.at[pl.ds(0, SIDES + local)], info, sems.at[2, 0])
    tally.start()
    order = [RADIUS] + [k for k in range(SIDES) if k != RADIUS]
    loads = []
    for k in order:
        loads.append(pltpu.make_async_copy(posh.at[k], posw.at[k], sems.at[0, k]))
        loads.append(pltpu.make_async_copy(anh.at[k], anw.at[k], sems.at[1, k]))
    for copy in loads:
        copy.start()
    for n, side in enumerate(order):
        loads[2 * n].wait()
        loads[2 * n + 1].wait()
        fields = anw[side].astype(F32)
        dens = fields[3 * local :]
        weights = [fields[a * local : (a + 1) * local] * dens for a in range(3)]
        centres = posw[side].astype(jnp.int32).astype(F32) * (1.0 / FIXED)
        spread_all(feat.at[side], [centres[a] for a in range(3)], weights)
    tally.wait()
    first = info[SIDES, 0, 7]

    def cluster_body(c, start):
        made = goal_rows(read_features(feat.at[RADIUS], c))
        for h in range(per_h):
            goal[per_h * c + h] = made[:, h * wide : (h + 1) * wide]

        def slot_body(s, offset):
            w = info[SIDES + c, 0, 8 + s] - first
            side = w // local
            inner = lax.rem(w, local)
            made, pulled = source_rows(read_features(feat.at[side], inner))
            for b in range(panels // 128):
                src[offset + b] = made[:, b * 128 : (b + 1) * 128]
                wgt[offset + b] = pulled[:, b * 128 : (b + 1) * 128]
            return offset + (info[side, 0, inner] + 127) // 128

        end = lax.fori_loop(0, info[SIDES + c, 0, 6], slot_body, start)
        pad_rows = lax.broadcasted_iota(jnp.int32, (48, 128), 0)
        src[end] = jnp.where(pad_rows >= 44, 1.0, 0.0).astype(BF16)
        wgt[end] = jnp.zeros((16, 128), BF16)
        stop = (end + 1) // 2 * 2
        begin[c] = start // 2
        spans[c] = (info[RADIUS, 0, c] + wide - 1) // wide
        return stop

    end = lax.fori_loop(0, local, cluster_body, 0)
    begin[local] = end // 2
    begin[local + 1] = end // 2
    spans[local] = 1
    acc[...] = jnp.zeros(acc.shape, F32)

    def advance(state):
        c, h, b = state
        over = b + 1 >= begin[jnp.minimum(c + 1, local)]
        h = jnp.where(over, h + 1, h)
        done = h >= spans[c]
        b = jnp.where(over, begin[c], b + 1)
        c_next = jnp.where(done, jnp.minimum(c + 1, local), c)
        b = jnp.where(done, begin[c_next], b)
        return c_next, jnp.where(done, 0, h), b

    def products(state, ref):
        c, h, b = state
        squares(src, b, goal[per_h * c + h], ref)

    def count_body(c, total):
        return total + spans[c] * (begin[c + 1] - begin[c])

    units = lax.fori_loop(0, local, count_body, 0)
    origin = (jnp.int32(0), jnp.int32(0), jnp.int32(0))
    products(origin, sq0)
    cubes(sq0, g0)
    second = advance(origin)
    products(second, sq1)

    def body(t, states):
        old, state = states
        for u in range(UNITS):
            later = advance(state)
            products(later, (sq0, sq1)[u % 2])
            cubes((sq1, sq0)[u % 2], (g1, g0)[u % 2])
            c, h, b = old
            acc[per_h * c + h] += gathered(wgt, b, (g0, g1)[u % 2])
            old, state = state, later
        return old, state

    lax.fori_loop(0, (units + UNITS - 1) // UNITS, body, (origin, second))
    for c in range(local):
        own = read_features(feat.at[RADIUS], c)
        for h in range(per_h):
            part = slice(h * wide, (h + 1) * wide)
            out[c : c + 1, part] = combine(own[:, part], acc[per_h * c + h])


def finish_kernel(
    roles,
    devs,
    cnt,
    glist,
    gkind,
    llist,
    lkind,
    momw,
    gmall,
    near,
    base,
    kry,
    maps_v,
    ups_v,
    fars_v,
    image_out,
    sums_out,
    red,
    send_sem,
    recv_sem,
):
    me, total = place(roles, devs)
    local, panels = near.shape
    coeffs = maps_v.shape[1]
    kinds = fars_v.shape[1]
    window = SIDES * local
    barrier = greet(me, roles, devs)

    groups = gmall[...].reshape(total, coeffs)
    g_rows = lax.broadcasted_iota(jnp.int32, (kinds, total), 0)
    g_lanes = lax.broadcasted_iota(jnp.int32, (kinds, total), 1)
    g_hot = jnp.zeros((kinds, total), F32)
    for n in range(glist.shape[1]):
        g_hot += jnp.where((g_rows == gkind[0, n]) & (g_lanes == glist[0, n]), 1.0, 0.0)
    g_hot = g_hot.astype(BF16)
    hi, mid, low = splits(groups)
    g_sum = mm(g_hot, hi.astype(BF16), NN) + mm(g_hot, mid.astype(BF16), NN)
    g_sum += mm(g_hot, low.astype(BF16), NN)
    g_both = halves(g_sum)

    lanes = lax.broadcasted_iota(jnp.int32, (local, window), 1)
    shift = (me - RADIUS) * local
    hots = [jnp.zeros((local, window), F32) for _ in range(kinds)]
    for n in range(llist.shape[1]):
        hit = lanes == (llist[:, n : n + 1] - shift)
        kind = jnp.broadcast_to(lkind[:, n : n + 1], (local, window))
        for o in range(kinds):
            hots[o] = hots[o] + jnp.where(hit & (kind == o), 1.0, 0.0)
    hot = jnp.concatenate(hots, axis=0).astype(BF16)
    held = jnp.concatenate([momw[side].astype(F32) for side in range(SIDES)], axis=0)
    summed = mm(hot, held.astype(BF16), NN)

    g_parts = jnp.zeros((kinds, coeffs), F32)
    for o in range(kinds):
        found = mm(g_both, fars_v[1, o], NT)
        found = found[:kinds] + found[kinds:]
        g_parts = jnp.where(row_is(found.shape, o), found, g_parts)
    g_local = jnp.sum(g_parts, axis=0, keepdims=True).astype(BF16)
    leaf = jnp.zeros((local, coeffs), F32)
    for o in range(kinds):
        found = mm(halves(summed[o * local : (o + 1) * local]), fars_v[0, o], NT)
        leaf = leaf + found[:local] + found[local:]
    g_wide = jnp.broadcast_to(g_local.astype(F32), (local, coeffs)).astype(BF16)
    down = jnp.zeros((local, coeffs), F32)
    for k in range(local):
        found = mm(g_wide, ups_v[k], NN)
        down = jnp.where(row_is(found.shape, k), found, down)
    leaf = (leaf + down).astype(BF16)
    far = jnp.zeros((local, panels), F32)
    for c in range(local):
        found = mm(leaf, maps_v[c], NN)
        far = jnp.where(row_is(found.shape, c), found, far)
    live = live_mask(cnt, (local, panels))
    image = jnp.where(live, base[...] + near[...] + far, 0.0)

    lane = lax.broadcasted_iota(jnp.int32, (1, 128), 1)
    count = kry.shape[0]
    row = jnp.zeros((1, 128), F32)
    for k in range(count + 1):
        part = image * (kry[k] if k < count else image)
        value = jnp.sum(jnp.sum(part, axis=0, keepdims=True), axis=1, keepdims=True)
        row = jnp.where(lane == k, value, row)
    red[me] = row
    image_out[...] = image
    pl.semaphore_wait(barrier, total - 1)

    def row_copy(slot, other):
        return pltpu.make_async_remote_copy(
            src_ref=red.at[me],
            dst_ref=red.at[slot],
            send_sem=send_sem.at[other],
            recv_sem=recv_sem.at[slot],
            device_id=coords(other, devs),
            device_id_type=MESH,
        )

    far_first(me, roles, devs, lambda other: row_copy(me, other).start())
    far_first(me, roles, devs, lambda other: row_copy(other, other).wait())
    scale = 1.0 / (total * local * panels)
    sums_out[...] = jnp.sum(red[...], axis=0) * scale


def update_kernel(sums_ref, image, kry, nxt, hess):
    count = kry.shape[0]
    sums = sums_ref[...]
    lane = lax.broadcasted_iota(jnp.int32, sums.shape, 1)
    rest = image[...]
    energy = sums[:, count : count + 1]
    for k in range(count):
        c_k = sums[:, k : k + 1]
        rest = rest - c_k * kry[k]
        energy = energy - c_k * c_k
    height = jnp.sqrt(energy + EPSILON)
    nxt[...] = rest / height
    hess[...] = jnp.where(lane == count, height, sums)[:, : count + 1]


def shards(
    roles,
    devs,
    positions,
    normals,
    panel_areas,
    panel_counts,
    near_lists,
    near_counts,
    leaf_lists,
    leaf_kinds,
    group_lists,
    group_kinds,
    block_inverse,
    moment_maps,
    up_operators,
    far_operators,
    krylov_basis,
):
    local, _, panels = positions.shape
    coeffs = moment_maps.shape[1]
    total = roles * devs
    wide = 256
    vmem = pl.BlockSpec(memory_space=pltpu.VMEM)
    smem = pl.BlockSpec(memory_space=pltpu.SMEM)
    hbm = pl.BlockSpec(memory_space=pltpu.HBM)
    dma = pltpu.SemaphoreType.DMA
    posw, anw, cntw, momw, gmall, base = pl.pallas_call(
        functools.partial(source_kernel, roles, devs),
        name="sources",
        out_shape=(
            jax.ShapeDtypeStruct((SPARE // (6 * local * panels), 3, local, panels), jnp.int16),
            jax.ShapeDtypeStruct((SPARE // (8 * local * panels), 4 * local, panels), BF16),
            jax.ShapeDtypeStruct((SPARE // 512, 1, 128), jnp.int32),
            jax.ShapeDtypeStruct((SIDES, local, coeffs), BF16),
            jax.ShapeDtypeStruct((total, 1, coeffs), F32),
            jax.ShapeDtypeStruct((local, panels), F32),
        ),
        in_specs=[smem] * 3 + [hbm] * 7,
        out_specs=(hbm,) * 6,
        scratch_shapes=[
            pltpu.VMEM((local, coeffs), BF16),
            pltpu.VMEM((1, coeffs), F32),
            pltpu.VMEM((local, panels), F32),
            pltpu.VMEM((3, local, panels), F32),
            pltpu.VMEM((3, local, panels), jnp.int16),
            pltpu.VMEM((4 * local, panels), BF16),
            pltpu.VMEM((1, 128), jnp.int32),
            pltpu.VMEM((local, 1, 128), jnp.int32),
            pltpu.VMEM((3, local, panels), F32),
            pltpu.VMEM((local, panels), F32),
            pltpu.VMEM((local, panels), F32),
            pltpu.VMEM(block_inverse.shape, BF16),
            pltpu.VMEM(moment_maps.shape, BF16),
            pltpu.VMEM(up_operators.shape, BF16),
            dma((13,)),
            dma((local,)),
            dma((5, 6)),
            dma((5, 6)),
            dma((total,)),
            dma((total,)),
            pltpu.VMEM((panels // 128, 8 * local, 128), F32),
            pltpu.VMEM((local * (panels // wide), 48, wide), BF16),
            pltpu.VMEM((local * (panels // 128), 48, 128), BF16),
            pltpu.VMEM((local * (panels // 128), 16, 128), BF16),
            pltpu.VMEM((256, wide), F32),
            pltpu.VMEM((256, wide), F32),
            pltpu.VMEM((256, wide), BF16),
            pltpu.VMEM((256, wide), BF16),
            pltpu.VMEM((local * (panels // wide), 16, wide), F32),
        ],
        compiler_params=pltpu.CompilerParams(
            collective_id=0, has_side_effects=True, vmem_limit_bytes=62 << 20
        ),
    )(
        panel_counts,
        near_lists,
        near_counts,
        jnp.transpose(positions, (1, 0, 2)),
        jnp.transpose(normals, (1, 0, 2)),
        panel_areas,
        krylov_basis,
        block_inverse,
        moment_maps,
        up_operators,
    )
    room = local * (near_lists.shape[1] * (panels // 128) + 1) + 8
    goals = (local + 1) * (panels // wide)
    near = pl.pallas_call(
        near_kernel,
        name="near",
        cost_estimate=pl.CostEstimate(
            flops=40 * local * panels * panels * (near_lists.shape[1] + 1),
            bytes_accessed=48 * local * panels * SIDES,
            transcendentals=local * panels * panels * (near_lists.shape[1] + 1),
        ),
        out_shape=jax.ShapeDtypeStruct((local, panels), F32),
        in_specs=[hbm, hbm, hbm],
        out_specs=vmem,
        scratch_shapes=[
            pltpu.SMEM((SIDES + local, 1, 128), jnp.int32),
            pltpu.VMEM((SIDES, 3, local, panels), jnp.int16),
            pltpu.VMEM((SIDES, 4 * local, panels), BF16),
            dma((3, SIDES)),
            pltpu.VMEM((SIDES, panels // 128, 8 * local, 128), F32),
            pltpu.VMEM((goals, 48, wide), BF16),
            pltpu.VMEM((room, 48, 128), BF16),
            pltpu.VMEM((room, 16, 128), BF16),
            pltpu.VMEM((256, wide), F32),
            pltpu.VMEM((256, wide), F32),
            pltpu.VMEM((256, wide), BF16),
            pltpu.VMEM((256, wide), BF16),
            pltpu.VMEM((goals, 16, wide), F32),
            pltpu.SMEM((local + 2,), jnp.int32),
            pltpu.SMEM((local + 2,), jnp.int32),
        ],
        compiler_params=pltpu.CompilerParams(vmem_limit_bytes=52 << 20),
    )(cntw, posw, anw)
    image, sums = pl.pallas_call(
        functools.partial(finish_kernel, roles, devs),
        name="finish",
        out_shape=(
            jax.ShapeDtypeStruct((local, panels), F32),
            jax.ShapeDtypeStruct((1, 128), F32),
        ),
        in_specs=[smem, smem, smem] + [vmem] * 10,
        out_specs=(vmem, vmem),
        scratch_shapes=[
            pltpu.VMEM((total, 1, 128), F32),
            dma((total,)),
            dma((total,)),
        ],
        compiler_params=pltpu.CompilerParams(
            collective_id=1, has_side_effects=True, vmem_limit_bytes=14 << 20
        ),
    )(
        panel_counts,
        group_lists,
        group_kinds,
        leaf_lists,
        leaf_kinds,
        momw,
        gmall,
        near,
        base,
        krylov_basis,
        moment_maps,
        up_operators,
        far_operators,
    )
    nxt, hess = pl.pallas_call(
        update_kernel,
        name="update",
        out_shape=(
            jax.ShapeDtypeStruct((local, panels), F32),
            jax.ShapeDtypeStruct((1, krylov_basis.shape[0] + 1), F32),
        ),
        in_specs=[vmem] * 3,
        out_specs=(vmem, vmem),
        compiler_params=pltpu.CompilerParams(vmem_limit_bytes=8 << 20),
    )(sums, image, krylov_basis)
    return nxt, jnp.reshape(hess, (krylov_basis.shape[0] + 1,))


def solution(mesh):
    roles, devs = mesh.shape["role"], mesh.shape["dev"]
    return jax.shard_map(
        functools.partial(shards, roles, devs),
        mesh=mesh,
        in_specs=(
            P(AXES, None, None),
            P(AXES, None, None),
            P(AXES, None),
            P(AXES),
            P(AXES, None),
            P(AXES),
            P(AXES, None),
            P(AXES, None),
            P(AXES, None),
            P(AXES, None),
            P(AXES, None, None),
            P(AXES, None, None),
            P(),
            P(),
            P(None, AXES, None),
        ),
        out_specs=(P(AXES, None), P()),
        check_vma=False,
    )
```

```python
import functools

import jax
import jax.numpy as jnp
from jax import lax
from jax.experimental import pallas as pl
from jax.experimental.pallas import tpu as pltpu
from jax.sharding import PartitionSpec as P

RADIUS = 3
SIDES = 2 * RADIUS + 1
SOFTEN = 0.01
EPSILON = 1e-06
UNITS = 24
SPARE = 12 << 20
FIXED = 32767.0
MESH = pl.DeviceIdType.MESH
NT = (((1,), (1,)), ((), ()))
NN = (((1,), (0,)), ((), ()))
TN = (((0,), (0,)), ((), ()))
F32 = jnp.float32
BF16 = jnp.bfloat16
AXES = ("role", "dev")


def mm(a, b, dims):
    return lax.dot_general(a, b, dims, preferred_element_type=F32)


def row_is(shape, k):
    return lax.broadcasted_iota(jnp.int32, shape, 0) == k


def place(roles, devs):
    me = lax.axis_index("role") * devs + lax.axis_index("dev")
    return me, roles * devs


def coords(linear, devs):
    return (linear // devs, lax.rem(linear, devs))


def far_first(me, roles, devs, visit):
    own = lax.rem(me, devs)

    def body(t, ends):
        low, high = ends
        left = own - low >= high - own
        other = jnp.where(left, low, high)
        for r in range(roles):
            visit(r * devs + other)
        return jnp.where(left, low + 1, low), jnp.where(left, high, high - 1)

    ends = (jnp.int32(0), jnp.int32(devs - 1))
    for t in range(devs - 1):
        ends = body(t, ends)
    for r in range(1, roles):
        visit(lax.rem(me + r * devs, roles * devs))


def greet(me, roles, devs):
    barrier = pltpu.get_barrier_semaphore()

    def visit(other):
        pl.semaphore_signal(barrier, inc=1, device_id=coords(other, devs), device_id_type=MESH)

    far_first(me, roles, devs, visit)
    return barrier


def live_mask(cnt_ref, shape):
    rows = lax.broadcasted_iota(jnp.int32, shape, 0)
    limit = jnp.zeros(shape, jnp.int32)
    for c in range(shape[0]):
        limit = jnp.where(rows == c, cnt_ref[c], limit)
    return lax.broadcasted_iota(jnp.int32, shape, 1) < limit


def halves(x):
    hi = x.astype(BF16).astype(F32)
    return jnp.concatenate([hi, x - hi], axis=0).astype(BF16)


def splits(x):
    hi = x.astype(BF16).astype(F32)
    rest = x - hi
    mid = rest.astype(BF16).astype(F32)
    return hi, mid, rest - mid


def pack(parts):
    return jnp.concatenate(parts, axis=0).astype(BF16)


def spread_all(feat, positions, weights):
    local, panels = positions[0].shape
    norm = jnp.zeros((local, panels), F32)
    inside = jnp.zeros((local, panels), F32)
    for y, w in zip(positions, weights):
        norm = norm + y * y
        inside = inside - y * w
    rows = list(positions) + [norm] + list(weights) + [inside]
    for k, value in enumerate(rows):
        for b in range(panels // 128):
            feat[b, k * local : (k + 1) * local, :] = value[:, b * 128 : (b + 1) * 128]


def read_features(feat, inner):
    at = pl.ds(inner, 8, stride=feat.shape[1] // 8)
    return jnp.concatenate([feat[b, at, :] for b in range(feat.shape[0])], axis=1)


def goal_rows(own):
    shape = own.shape
    rows = lax.broadcasted_iota(jnp.int32, shape, 0)
    x = jnp.where(rows < 3, -2.0 * own, jnp.where(rows == 3, own + SOFTEN, 0.0))
    hi, mid, low = splits(x)
    norms = [jnp.broadcast_to(part[3:4], shape) for part in (hi, mid, low)]
    firm = jnp.where(rows < 3, hi, jnp.where(rows == 3, 1.0, 0.0))
    soft = jnp.where(rows < 3, mid, 0.0)
    last = jnp.where(rows < 3, low, 0.0)
    tail = soft
    for k in range(3):
        tail = jnp.where(rows == 4 + k, norms[k], tail)
    return pack([firm, firm, firm, soft, last, tail])


def source_rows(own):
    rows = lax.broadcasted_iota(jnp.int32, own.shape, 0)
    hi, mid, low = splits(own)
    made = pack([hi, mid, low, hi, hi, jnp.where(rows < 4, mid, 1.0)])
    return made, pack([jnp.where(rows < 4, pltpu.roll(mid, 4, 0), hi), low])


def squares(src, block, target, ref):
    for k in range(2):
        ref[k * 128 : (k + 1) * 128, :] = mm(src[2 * block + k], target, TN)


def cubes(a, b):
    inverse = lax.rsqrt(a[...])
    b[...] = (inverse * inverse * inverse).astype(BF16)


def gathered(wgt, block, ref):
    both = jnp.concatenate([wgt[2 * block], wgt[2 * block + 1]], axis=1)
    return mm(both, ref[...], NN)


def combine(own, got):
    total = got[:8] + pltpu.roll(got[:8], 4, 0) + got[8:]
    rows = lax.broadcasted_iota(jnp.int32, total.shape, 0)
    part = total * pltpu.roll(own, 4, 0)
    value = jnp.where(rows < 4, 0.0, jnp.where(rows == 7, total, part))
    return jnp.sum(value, axis=0, keepdims=True)


def own_near(pos_v, nrm_parts, density, feat, goal, src, wgt, sqs, gs, acc, out):
    local, panels = density.shape
    wide = goal.shape[2]
    per_h = panels // wide
    blocks = panels // 256
    positions = [pos_v[a] for a in range(3)]
    spread_all(feat, positions, [part * density for part in nrm_parts])
    for c in range(local):
        own = read_features(feat, c)
        made = goal_rows(own)
        for h in range(per_h):
            goal[per_h * c + h] = made[:, h * wide : (h + 1) * wide]
        made, pulled = source_rows(own)
        for b in range(panels // 128):
            src[2 * blocks * c + b] = made[:, b * 128 : (b + 1) * 128]
            wgt[2 * blocks * c + b] = pulled[:, b * 128 : (b + 1) * 128]
    acc[...] = jnp.zeros(acc.shape, F32)
    units = local * per_h * blocks

    def place_of(n):
        n = lax.rem(n, units)
        c = n // (per_h * blocks)
        return n // blocks, c * blocks + lax.rem(n, blocks)

    def start(n, ref):
        g, b = place_of(n)
        squares(src, b, goal[g], ref)

    start(0, sqs[0])
    cubes(sqs[0], gs[0])
    start(1, sqs[1])
    steps = 16

    def body(t, carry):
        for u in range(steps):
            n = t * steps + u
            start(n + 2, sqs[u % 2])
            cubes(sqs[(u + 1) % 2], gs[(u + 1) % 2])
            g, b = place_of(n)
            acc[g] += gathered(wgt, b, gs[u % 2])
        return carry

    lax.fori_loop(0, units // steps, body, 0)
    for c in range(local):
        own = read_features(feat, c)
        for h in range(per_h):
            part = slice(h * wide, (h + 1) * wide)
            out[c : c + 1, part] = out[c : c + 1, part] + combine(own[:, part], acc[per_h * c + h])


def source_kernel(
    roles,
    devs,
    cnth,
    nearh,
    usedh,
    pos,
    nrm,
    area,
    kry,
    binv,
    maps,
    ups,
    posw,
    anw,
    cntw,
    momw,
    gmall,
    base,
    mask,
    cnt,
    near,
    used,
    mom_v,
    grp_v,
    base_v,
    mask_v,
    pos_v,
    fix_v,
    an_v,
    cnt_v,
    info_v,
    nrm_v,
    area_v,
    kry_v,
    binv_v,
    maps_v,
    ups_v,
    local_sem,
    big_sem,
    send_sem,
    recv_sem,
    gsend,
    grecv,
    feat,
    goal,
    src,
    wgt,
    sq0,
    sq1,
    g0,
    g1,
    acc,
):
    me, total = place(roles, devs)
    local, panels = area.shape
    coeffs = maps_v.shape[1]
    barrier = greet(me, roles, devs)
    copies = []
    for c in range(local):
        copies.append(pltpu.make_async_copy(binv.at[c], binv_v.at[c], big_sem.at[c]))
    map_copy = pltpu.make_async_copy(maps, maps_v, local_sem.at[0])
    up_copy = pltpu.make_async_copy(ups, ups_v, local_sem.at[1])
    small = [
        pltpu.make_async_copy(cnth, cnt, local_sem.at[13]),
        pltpu.make_async_copy(nearh, near, local_sem.at[14]),
        pltpu.make_async_copy(usedh, used, local_sem.at[15]),
        pltpu.make_async_copy(pos, pos_v, local_sem.at[2]),
        pltpu.make_async_copy(nrm, nrm_v, local_sem.at[3]),
        pltpu.make_async_copy(area, area_v, local_sem.at[4]),
        pltpu.make_async_copy(kry.at[kry.shape[0] - 1], kry_v, local_sem.at[5]),
    ]
    for copy in small + copies:
        copy.start()
    home = [
        pltpu.make_async_copy(fix_v, posw.at[RADIUS], local_sem.at[6]),
        pltpu.make_async_copy(an_v, anw.at[RADIUS], local_sem.at[7]),
        pltpu.make_async_copy(cnt_v, cntw.at[RADIUS], local_sem.at[8]),
        pltpu.make_async_copy(info_v, cntw.at[pl.ds(SIDES, local)], local_sem.at[9]),
        pltpu.make_async_copy(mom_v, momw.at[RADIUS], local_sem.at[10]),
        pltpu.make_async_copy(grp_v, gmall.at[me], local_sem.at[11]),
        pltpu.make_async_copy(base_v, base, local_sem.at[12]),
        pltpu.make_async_copy(mask_v, mask, local_sem.at[16]),
    ]
    map_copy.start()
    up_copy.start()
    for copy in small:
        copy.wait()
    fix_v[...] = jnp.floor(pos_v[...] * FIXED + 0.5).astype(jnp.int32).astype(jnp.int16)
    home[0].start()
    parts = [(nrm_v[a] * area_v[...]).astype(BF16).astype(F32) for a in range(3)]
    an_v[: 3 * local] = jnp.concatenate(parts, axis=0).astype(BF16)
    lane = lax.broadcasted_iota(jnp.int32, (1, 128), 1)
    counts = jnp.zeros((1, 128), jnp.int32)
    for c in range(local):
        counts = jnp.where(lane == c, cnt[c], counts)
    cnt_v[...] = counts
    home[2].start()
    for c in range(local):
        row = jnp.where(lane == 6, used[c], (me - RADIUS) * local)
        for n in range(near.shape[1]):
            row = jnp.where(lane == 8 + n, near[c, n], row)
        info_v[c] = row
    home[3].start()
    pl.semaphore_wait(barrier, total - 1)

    def to_neighbours(own, ref, kind, rows=None):
        made = []

        def slot(side):
            return ref.at[side] if rows is None else ref.at[side, rows]

        for n, d in enumerate([1, -1, 2, -2, 3, -3]):
            made.append(
                pltpu.make_async_remote_copy(
                    src_ref=own if rows is None else own.at[rows],
                    dst_ref=slot(RADIUS - d),
                    send_sem=send_sem.at[kind, n],
                    recv_sem=recv_sem.at[kind, n],
                    device_id=coords(lax.rem(me + d + total, total), devs),
                    device_id_type=MESH,
                )
            )
        for copy in made:
            copy.start()
        return made

    sent = to_neighbours(fix_v, posw, 0)
    sent += to_neighbours(an_v, anw, 4, pl.ds(0, 3 * local))
    sent += to_neighbours(cnt_v, cntw, 1)
    live = live_mask(cnt, (local, panels))
    current = kry_v[...].astype(BF16)
    density = jnp.zeros((local, panels), F32)
    for c in range(local):
        copies[c].wait()
        found = mm(current, binv_v[c], NT)
        density = jnp.where(row_is(found.shape, c), found, density)
    rounded = jnp.where(live, density, 0.0).astype(BF16)
    an_v[3 * local :] = rounded
    base_v[...] = 0.5 * rounded.astype(F32)
    mask_v[...] = jnp.where(live, 1.0, 0.0)
    home[7].start()
    home[1].start()
    sent += to_neighbours(an_v, anw, 2, pl.ds(3 * local, local))
    map_copy.wait()
    moments = jnp.zeros((local, coeffs), F32)
    for c in range(local):
        found = mm(rounded, maps_v[c], NT)
        moments = jnp.where(row_is(found.shape, c), found, moments)
    moments = moments.astype(BF16)
    mom_v[...] = moments
    home[4].start()
    sent += to_neighbours(mom_v, momw, 3)
    up_copy.wait()
    merged = jnp.zeros((local, coeffs), F32)
    for k in range(local):
        found = mm(moments, ups_v[k], NT)
        merged = jnp.where(row_is(found.shape, k), found, merged)
    grp_v[...] = jnp.sum(merged, axis=0, keepdims=True)
    home[5].start()

    def group_copy(slot, other):
        return pltpu.make_async_remote_copy(
            src_ref=grp_v,
            dst_ref=gmall.at[slot],
            send_sem=gsend.at[other],
            recv_sem=grecv.at[slot],
            device_id=coords(other, devs),
            device_id_type=MESH,
        )

    far_first(me, roles, devs, lambda other: group_copy(me, other).start())
    own_near(
        pos_v, parts, rounded.astype(F32), feat, goal, src, wgt, (sq0, sq1), (g0, g1), acc, base_v
    )
    home[6].start()
    for copy in home + sent:
        copy.wait()
    far_first(me, roles, devs, lambda other: group_copy(other, other).wait())


def near_kernel(
    infoh,
    posh,
    anh,
    out,
    info,
    posw,
    anw,
    sems,
    feat,
    goal,
    src,
    wgt,
    sq0,
    sq1,
    g0,
    g1,
    acc,
    begin,
    spans,
):
    local, panels = out.shape
    wide = goal.shape[2]
    per_h = panels // wide
    tally = pltpu.make_async_copy(infoh.at[pl.ds(0, SIDES + local)], info, sems.at[2, 0])
    tally.start()
    order = [RADIUS] + [k for k in range(SIDES) if k != RADIUS]
    loads = []
    for k in order:
        loads.append(pltpu.make_async_copy(posh.at[k], posw.at[k], sems.at[0, k]))
        loads.append(pltpu.make_async_copy(anh.at[k], anw.at[k], sems.at[1, k]))
    for copy in loads:
        copy.start()
    for n, side in enumerate(order):
        loads[2 * n].wait()
        loads[2 * n + 1].wait()
        fields = anw[side].astype(F32)
        dens = fields[3 * local :]
        weights = [fields[a * local : (a + 1) * local] * dens for a in range(3)]
        centres = posw[side].astype(jnp.int32).astype(F32) * (1.0 / FIXED)
        spread_all(feat.at[side], [centres[a] for a in range(3)], weights)
    tally.wait()
    first = info[SIDES, 0, 7]

    def cluster_body(c, start):
        made = goal_rows(read_features(feat.at[RADIUS], c))
        for h in range(per_h):
            goal[per_h * c + h] = made[:, h * wide : (h + 1) * wide]

        def slot_body(s, offset):
            w = info[SIDES + c, 0, 8 + s] - first
            side = w // local
            inner = lax.rem(w, local)
            made, pulled = source_rows(read_features(feat.at[side], inner))
            for b in range(panels // 128):
                src[offset + b] = made[:, b * 128 : (b + 1) * 128]
                wgt[offset + b] = pulled[:, b * 128 : (b + 1) * 128]
            return offset + (info[side, 0, inner] + 127) // 128

        end = lax.fori_loop(0, info[SIDES + c, 0, 6], slot_body, start)
        pad_rows = lax.broadcasted_iota(jnp.int32, (48, 128), 0)
        src[end] = jnp.where(pad_rows >= 44, 1.0, 0.0).astype(BF16)
        wgt[end] = jnp.zeros((16, 128), BF16)
        stop = (end + 1) // 2 * 2
        begin[c] = start // 2
        spans[c] = (info[RADIUS, 0, c] + wide - 1) // wide
        return stop

    end = lax.fori_loop(0, local, cluster_body, 0)
    begin[local] = end // 2
    begin[local + 1] = end // 2
    spans[local] = 1
    acc[...] = jnp.zeros(acc.shape, F32)

    def advance(state):
        c, h, b = state
        over = b + 1 >= begin[jnp.minimum(c + 1, local)]
        h = jnp.where(over, h + 1, h)
        done = h >= spans[c]
        b = jnp.where(over, begin[c], b + 1)
        c_next = jnp.where(done, jnp.minimum(c + 1, local), c)
        b = jnp.where(done, begin[c_next], b)
        return c_next, jnp.where(done, 0, h), b

    def products(state, ref):
        c, h, b = state
        squares(src, b, goal[per_h * c + h], ref)

    def count_body(c, total):
        return total + spans[c] * (begin[c + 1] - begin[c])

    units = lax.fori_loop(0, local, count_body, 0)
    origin = (jnp.int32(0), jnp.int32(0), jnp.int32(0))
    products(origin, sq0)
    cubes(sq0, g0)
    second = advance(origin)
    products(second, sq1)

    def body(t, states):
        old, state = states
        for u in range(UNITS):
            later = advance(state)
            products(later, (sq0, sq1)[u % 2])
            cubes((sq1, sq0)[u % 2], (g1, g0)[u % 2])
            c, h, b = old
            acc[per_h * c + h] += gathered(wgt, b, (g0, g1)[u % 2])
            old, state = state, later
        return old, state

    lax.fori_loop(0, (units + UNITS - 1) // UNITS, body, (origin, second))
    for c in range(local):
        own = read_features(feat.at[RADIUS], c)
        for h in range(per_h):
            part = slice(h * wide, (h + 1) * wide)
            out[c : c + 1, part] = combine(own[:, part], acc[per_h * c + h])


def finish_kernel(
    roles,
    devs,
    live,
    glist,
    gkind,
    llist,
    lkind,
    momw,
    gmall,
    near,
    base,
    kry,
    maps_v,
    ups_v,
    fars_v,
    image_out,
    sums_out,
    red,
    send_sem,
    recv_sem,
):
    me, total = place(roles, devs)
    local, panels = near.shape
    coeffs = maps_v.shape[1]
    kinds = fars_v.shape[1]
    window = SIDES * local
    barrier = greet(me, roles, devs)

    groups = gmall[...].reshape(total, coeffs)
    g_rows = lax.broadcasted_iota(jnp.int32, (kinds, total), 0)
    g_lanes = lax.broadcasted_iota(jnp.int32, (kinds, total), 1)
    g_hot = jnp.zeros((kinds, total), F32)
    for n in range(glist.shape[1]):
        g_hot += jnp.where((g_rows == gkind[:, n : n + 1]) & (g_lanes == glist[:, n : n + 1]), 1.0, 0.0)
    g_hot = g_hot.astype(BF16)
    hi, mid, low = splits(groups)
    g_sum = mm(g_hot, hi.astype(BF16), NN) + mm(g_hot, mid.astype(BF16), NN)
    g_sum += mm(g_hot, low.astype(BF16), NN)
    g_both = halves(g_sum)

    lanes = lax.broadcasted_iota(jnp.int32, (local, window), 1)
    shift = (me - RADIUS) * local
    hots = [jnp.zeros((local, window), F32) for _ in range(kinds)]
    for n in range(llist.shape[1]):
        hit = lanes == (llist[:, n : n + 1] - shift)
        kind = jnp.broadcast_to(lkind[:, n : n + 1], (local, window))
        for o in range(kinds):
            hots[o] = hots[o] + jnp.where(hit & (kind == o), 1.0, 0.0)
    hot = jnp.concatenate(hots, axis=0).astype(BF16)
    held = jnp.concatenate([momw[side].astype(F32) for side in range(SIDES)], axis=0)
    summed = mm(hot, held.astype(BF16), NN)

    g_parts = jnp.zeros((kinds, coeffs), F32)
    for o in range(kinds):
        found = mm(g_both, fars_v[1, o], NT)
        found = found[:kinds] + found[kinds:]
        g_parts = jnp.where(row_is(found.shape, o), found, g_parts)
    g_local = jnp.sum(g_parts, axis=0, keepdims=True).astype(BF16)
    leaf = jnp.zeros((local, coeffs), F32)
    for o in range(kinds):
        found = mm(halves(summed[o * local : (o + 1) * local]), fars_v[0, o], NT)
        leaf = leaf + found[:local] + found[local:]
    g_wide = jnp.broadcast_to(g_local.astype(F32), (local, coeffs)).astype(BF16)
    down = jnp.zeros((local, coeffs), F32)
    for k in range(local):
        found = mm(g_wide, ups_v[k], NN)
        down = jnp.where(row_is(found.shape, k), found, down)
    leaf = (leaf + down).astype(BF16)
    far = jnp.zeros((local, panels), F32)
    for c in range(local):
        found = mm(leaf, maps_v[c], NN)
        far = jnp.where(row_is(found.shape, c), found, far)
    image = jnp.where(live[...] > 0.5, base[...] + near[...] + far, 0.0)

    lane = lax.broadcasted_iota(jnp.int32, (1, 128), 1)
    count = kry.shape[0]
    row = jnp.zeros((1, 128), F32)
    for k in range(count + 1):
        part = image * (kry[k] if k < count else image)
        value = jnp.sum(jnp.sum(part, axis=0, keepdims=True), axis=1, keepdims=True)
        row = jnp.where(lane == k, value, row)
    red[me] = row
    image_out[...] = image
    pl.semaphore_wait(barrier, total - 1)

    def row_copy(slot, other):
        return pltpu.make_async_remote_copy(
            src_ref=red.at[me],
            dst_ref=red.at[slot],
            send_sem=send_sem.at[other],
            recv_sem=recv_sem.at[slot],
            device_id=coords(other, devs),
            device_id_type=MESH,
        )

    far_first(me, roles, devs, lambda other: row_copy(me, other).start())
    far_first(me, roles, devs, lambda other: row_copy(other, other).wait())
    scale = 1.0 / (total * local * panels)
    sums_out[...] = jnp.sum(red[...], axis=0) * scale


def update_kernel(sums_ref, image, kry, nxt, hess):
    count = kry.shape[0]
    sums = sums_ref[...]
    lane = lax.broadcasted_iota(jnp.int32, sums.shape, 1)
    rest = image[...]
    energy = sums[:, count : count + 1]
    for k in range(count):
        c_k = sums[:, k : k + 1]
        rest = rest - c_k * kry[k]
        energy = energy - c_k * c_k
    height = jnp.sqrt(energy + EPSILON)
    nxt[...] = rest / height
    hess[...] = jnp.where(lane == count, height, sums)[:, : count + 1]


def shards(
    roles,
    devs,
    positions,
    normals,
    panel_areas,
    panel_counts,
    near_lists,
    near_counts,
    leaf_lists,
    leaf_kinds,
    group_lists,
    group_kinds,
    block_inverse,
    moment_maps,
    up_operators,
    far_operators,
    krylov_basis,
):
    local, _, panels = positions.shape
    coeffs = moment_maps.shape[1]
    total = roles * devs
    wide = 256
    vmem = pl.BlockSpec(memory_space=pltpu.VMEM)
    smem = pl.BlockSpec(memory_space=pltpu.SMEM)
    hbm = pl.BlockSpec(memory_space=pltpu.HBM)
    dma = pltpu.SemaphoreType.DMA
    posw, anw, cntw, momw, gmall, base, live = pl.pallas_call(
        functools.partial(source_kernel, roles, devs),
        name="sources",
        out_shape=(
            jax.ShapeDtypeStruct((SPARE // (6 * local * panels), 3, local, panels), jnp.int16),
            jax.ShapeDtypeStruct((SPARE // (8 * local * panels), 4 * local, panels), BF16),
            jax.ShapeDtypeStruct((SPARE // 512, 1, 128), jnp.int32),
            jax.ShapeDtypeStruct((SIDES, local, coeffs), BF16),
            jax.ShapeDtypeStruct((total, 1, coeffs), F32),
            jax.ShapeDtypeStruct((local, panels), F32),
            jax.ShapeDtypeStruct((local, panels), F32),
        ),
        in_specs=[hbm] * 10,
        out_specs=(hbm,) * 7,
        scratch_shapes=[
            pltpu.SMEM(panel_counts.shape, jnp.int32),
            pltpu.SMEM(near_lists.shape, jnp.int32),
            pltpu.SMEM(near_counts.shape, jnp.int32),
            pltpu.VMEM((local, coeffs), BF16),
            pltpu.VMEM((1, coeffs), F32),
            pltpu.VMEM((local, panels), F32),
            pltpu.VMEM((local, panels), F32),
            pltpu.VMEM((3, local, panels), F32),
            pltpu.VMEM((3, local, panels), jnp.int16),
            pltpu.VMEM((4 * local, panels), BF16),
            pltpu.VMEM((1, 128), jnp.int32),
            pltpu.VMEM((local, 1, 128), jnp.int32),
            pltpu.VMEM((3, local, panels), F32),
            pltpu.VMEM((local, panels), F32),
            pltpu.VMEM((local, panels), F32),
            pltpu.VMEM(block_inverse.shape, BF16),
            pltpu.VMEM(moment_maps.shape, BF16),
            pltpu.VMEM(up_operators.shape, BF16),
            dma((17,)),
            dma((local,)),
            dma((5, 6)),
            dma((5, 6)),
            dma((total,)),
            dma((total,)),
            pltpu.VMEM((panels // 128, 8 * local, 128), F32),
            pltpu.VMEM((local * (panels // wide), 48, wide), BF16),
            pltpu.VMEM((local * (panels // 128), 48, 128), BF16),
            pltpu.VMEM((local * (panels // 128), 16, 128), BF16),
            pltpu.VMEM((256, wide), F32),
            pltpu.VMEM((256, wide), F32),
            pltpu.VMEM((256, wide), BF16),
            pltpu.VMEM((256, wide), BF16),
            pltpu.VMEM((local * (panels // wide), 16, wide), F32),
        ],
        compiler_params=pltpu.CompilerParams(
            collective_id=0, has_side_effects=True, vmem_limit_bytes=62 << 20
        ),
    )(
        panel_counts,
        near_lists,
        near_counts,
        jnp.transpose(positions, (1, 0, 2)),
        jnp.transpose(normals, (1, 0, 2)),
        panel_areas,
        krylov_basis,
        block_inverse,
        moment_maps,
        up_operators,
    )
    room = local * (near_lists.shape[1] * (panels // 128) + 1) + 8
    goals = (local + 1) * (panels // wide)
    near = pl.pallas_call(
        near_kernel,
        name="near",
        cost_estimate=pl.CostEstimate(
            flops=40 * local * panels * panels * (near_lists.shape[1] + 1),
            bytes_accessed=48 * local * panels * SIDES,
            transcendentals=local * panels * panels * (near_lists.shape[1] + 1),
        ),
        out_shape=jax.ShapeDtypeStruct((local, panels), F32),
        in_specs=[hbm, hbm, hbm],
        out_specs=vmem,
        scratch_shapes=[
            pltpu.SMEM((SIDES + local, 1, 128), jnp.int32),
            pltpu.VMEM((SIDES, 3, local, panels), jnp.int16),
            pltpu.VMEM((SIDES, 4 * local, panels), BF16),
            dma((3, SIDES)),
            pltpu.VMEM((SIDES, panels // 128, 8 * local, 128), F32),
            pltpu.VMEM((goals, 48, wide), BF16),
            pltpu.VMEM((room, 48, 128), BF16),
            pltpu.VMEM((room, 16, 128), BF16),
            pltpu.VMEM((256, wide), F32),
            pltpu.VMEM((256, wide), F32),
            pltpu.VMEM((256, wide), BF16),
            pltpu.VMEM((256, wide), BF16),
            pltpu.VMEM((goals, 16, wide), F32),
            pltpu.SMEM((local + 2,), jnp.int32),
            pltpu.SMEM((local + 2,), jnp.int32),
        ],
        compiler_params=pltpu.CompilerParams(vmem_limit_bytes=52 << 20),
    )(cntw, posw, anw)
    image, sums = pl.pallas_call(
        functools.partial(finish_kernel, roles, devs),
        name="finish",
        out_shape=(
            jax.ShapeDtypeStruct((local, panels), F32),
            jax.ShapeDtypeStruct((1, 128), F32),
        ),
        in_specs=[vmem] * 13,
        out_specs=(vmem, vmem),
        scratch_shapes=[
            pltpu.VMEM((total, 1, 128), F32),
            dma((total,)),
            dma((total,)),
        ],
        compiler_params=pltpu.CompilerParams(
            collective_id=1, has_side_effects=True, vmem_limit_bytes=14 << 20
        ),
    )(
        live,
        group_lists,
        group_kinds,
        leaf_lists,
        leaf_kinds,
        momw,
        gmall,
        near,
        base,
        krylov_basis,
        moment_maps,
        up_operators,
        far_operators,
    )
    nxt, hess = pl.pallas_call(
        update_kernel,
        name="update",
        out_shape=(
            jax.ShapeDtypeStruct((local, panels), F32),
            jax.ShapeDtypeStruct((1, krylov_basis.shape[0] + 1), F32),
        ),
        in_specs=[vmem] * 3,
        out_specs=(vmem, vmem),
        compiler_params=pltpu.CompilerParams(vmem_limit_bytes=8 << 20),
    )(sums, image, krylov_basis)
    return nxt, jnp.reshape(hess, (krylov_basis.shape[0] + 1,))


def solution(mesh):
    roles, devs = mesh.shape["role"], mesh.shape["dev"]
    return jax.shard_map(
        functools.partial(shards, roles, devs),
        mesh=mesh,
        in_specs=(
            P(AXES, None, None),
            P(AXES, None, None),
            P(AXES, None),
            P(AXES),
            P(AXES, None),
            P(AXES),
            P(AXES, None),
            P(AXES, None),
            P(AXES, None),
            P(AXES, None),
            P(AXES, None, None),
            P(AXES, None, None),
            P(),
            P(),
            P(None, AXES, None),
        ),
        out_specs=(P(AXES, None), P()),
        check_vma=False,
    )
```

```python
import functools

import jax
import jax.numpy as jnp
from jax import lax
from jax.experimental import pallas as pl
from jax.experimental.pallas import tpu as pltpu
from jax.sharding import PartitionSpec as P

RADIUS = 3
SIDES = 2 * RADIUS + 1
SOFTEN = 0.01
EPSILON = 1e-06
UNITS = 32
FEW = 16
SPARE = 12 << 20
FIXED = 32767.0
MESH = pl.DeviceIdType.MESH
NT = (((1,), (1,)), ((), ()))
NN = (((1,), (0,)), ((), ()))
TN = (((0,), (0,)), ((), ()))
F32 = jnp.float32
BF16 = jnp.bfloat16
AXES = ("role", "dev")


def mm(a, b, dims):
    return lax.dot_general(a, b, dims, preferred_element_type=F32)


def row_is(shape, k):
    return lax.broadcasted_iota(jnp.int32, shape, 0) == k


def place(roles, devs):
    me = lax.axis_index("role") * devs + lax.axis_index("dev")
    return me, roles * devs


def coords(linear, devs):
    return (linear // devs, lax.rem(linear, devs))


def far_first(me, roles, devs, visit):
    own = lax.rem(me, devs)

    def body(t, ends):
        low, high = ends
        left = own - low >= high - own
        other = jnp.where(left, low, high)
        for r in range(roles):
            visit(r * devs + other)
        return jnp.where(left, low + 1, low), jnp.where(left, high, high - 1)

    ends = (jnp.int32(0), jnp.int32(devs - 1))
    for t in range(devs - 1):
        ends = body(t, ends)
    for r in range(1, roles):
        visit(lax.rem(me + r * devs, roles * devs))


def greet(me, roles, devs):
    barrier = pltpu.get_barrier_semaphore()

    def visit(other):
        pl.semaphore_signal(barrier, inc=1, device_id=coords(other, devs), device_id_type=MESH)

    far_first(me, roles, devs, visit)
    return barrier


def live_mask(cnt_ref, shape):
    rows = lax.broadcasted_iota(jnp.int32, shape, 0)
    limit = jnp.zeros(shape, jnp.int32)
    for c in range(shape[0]):
        limit = jnp.where(rows == c, cnt_ref[c], limit)
    return lax.broadcasted_iota(jnp.int32, shape, 1) < limit


def halves(x):
    hi = x.astype(BF16).astype(F32)
    return jnp.concatenate([hi, x - hi], axis=0).astype(BF16)


def splits(x):
    hi = x.astype(BF16).astype(F32)
    rest = x - hi
    mid = rest.astype(BF16).astype(F32)
    return hi, mid, rest - mid


def pack(parts):
    return jnp.concatenate(parts, axis=0).astype(BF16)


def spread_all(feat, positions, weights):
    local, panels = positions[0].shape
    norm = jnp.zeros((local, panels), F32)
    inside = jnp.zeros((local, panels), F32)
    for y, w in zip(positions, weights):
        norm = norm + y * y
        inside = inside - y * w
    rows = list(positions) + [norm] + list(weights) + [inside]
    for k, value in enumerate(rows):
        for b in range(panels // 128):
            feat[b, k * local : (k + 1) * local, :] = value[:, b * 128 : (b + 1) * 128]


def read_features(feat, inner):
    at = pl.ds(inner, 8, stride=feat.shape[1] // 8)
    return jnp.concatenate([feat[b, at, :] for b in range(feat.shape[0])], axis=1)


def goal_rows(own):
    shape = own.shape
    rows = lax.broadcasted_iota(jnp.int32, shape, 0)
    x = jnp.where(rows < 3, -2.0 * own, jnp.where(rows == 3, own + SOFTEN, 0.0))
    hi, mid, low = splits(x)
    norms = [jnp.broadcast_to(part[3:4], shape) for part in (hi, mid, low)]
    firm = jnp.where(rows < 3, hi, jnp.where(rows == 3, 1.0, 0.0))
    soft = jnp.where(rows < 3, mid, 0.0)
    last = jnp.where(rows < 3, low, 0.0)
    tail = soft
    for k in range(3):
        tail = jnp.where(rows == 4 + k, norms[k], tail)
    return pack([firm, firm, firm, soft, last, tail])


def source_rows(own):
    rows = lax.broadcasted_iota(jnp.int32, own.shape, 0)
    hi, mid, low = splits(own)
    made = pack([hi, mid, low, hi, hi, jnp.where(rows < 4, mid, 1.0)])
    return made, pack([jnp.where(rows < 4, pltpu.roll(mid, 4, 0), hi), low])


def squares(src, block, target, ref):
    for k in range(2):
        ref[k * 128 : (k + 1) * 128, :] = mm(src[2 * block + k], target, TN)


def cubes(a, b):
    inverse = lax.rsqrt(a[...])
    b[...] = (inverse * inverse * inverse).astype(BF16)


def gathered(wgt, block, ref):
    both = jnp.concatenate([wgt[2 * block], wgt[2 * block + 1]], axis=1)
    return mm(both, ref[...], NN)


def combine(own, got):
    total = got[:8] + pltpu.roll(got[:8], 4, 0) + got[8:]
    rows = lax.broadcasted_iota(jnp.int32, total.shape, 0)
    part = total * pltpu.roll(own, 4, 0)
    value = jnp.where(rows < 4, 0.0, jnp.where(rows == 7, total, part))
    return jnp.sum(value, axis=0, keepdims=True)


def own_near(pos_v, nrm_parts, density, feat, goal, src, wgt, sqs, gs, acc, out):
    local, panels = density.shape
    wide = goal.shape[2]
    per_h = panels // wide
    blocks = panels // 256
    positions = [pos_v[a] for a in range(3)]
    spread_all(feat, positions, [part * density for part in nrm_parts])
    for c in range(local):
        own = read_features(feat, c)
        made = goal_rows(own)
        for h in range(per_h):
            goal[per_h * c + h] = made[:, h * wide : (h + 1) * wide]
        made, pulled = source_rows(own)
        for b in range(panels // 128):
            src[2 * blocks * c + b] = made[:, b * 128 : (b + 1) * 128]
            wgt[2 * blocks * c + b] = pulled[:, b * 128 : (b + 1) * 128]
    acc[...] = jnp.zeros(acc.shape, F32)
    units = local * per_h * blocks

    def place_of(n):
        n = lax.rem(n, units)
        c = n // (per_h * blocks)
        return n // blocks, c * blocks + lax.rem(n, blocks)

    def start(n, ref):
        g, b = place_of(n)
        squares(src, b, goal[g], ref)

    start(0, sqs[0])
    cubes(sqs[0], gs[0])
    start(1, sqs[1])
    steps = 16

    def body(t, carry):
        for u in range(steps):
            n = t * steps + u
            start(n + 2, sqs[u % 2])
            cubes(sqs[(u + 1) % 2], gs[(u + 1) % 2])
            g, b = place_of(n)
            acc[g] += gathered(wgt, b, gs[u % 2])
        return carry

    lax.fori_loop(0, units // steps, body, 0)
    for c in range(local):
        own = read_features(feat, c)
        for h in range(per_h):
            part = slice(h * wide, (h + 1) * wide)
            out[c : c + 1, part] = out[c : c + 1, part] + combine(own[:, part], acc[per_h * c + h])


def source_kernel(
    roles,
    devs,
    cnth,
    nearh,
    usedh,
    pos,
    nrm,
    area,
    kry,
    binv,
    maps,
    ups,
    posw,
    anw,
    denw,
    cntw,
    momw,
    gmall,
    base,
    mask,
    cnt,
    near,
    used,
    mom_v,
    grp_v,
    base_v,
    mask_v,
    pos_v,
    fix_v,
    an_v,
    den_v,
    cnt_v,
    info_v,
    nrm_v,
    area_v,
    kry_v,
    binv_v,
    maps_v,
    ups_v,
    local_sem,
    big_sem,
    send_sem,
    recv_sem,
    gsend,
    grecv,
    feat,
    goal,
    src,
    wgt,
    sq0,
    sq1,
    g0,
    g1,
    acc,
):
    me, total = place(roles, devs)
    local, panels = area.shape
    coeffs = maps_v.shape[1]
    barrier = greet(me, roles, devs)
    copies = []
    for c in range(local):
        copies.append(pltpu.make_async_copy(binv.at[c], binv_v.at[c], big_sem.at[c]))
    map_copy = pltpu.make_async_copy(maps, maps_v, local_sem.at[0])
    up_copy = pltpu.make_async_copy(ups, ups_v, local_sem.at[1])
    small = [
        pltpu.make_async_copy(cnth, cnt, local_sem.at[13]),
        pltpu.make_async_copy(nearh, near, local_sem.at[14]),
        pltpu.make_async_copy(usedh, used, local_sem.at[15]),
        pltpu.make_async_copy(pos, pos_v, local_sem.at[2]),
        pltpu.make_async_copy(nrm, nrm_v, local_sem.at[3]),
        pltpu.make_async_copy(area, area_v, local_sem.at[4]),
        pltpu.make_async_copy(kry.at[kry.shape[0] - 1], kry_v, local_sem.at[5]),
    ]
    for copy in small + copies:
        copy.start()
    home = [
        pltpu.make_async_copy(fix_v, posw.at[RADIUS], local_sem.at[6]),
        pltpu.make_async_copy(an_v, anw.at[RADIUS], local_sem.at[7]),
        pltpu.make_async_copy(cnt_v, cntw.at[RADIUS], local_sem.at[8]),
        pltpu.make_async_copy(info_v, cntw.at[pl.ds(SIDES, local)], local_sem.at[9]),
        pltpu.make_async_copy(mom_v, momw.at[RADIUS], local_sem.at[10]),
        pltpu.make_async_copy(grp_v, gmall.at[me], local_sem.at[11]),
        pltpu.make_async_copy(base_v, base, local_sem.at[12]),
        pltpu.make_async_copy(mask_v, mask, local_sem.at[16]),
        pltpu.make_async_copy(den_v, denw.at[RADIUS], local_sem.at[17]),
    ]
    map_copy.start()
    up_copy.start()
    for copy in small:
        copy.wait()
    fix_v[...] = jnp.floor(pos_v[...] * FIXED + 0.5).astype(jnp.int32).astype(jnp.int16)
    home[0].start()
    parts = [(nrm_v[a] * area_v[...]).astype(BF16).astype(F32) for a in range(3)]
    an_v[...] = jnp.concatenate(parts, axis=0).astype(BF16)
    home[1].start()
    lane = lax.broadcasted_iota(jnp.int32, (1, 128), 1)
    counts = jnp.zeros((1, 128), jnp.int32)
    for c in range(local):
        counts = jnp.where(lane == c, cnt[c], counts)
    cnt_v[...] = counts
    home[2].start()
    for c in range(local):
        row = jnp.where(lane == 6, used[c], (me - RADIUS) * local)
        for n in range(near.shape[1]):
            row = jnp.where(lane == 8 + n, near[c, n], row)
        info_v[c] = row
    home[3].start()
    pl.semaphore_wait(barrier, total - 1)

    def to_neighbours(own, ref, kind):
        made = []
        for n, d in enumerate([3, -3, 2, -2, 1, -1]):
            made.append(
                pltpu.make_async_remote_copy(
                    src_ref=own,
                    dst_ref=ref.at[RADIUS - d],
                    send_sem=send_sem.at[kind, n],
                    recv_sem=recv_sem.at[kind, n],
                    device_id=coords(lax.rem(me + d + total, total), devs),
                    device_id_type=MESH,
                )
            )
        for copy in made:
            copy.start()
        return made

    sent = to_neighbours(fix_v, posw, 0)
    sent += to_neighbours(an_v, anw, 4)
    sent += to_neighbours(cnt_v, cntw, 1)
    live = live_mask(cnt, (local, panels))
    current = kry_v[...].astype(BF16)
    density = jnp.zeros((local, panels), F32)
    for c in range(local):
        copies[c].wait()
        found = mm(current, binv_v[c], NT)
        density = jnp.where(row_is(found.shape, c), found, density)
    rounded = jnp.where(live, density, 0.0).astype(BF16)
    den_v[...] = rounded
    base_v[...] = 0.5 * rounded.astype(F32)
    mask_v[...] = jnp.where(live, 1.0, 0.0)
    home[7].start()
    home[8].start()
    sent += to_neighbours(den_v, denw, 2)
    map_copy.wait()
    moments = jnp.zeros((local, coeffs), F32)
    for c in range(local):
        found = mm(rounded, maps_v[c], NT)
        moments = jnp.where(row_is(found.shape, c), found, moments)
    moments = moments.astype(BF16)
    mom_v[...] = moments
    home[4].start()
    sent += to_neighbours(mom_v, momw, 3)
    up_copy.wait()
    merged = jnp.zeros((local, coeffs), F32)
    for k in range(local):
        found = mm(moments, ups_v[k], NT)
        merged = jnp.where(row_is(found.shape, k), found, merged)
    grp_v[...] = jnp.sum(merged, axis=0, keepdims=True)
    home[5].start()

    def group_copy(slot, other):
        return pltpu.make_async_remote_copy(
            src_ref=grp_v,
            dst_ref=gmall.at[slot],
            send_sem=gsend.at[other],
            recv_sem=grecv.at[slot],
            device_id=coords(other, devs),
            device_id_type=MESH,
        )

    far_first(me, roles, devs, lambda other: group_copy(me, other).start())
    own_near(
        pos_v, parts, rounded.astype(F32), feat, goal, src, wgt, (sq0, sq1), (g0, g1), acc, base_v
    )
    home[6].start()
    for copy in home + sent:
        copy.wait()
    far_first(me, roles, devs, lambda other: group_copy(other, other).wait())


def near_kernel(
    infoh,
    posh,
    anh,
    denh,
    out,
    info,
    posw,
    anw,
    denw,
    sems,
    feat,
    goal,
    src,
    wgt,
    sq0,
    sq1,
    g0,
    g1,
    acc,
    begin,
    spans,
):
    local, panels = out.shape
    wide = goal.shape[2]
    per_h = panels // wide
    tally = pltpu.make_async_copy(infoh.at[pl.ds(0, SIDES + local)], info, sems.at[2, 0])
    tally.start()
    thick = pltpu.make_async_copy(denh.at[pl.ds(0, SIDES)], denw, sems.at[2, 1])
    order = [RADIUS] + [k for k in range(SIDES) if k != RADIUS]
    loads = []
    for k in order:
        loads.append(pltpu.make_async_copy(posh.at[k], posw.at[k], sems.at[0, k]))
        loads.append(pltpu.make_async_copy(anh.at[k], anw.at[k], sems.at[1, k]))
    for copy in [thick] + loads:
        copy.start()
    thick.wait()
    for n, side in enumerate(order):
        loads[2 * n].wait()
        loads[2 * n + 1].wait()
        fields = anw[side].astype(F32)
        dens = denw[side].astype(F32)
        weights = [fields[a * local : (a + 1) * local] * dens for a in range(3)]
        centres = posw[side].astype(jnp.int32).astype(F32) * (1.0 / FIXED)
        spread_all(feat.at[side], [centres[a] for a in range(3)], weights)
    tally.wait()
    first = info[SIDES, 0, 7]

    def cluster_body(c, start):
        made = goal_rows(read_features(feat.at[RADIUS], c))
        for h in range(per_h):
            goal[per_h * c + h] = made[:, h * wide : (h + 1) * wide]

        def slot_body(s, offset):
            w = info[SIDES + c, 0, 8 + s] - first
            side = w // local
            inner = lax.rem(w, local)
            made, pulled = source_rows(read_features(feat.at[side], inner))
            for b in range(panels // 128):
                src[offset + b] = made[:, b * 128 : (b + 1) * 128]
                wgt[offset + b] = pulled[:, b * 128 : (b + 1) * 128]
            return offset + (info[side, 0, inner] + 127) // 128

        end = lax.fori_loop(0, info[SIDES + c, 0, 6], slot_body, start)
        pad_rows = lax.broadcasted_iota(jnp.int32, (48, 128), 0)
        src[end] = jnp.where(pad_rows >= 44, 1.0, 0.0).astype(BF16)
        wgt[end] = jnp.zeros((16, 128), BF16)
        stop = (end + 1) // 2 * 2
        begin[c] = start // 2
        spans[c] = (info[RADIUS, 0, c] + wide - 1) // wide
        return stop

    end = lax.fori_loop(0, local, cluster_body, 0)
    begin[local] = end // 2
    begin[local + 1] = end // 2
    spans[local] = 1
    acc[...] = jnp.zeros(acc.shape, F32)

    def advance(state):
        c, h, b = state
        over = b + 1 >= begin[jnp.minimum(c + 1, local)]
        h = jnp.where(over, h + 1, h)
        done = h >= spans[c]
        b = jnp.where(over, begin[c], b + 1)
        c_next = jnp.where(done, jnp.minimum(c + 1, local), c)
        b = jnp.where(done, begin[c_next], b)
        return c_next, jnp.where(done, 0, h), b

    def products(state, ref):
        c, h, b = state
        squares(src, b, goal[per_h * c + h], ref)

    def count_body(c, total):
        return total + spans[c] * (begin[c + 1] - begin[c])

    units = lax.fori_loop(0, local, count_body, 0)
    origin = (jnp.int32(0), jnp.int32(0), jnp.int32(0))
    products(origin, sq0)
    cubes(sq0, g0)
    second = advance(origin)
    products(second, sq1)

    def body(many, t, states):
        old, state = states
        for u in range(many):
            later = advance(state)
            products(later, (sq0, sq1)[u % 2])
            cubes((sq1, sq0)[u % 2], (g1, g0)[u % 2])
            c, h, b = old
            acc[per_h * c + h] += gathered(wgt, b, (g0, g1)[u % 2])
            old, state = state, later
        return old, state

    full = (units + UNITS - FEW - 1) // UNITS
    states = lax.fori_loop(0, full, functools.partial(body, UNITS), (origin, second))
    left = units - full * UNITS
    lax.fori_loop(0, (left + FEW - 1) // FEW, functools.partial(body, FEW), states)
    for c in range(local):
        own = read_features(feat.at[RADIUS], c)
        for h in range(per_h):
            part = slice(h * wide, (h + 1) * wide)
            out[c : c + 1, part] = combine(own[:, part], acc[per_h * c + h])


def finish_kernel(
    roles,
    devs,
    live,
    glist,
    gkind,
    llist,
    lkind,
    momw,
    gmall,
    near,
    base,
    kry,
    maps_v,
    ups_v,
    fars_v,
    image_out,
    sums_out,
    red,
    send_sem,
    recv_sem,
):
    me, total = place(roles, devs)
    local, panels = near.shape
    coeffs = maps_v.shape[1]
    kinds = fars_v.shape[1]
    window = SIDES * local
    barrier = greet(me, roles, devs)

    groups = gmall[...].reshape(total, coeffs)
    g_rows = lax.broadcasted_iota(jnp.int32, (kinds, total), 0)
    g_lanes = lax.broadcasted_iota(jnp.int32, (kinds, total), 1)
    g_hot = jnp.zeros((kinds, total), F32)
    for n in range(glist.shape[1]):
        g_hot += jnp.where((g_rows == gkind[:, n : n + 1]) & (g_lanes == glist[:, n : n + 1]), 1.0, 0.0)
    g_hot = g_hot.astype(BF16)
    hi, mid, low = splits(groups)
    g_sum = mm(g_hot, hi.astype(BF16), NN) + mm(g_hot, mid.astype(BF16), NN)
    g_sum += mm(g_hot, low.astype(BF16), NN)
    g_both = halves(g_sum)

    lanes = lax.broadcasted_iota(jnp.int32, (local, window), 1)
    shift = (me - RADIUS) * local
    hots = [jnp.zeros((local, window), F32) for _ in range(kinds)]
    for n in range(llist.shape[1]):
        hit = lanes == (llist[:, n : n + 1] - shift)
        kind = jnp.broadcast_to(lkind[:, n : n + 1], (local, window))
        for o in range(kinds):
            hots[o] = hots[o] + jnp.where(hit & (kind == o), 1.0, 0.0)
    hot = jnp.concatenate(hots, axis=0).astype(BF16)
    held = jnp.concatenate([momw[side].astype(F32) for side in range(SIDES)], axis=0)
    summed = mm(hot, held.astype(BF16), NN)

    g_parts = jnp.zeros((kinds, coeffs), F32)
    for o in range(kinds):
        found = mm(g_both, fars_v[1, o], NT)
        found = found[:kinds] + found[kinds:]
        g_parts = jnp.where(row_is(found.shape, o), found, g_parts)
    g_local = jnp.sum(g_parts, axis=0, keepdims=True).astype(BF16)
    leaf = jnp.zeros((local, coeffs), F32)
    for o in range(kinds):
        found = mm(halves(summed[o * local : (o + 1) * local]), fars_v[0, o], NT)
        leaf = leaf + found[:local] + found[local:]
    g_wide = jnp.broadcast_to(g_local.astype(F32), (local, coeffs)).astype(BF16)
    down = jnp.zeros((local, coeffs), F32)
    for k in range(local):
        found = mm(g_wide, ups_v[k], NN)
        down = jnp.where(row_is(found.shape, k), found, down)
    leaf = (leaf + down).astype(BF16)
    far = jnp.zeros((local, panels), F32)
    for c in range(local):
        found = mm(leaf, maps_v[c], NN)
        far = jnp.where(row_is(found.shape, c), found, far)
    image = jnp.where(live[...] > 0.5, base[...] + near[...] + far, 0.0)

    lane = lax.broadcasted_iota(jnp.int32, (1, 128), 1)
    count = kry.shape[0]
    row = jnp.zeros((1, 128), F32)
    for k in range(count + 1):
        part = image * (kry[k] if k < count else image)
        value = jnp.sum(jnp.sum(part, axis=0, keepdims=True), axis=1, keepdims=True)
        row = jnp.where(lane == k, value, row)
    red[me] = row
    image_out[...] = image
    pl.semaphore_wait(barrier, total - 1)

    def row_copy(slot, other):
        return pltpu.make_async_remote_copy(
            src_ref=red.at[me],
            dst_ref=red.at[slot],
            send_sem=send_sem.at[other],
            recv_sem=recv_sem.at[slot],
            device_id=coords(other, devs),
            device_id_type=MESH,
        )

    far_first(me, roles, devs, lambda other: row_copy(me, other).start())
    far_first(me, roles, devs, lambda other: row_copy(other, other).wait())
    scale = 1.0 / (total * local * panels)
    sums_out[...] = jnp.sum(red[...], axis=0) * scale


def update_kernel(sums_ref, image, kry, nxt, hess):
    count = kry.shape[0]
    sums = sums_ref[...]
    lane = lax.broadcasted_iota(jnp.int32, sums.shape, 1)
    rest = image[...]
    energy = sums[:, count : count + 1]
    for k in range(count):
        c_k = sums[:, k : k + 1]
        rest = rest - c_k * kry[k]
        energy = energy - c_k * c_k
    height = jnp.sqrt(energy + EPSILON)
    nxt[...] = rest / height
    hess[...] = jnp.where(lane == count, height, sums)[:, : count + 1]


def shards(
    roles,
    devs,
    positions,
    normals,
    panel_areas,
    panel_counts,
    near_lists,
    near_counts,
    leaf_lists,
    leaf_kinds,
    group_lists,
    group_kinds,
    block_inverse,
    moment_maps,
    up_operators,
    far_operators,
    krylov_basis,
):
    local, _, panels = positions.shape
    coeffs = moment_maps.shape[1]
    total = roles * devs
    wide = 256
    vmem = pl.BlockSpec(memory_space=pltpu.VMEM)
    smem = pl.BlockSpec(memory_space=pltpu.SMEM)
    hbm = pl.BlockSpec(memory_space=pltpu.HBM)
    dma = pltpu.SemaphoreType.DMA
    posw, anw, denw, cntw, momw, gmall, base, live = pl.pallas_call(
        functools.partial(source_kernel, roles, devs),
        name="sources",
        out_shape=(
            jax.ShapeDtypeStruct((SPARE // (6 * local * panels), 3, local, panels), jnp.int16),
            jax.ShapeDtypeStruct((SPARE // (6 * local * panels), 3 * local, panels), BF16),
            jax.ShapeDtypeStruct((SPARE // (2 * local * panels), local, panels), BF16),
            jax.ShapeDtypeStruct((SPARE // 512, 1, 128), jnp.int32),
            jax.ShapeDtypeStruct((SIDES, local, coeffs), BF16),
            jax.ShapeDtypeStruct((total, 1, coeffs), F32),
            jax.ShapeDtypeStruct((local, panels), F32),
            jax.ShapeDtypeStruct((local, panels), F32),
        ),
        in_specs=[hbm] * 10,
        out_specs=(hbm,) * 8,
        scratch_shapes=[
            pltpu.SMEM(panel_counts.shape, jnp.int32),
            pltpu.SMEM(near_lists.shape, jnp.int32),
            pltpu.SMEM(near_counts.shape, jnp.int32),
            pltpu.VMEM((local, coeffs), BF16),
            pltpu.VMEM((1, coeffs), F32),
            pltpu.VMEM((local, panels), F32),
            pltpu.VMEM((local, panels), F32),
            pltpu.VMEM((3, local, panels), F32),
            pltpu.VMEM((3, local, panels), jnp.int16),
            pltpu.VMEM((3 * local, panels), BF16),
            pltpu.VMEM((local, panels), BF16),
            pltpu.VMEM((1, 128), jnp.int32),
            pltpu.VMEM((local, 1, 128), jnp.int32),
            pltpu.VMEM((3, local, panels), F32),
            pltpu.VMEM((local, panels), F32),
            pltpu.VMEM((local, panels), F32),
            pltpu.VMEM(block_inverse.shape, BF16),
            pltpu.VMEM(moment_maps.shape, BF16),
            pltpu.VMEM(up_operators.shape, BF16),
            dma((18,)),
            dma((local,)),
            dma((5, 6)),
            dma((5, 6)),
            dma((total,)),
            dma((total,)),
            pltpu.VMEM((panels // 128, 8 * local, 128), F32),
            pltpu.VMEM((local * (panels // wide), 48, wide), BF16),
            pltpu.VMEM((local * (panels // 128), 48, 128), BF16),
            pltpu.VMEM((local * (panels // 128), 16, 128), BF16),
            pltpu.VMEM((256, wide), F32),
            pltpu.VMEM((256, wide), F32),
            pltpu.VMEM((256, wide), BF16),
            pltpu.VMEM((256, wide), BF16),
            pltpu.VMEM((local * (panels // wide), 16, wide), F32),
        ],
        compiler_params=pltpu.CompilerParams(
            collective_id=0, has_side_effects=True, vmem_limit_bytes=62 << 20
        ),
    )(
        panel_counts,
        near_lists,
        near_counts,
        jnp.transpose(positions, (1, 0, 2)),
        jnp.transpose(normals, (1, 0, 2)),
        panel_areas,
        krylov_basis,
        block_inverse,
        moment_maps,
        up_operators,
    )
    room = local * (near_lists.shape[1] * (panels // 128) + 1) + 8
    goals = (local + 1) * (panels // wide)
    near = pl.pallas_call(
        near_kernel,
        name="near",
        cost_estimate=pl.CostEstimate(
            flops=40 * local * panels * panels * (near_lists.shape[1] + 1),
            bytes_accessed=48 * local * panels * SIDES,
            transcendentals=local * panels * panels * (near_lists.shape[1] + 1),
        ),
        out_shape=jax.ShapeDtypeStruct((local, panels), F32),
        in_specs=[hbm] * 4,
        out_specs=vmem,
        scratch_shapes=[
            pltpu.SMEM((SIDES + local, 1, 128), jnp.int32),
            pltpu.VMEM((SIDES, 3, local, panels), jnp.int16),
            pltpu.VMEM((SIDES, 3 * local, panels), BF16),
            pltpu.VMEM((SIDES, local, panels), BF16),
            dma((3, SIDES)),
            pltpu.VMEM((SIDES, panels // 128, 8 * local, 128), F32),
            pltpu.VMEM((goals, 48, wide), BF16),
            pltpu.VMEM((room, 48, 128), BF16),
            pltpu.VMEM((room, 16, 128), BF16),
            pltpu.VMEM((256, wide), F32),
            pltpu.VMEM((256, wide), F32),
            pltpu.VMEM((256, wide), BF16),
            pltpu.VMEM((256, wide), BF16),
            pltpu.VMEM((goals, 16, wide), F32),
            pltpu.SMEM((local + 2,), jnp.int32),
            pltpu.SMEM((local + 2,), jnp.int32),
        ],
        compiler_params=pltpu.CompilerParams(vmem_limit_bytes=52 << 20),
    )(cntw, posw, anw, denw)
    image, sums = pl.pallas_call(
        functools.partial(finish_kernel, roles, devs),
        name="finish",
        out_shape=(
            jax.ShapeDtypeStruct((local, panels), F32),
            jax.ShapeDtypeStruct((1, 128), F32),
        ),
        in_specs=[vmem] * 13,
        out_specs=(vmem, vmem),
        scratch_shapes=[
            pltpu.VMEM((total, 1, 128), F32),
            dma((total,)),
            dma((total,)),
        ],
        compiler_params=pltpu.CompilerParams(
            collective_id=1, has_side_effects=True, vmem_limit_bytes=14 << 20
        ),
    )(
        live,
        group_lists,
        group_kinds,
        leaf_lists,
        leaf_kinds,
        momw,
        gmall,
        near,
        base,
        krylov_basis,
        moment_maps,
        up_operators,
        far_operators,
    )
    nxt, hess = pl.pallas_call(
        update_kernel,
        name="update",
        out_shape=(
            jax.ShapeDtypeStruct((local, panels), F32),
            jax.ShapeDtypeStruct((1, krylov_basis.shape[0] + 1), F32),
        ),
        in_specs=[vmem] * 3,
        out_specs=(vmem, vmem),
        compiler_params=pltpu.CompilerParams(vmem_limit_bytes=8 << 20),
    )(sums, image, krylov_basis)
    return nxt, jnp.reshape(hess, (krylov_basis.shape[0] + 1,))


def solution(mesh):
    roles, devs = mesh.shape["role"], mesh.shape["dev"]
    return jax.shard_map(
        functools.partial(shards, roles, devs),
        mesh=mesh,
        in_specs=(
            P(AXES, None, None),
            P(AXES, None, None),
            P(AXES, None),
            P(AXES),
            P(AXES, None),
            P(AXES),
            P(AXES, None),
            P(AXES, None),
            P(AXES, None),
            P(AXES, None),
            P(AXES, None, None),
            P(AXES, None, None),
            P(),
            P(),
            P(None, AXES, None),
        ),
        out_specs=(P(AXES, None), P()),
        check_vma=False,
    )
```

```python
import functools

import jax
import jax.numpy as jnp
from jax import lax
from jax.experimental import pallas as pl
from jax.experimental.pallas import tpu as pltpu
from jax.sharding import PartitionSpec as P

RADIUS = 3
SIDES = 2 * RADIUS + 1
SOFTEN = 0.01
EPSILON = 1e-06
BODIES = (32, 16, 8)
SPARE = 12 << 20
FIXED = 32767.0
MESH = pl.DeviceIdType.MESH
NT = (((1,), (1,)), ((), ()))
NN = (((1,), (0,)), ((), ()))
TN = (((0,), (0,)), ((), ()))
F32 = jnp.float32
BF16 = jnp.bfloat16
AXES = ("role", "dev")


def mm(a, b, dims):
    return lax.dot_general(a, b, dims, preferred_element_type=F32)


def row_is(shape, k):
    return lax.broadcasted_iota(jnp.int32, shape, 0) == k


def place(roles, devs):
    me = lax.axis_index("role") * devs + lax.axis_index("dev")
    return me, roles * devs


def coords(linear, devs):
    return (linear // devs, lax.rem(linear, devs))


def far_first(me, roles, devs, visit):
    own = lax.rem(me, devs)

    def body(t, ends):
        low, high = ends
        left = own - low >= high - own
        other = jnp.where(left, low, high)
        for r in range(roles):
            visit(r * devs + other)
        return jnp.where(left, low + 1, low), jnp.where(left, high, high - 1)

    ends = (jnp.int32(0), jnp.int32(devs - 1))
    for t in range(devs - 1):
        ends = body(t, ends)
    for r in range(1, roles):
        visit(lax.rem(me + r * devs, roles * devs))


def greet(me, roles, devs):
    barrier = pltpu.get_barrier_semaphore()

    def visit(other):
        pl.semaphore_signal(barrier, inc=1, device_id=coords(other, devs), device_id_type=MESH)

    far_first(me, roles, devs, visit)
    return barrier


def live_mask(cnt_ref, shape):
    rows = lax.broadcasted_iota(jnp.int32, shape, 0)
    limit = jnp.zeros(shape, jnp.int32)
    for c in range(shape[0]):
        limit = jnp.where(rows == c, cnt_ref[c], limit)
    return lax.broadcasted_iota(jnp.int32, shape, 1) < limit


def halves(x):
    hi = x.astype(BF16).astype(F32)
    return jnp.concatenate([hi, x - hi], axis=0).astype(BF16)


def splits(x):
    hi = x.astype(BF16).astype(F32)
    rest = x - hi
    mid = rest.astype(BF16).astype(F32)
    return hi, mid, rest - mid


def pack(parts):
    return jnp.concatenate(parts, axis=0).astype(BF16)


def spread_all(feat, positions, weights):
    local, panels = positions[0].shape
    norm = jnp.zeros((local, panels), F32)
    inside = jnp.zeros((local, panels), F32)
    for y, w in zip(positions, weights):
        norm = norm + y * y
        inside = inside - y * w
    rows = list(positions) + [norm] + list(weights) + [inside]
    for k, value in enumerate(rows):
        for b in range(panels // 128):
            feat[b, k * local : (k + 1) * local, :] = value[:, b * 128 : (b + 1) * 128]


def read_features(feat, inner):
    at = pl.ds(inner, 8, stride=feat.shape[1] // 8)
    return jnp.concatenate([feat[b, at, :] for b in range(feat.shape[0])], axis=1)


def goal_rows(own):
    shape = own.shape
    rows = lax.broadcasted_iota(jnp.int32, shape, 0)
    x = jnp.where(rows < 3, -2.0 * own, jnp.where(rows == 3, own + SOFTEN, 0.0))
    hi, mid, low = splits(x)
    norms = [jnp.broadcast_to(part[3:4], shape) for part in (hi, mid, low)]
    firm = jnp.where(rows < 3, hi, jnp.where(rows == 3, 1.0, 0.0))
    soft = jnp.where(rows < 3, mid, 0.0)
    last = jnp.where(rows < 3, low, 0.0)
    tail = soft
    for k in range(3):
        tail = jnp.where(rows == 4 + k, norms[k], tail)
    return pack([firm, firm, firm, soft, last, tail])


def source_rows(own):
    rows = lax.broadcasted_iota(jnp.int32, own.shape, 0)
    hi, mid, low = splits(own)
    made = pack([hi, mid, low, hi, hi, jnp.where(rows < 4, mid, 1.0)])
    return made, pack([jnp.where(rows < 4, pltpu.roll(mid, 4, 0), hi), low])


def squares(src, block, target, ref):
    for k in range(2):
        ref[k * 128 : (k + 1) * 128, :] = mm(src[2 * block + k], target, TN)


def cubes(a, b):
    inverse = lax.rsqrt(a[...])
    b[...] = (inverse * inverse * inverse).astype(BF16)


def gathered(wgt, block, ref):
    both = jnp.concatenate([wgt[2 * block], wgt[2 * block + 1]], axis=1)
    return mm(both, ref[...], NN)


def combine(own, got):
    total = got[:8] + pltpu.roll(got[:8], 4, 0) + got[8:]
    rows = lax.broadcasted_iota(jnp.int32, total.shape, 0)
    part = total * pltpu.roll(own, 4, 0)
    value = jnp.where(rows < 4, 0.0, jnp.where(rows == 7, total, part))
    return jnp.sum(value, axis=0, keepdims=True)


def own_near(pos_v, nrm_parts, density, feat, goal, src, wgt, sqs, gs, acc, out):
    local, panels = density.shape
    wide = goal.shape[2]
    per_h = panels // wide
    blocks = panels // 256
    positions = [pos_v[a] for a in range(3)]
    spread_all(feat, positions, [part * density for part in nrm_parts])
    for c in range(local):
        own = read_features(feat, c)
        made = goal_rows(own)
        for h in range(per_h):
            goal[per_h * c + h] = made[:, h * wide : (h + 1) * wide]
        made, pulled = source_rows(own)
        for b in range(panels // 128):
            src[2 * blocks * c + b] = made[:, b * 128 : (b + 1) * 128]
            wgt[2 * blocks * c + b] = pulled[:, b * 128 : (b + 1) * 128]
    acc[...] = jnp.zeros(acc.shape, F32)
    units = local * per_h * blocks

    def place_of(n):
        n = lax.rem(n, units)
        c = n // (per_h * blocks)
        return n // blocks, c * blocks + lax.rem(n, blocks)

    def start(n, ref):
        g, b = place_of(n)
        squares(src, b, goal[g], ref)

    start(0, sqs[0])
    cubes(sqs[0], gs[0])
    start(1, sqs[1])
    steps = 16

    def body(t, carry):
        for u in range(steps):
            n = t * steps + u
            start(n + 2, sqs[u % 2])
            cubes(sqs[(u + 1) % 2], gs[(u + 1) % 2])
            g, b = place_of(n)
            acc[g] += gathered(wgt, b, gs[u % 2])
        return carry

    lax.fori_loop(0, units // steps, body, 0)
    for c in range(local):
        own = read_features(feat, c)
        for h in range(per_h):
            part = slice(h * wide, (h + 1) * wide)
            out[c : c + 1, part] = out[c : c + 1, part] + combine(own[:, part], acc[per_h * c + h])


def source_kernel(
    roles,
    devs,
    cnth,
    nearh,
    usedh,
    pos,
    nrm,
    area,
    kry,
    binv,
    maps,
    ups,
    posw,
    anw,
    denw,
    cntw,
    momw,
    gmall,
    base,
    mask,
    cnt,
    near,
    used,
    mom_v,
    grp_v,
    base_v,
    mask_v,
    pos_v,
    fix_v,
    an_v,
    den_v,
    cnt_v,
    info_v,
    nrm_v,
    area_v,
    kry_v,
    binv_v,
    maps_v,
    ups_v,
    local_sem,
    big_sem,
    send_sem,
    recv_sem,
    gsend,
    grecv,
    feat,
    goal,
    src,
    wgt,
    sq0,
    sq1,
    g0,
    g1,
    acc,
):
    me, total = place(roles, devs)
    local, panels = area.shape
    coeffs = maps_v.shape[1]
    barrier = greet(me, roles, devs)
    copies = []
    for c in range(local):
        copies.append(pltpu.make_async_copy(binv.at[c], binv_v.at[c], big_sem.at[c]))
    map_copy = pltpu.make_async_copy(maps, maps_v, local_sem.at[0])
    up_copy = pltpu.make_async_copy(ups, ups_v, local_sem.at[1])
    small = [
        pltpu.make_async_copy(cnth, cnt, local_sem.at[13]),
        pltpu.make_async_copy(nearh, near, local_sem.at[14]),
        pltpu.make_async_copy(usedh, used, local_sem.at[15]),
        pltpu.make_async_copy(pos, pos_v, local_sem.at[2]),
        pltpu.make_async_copy(nrm, nrm_v, local_sem.at[3]),
        pltpu.make_async_copy(area, area_v, local_sem.at[4]),
        pltpu.make_async_copy(kry.at[kry.shape[0] - 1], kry_v, local_sem.at[5]),
    ]
    for copy in small + copies:
        copy.start()
    home = [
        pltpu.make_async_copy(fix_v, posw.at[RADIUS], local_sem.at[6]),
        pltpu.make_async_copy(an_v, anw.at[RADIUS], local_sem.at[7]),
        pltpu.make_async_copy(cnt_v, cntw.at[RADIUS], local_sem.at[8]),
        pltpu.make_async_copy(info_v, cntw.at[pl.ds(SIDES, local)], local_sem.at[9]),
        pltpu.make_async_copy(mom_v, momw.at[RADIUS], local_sem.at[10]),
        pltpu.make_async_copy(grp_v, gmall.at[me], local_sem.at[11]),
        pltpu.make_async_copy(base_v, base, local_sem.at[12]),
        pltpu.make_async_copy(mask_v, mask, local_sem.at[16]),
        pltpu.make_async_copy(den_v, denw.at[RADIUS], local_sem.at[17]),
    ]
    map_copy.start()
    up_copy.start()
    for copy in small:
        copy.wait()
    fix_v[...] = jnp.floor(pos_v[...] * FIXED + 0.5).astype(jnp.int32).astype(jnp.int16)
    home[0].start()
    parts = [(nrm_v[a] * area_v[...]).astype(BF16).astype(F32) for a in range(3)]
    an_v[...] = jnp.concatenate(parts, axis=0).astype(BF16)
    home[1].start()
    lane = lax.broadcasted_iota(jnp.int32, (1, 128), 1)
    counts = jnp.zeros((1, 128), jnp.int32)
    for c in range(local):
        counts = jnp.where(lane == c, cnt[c], counts)
    cnt_v[...] = counts
    home[2].start()
    for c in range(local):
        row = jnp.where(lane == 6, used[c], (me - RADIUS) * local)
        for n in range(near.shape[1]):
            row = jnp.where(lane == 8 + n, near[c, n], row)
        info_v[c] = row
    home[3].start()
    pl.semaphore_wait(barrier, total - 1)

    def to_neighbours(own, ref, kind):
        made = []
        for n, d in enumerate([3, -3, 2, -2, 1, -1]):
            made.append(
                pltpu.make_async_remote_copy(
                    src_ref=own,
                    dst_ref=ref.at[RADIUS - d],
                    send_sem=send_sem.at[kind, n],
                    recv_sem=recv_sem.at[kind, n],
                    device_id=coords(lax.rem(me + d + total, total), devs),
                    device_id_type=MESH,
                )
            )
        for copy in made:
            copy.start()
        return made

    sent = to_neighbours(fix_v, posw, 0)
    sent += to_neighbours(an_v, anw, 4)
    sent += to_neighbours(cnt_v, cntw, 1)
    live = live_mask(cnt, (local, panels))
    current = kry_v[...].astype(BF16)
    density = jnp.zeros((local, panels), F32)
    for c in range(local):
        copies[c].wait()
        found = mm(current, binv_v[c], NT)
        density = jnp.where(row_is(found.shape, c), found, density)
    rounded = jnp.where(live, density, 0.0).astype(BF16)
    den_v[...] = rounded
    base_v[...] = 0.5 * rounded.astype(F32)
    mask_v[...] = jnp.where(live, 1.0, 0.0)
    home[7].start()
    home[8].start()
    sent += to_neighbours(den_v, denw, 2)
    map_copy.wait()
    moments = jnp.zeros((local, coeffs), F32)
    for c in range(local):
        found = mm(rounded, maps_v[c], NT)
        moments = jnp.where(row_is(found.shape, c), found, moments)
    moments = moments.astype(BF16)
    mom_v[...] = moments
    home[4].start()
    sent += to_neighbours(mom_v, momw, 3)
    up_copy.wait()
    merged = jnp.zeros((local, coeffs), F32)
    for k in range(local):
        found = mm(moments, ups_v[k], NT)
        merged = jnp.where(row_is(found.shape, k), found, merged)
    grp_v[...] = jnp.sum(merged, axis=0, keepdims=True)
    home[5].start()

    def group_copy(slot, other):
        return pltpu.make_async_remote_copy(
            src_ref=grp_v,
            dst_ref=gmall.at[slot],
            send_sem=gsend.at[other],
            recv_sem=grecv.at[slot],
            device_id=coords(other, devs),
            device_id_type=MESH,
        )

    far_first(me, roles, devs, lambda other: group_copy(me, other).start())
    own_near(
        pos_v, parts, rounded.astype(F32), feat, goal, src, wgt, (sq0, sq1), (g0, g1), acc, base_v
    )
    home[6].start()
    for copy in home + sent:
        copy.wait()
    far_first(me, roles, devs, lambda other: group_copy(other, other).wait())


def near_kernel(
    infoh,
    posh,
    anh,
    denh,
    out,
    info,
    posw,
    anw,
    denw,
    sems,
    feat,
    goal,
    src,
    wgt,
    sq0,
    sq1,
    g0,
    g1,
    acc,
    begin,
    spans,
):
    local, panels = out.shape
    wide = goal.shape[2]
    per_h = panels // wide
    tally = pltpu.make_async_copy(infoh.at[pl.ds(0, SIDES + local)], info, sems.at[2, 0])
    tally.start()
    thick = pltpu.make_async_copy(denh.at[pl.ds(0, SIDES)], denw, sems.at[2, 1])
    order = [RADIUS] + [k for k in range(SIDES) if k != RADIUS]
    loads = []
    for k in order:
        loads.append(pltpu.make_async_copy(posh.at[k], posw.at[k], sems.at[0, k]))
        loads.append(pltpu.make_async_copy(anh.at[k], anw.at[k], sems.at[1, k]))
    for copy in [thick] + loads:
        copy.start()
    thick.wait()
    for n, side in enumerate(order):
        loads[2 * n].wait()
        loads[2 * n + 1].wait()
        fields = anw[side].astype(F32)
        dens = denw[side].astype(F32)
        weights = [fields[a * local : (a + 1) * local] * dens for a in range(3)]
        centres = posw[side].astype(jnp.int32).astype(F32) * (1.0 / FIXED)
        spread_all(feat.at[side], [centres[a] for a in range(3)], weights)
    tally.wait()
    first = info[SIDES, 0, 7]

    def cluster_body(c, start):
        made = goal_rows(read_features(feat.at[RADIUS], c))
        for h in range(per_h):
            goal[per_h * c + h] = made[:, h * wide : (h + 1) * wide]

        def slot_body(s, offset):
            w = info[SIDES + c, 0, 8 + s] - first
            side = w // local
            inner = lax.rem(w, local)
            made, pulled = source_rows(read_features(feat.at[side], inner))
            for b in range(panels // 128):
                src[offset + b] = made[:, b * 128 : (b + 1) * 128]
                wgt[offset + b] = pulled[:, b * 128 : (b + 1) * 128]
            return offset + (info[side, 0, inner] + 127) // 128

        end = lax.fori_loop(0, info[SIDES + c, 0, 6], slot_body, start)
        pad_rows = lax.broadcasted_iota(jnp.int32, (48, 128), 0)
        src[end] = jnp.where(pad_rows >= 44, 1.0, 0.0).astype(BF16)
        wgt[end] = jnp.zeros((16, 128), BF16)
        stop = (end + 1) // 2 * 2
        begin[c] = start // 2
        spans[c] = (info[RADIUS, 0, c] + wide - 1) // wide
        return stop

    end = lax.fori_loop(0, local, cluster_body, 0)
    begin[local] = end // 2
    begin[local + 1] = end // 2
    spans[local] = 1
    acc[...] = jnp.zeros(acc.shape, F32)

    def advance(state):
        c, h, b = state
        over = b + 1 >= begin[jnp.minimum(c + 1, local)]
        h = jnp.where(over, h + 1, h)
        done = h >= spans[c]
        b = jnp.where(over, begin[c], b + 1)
        c_next = jnp.where(done, jnp.minimum(c + 1, local), c)
        b = jnp.where(done, begin[c_next], b)
        return c_next, jnp.where(done, 0, h), b

    def products(state, ref):
        c, h, b = state
        squares(src, b, goal[per_h * c + h], ref)

    def count_body(c, total):
        return total + spans[c] * (begin[c + 1] - begin[c])

    units = lax.fori_loop(0, local, count_body, 0)
    origin = (jnp.int32(0), jnp.int32(0), jnp.int32(0))
    products(origin, sq0)
    cubes(sq0, g0)
    second = advance(origin)
    products(second, sq1)

    def body(many, t, states):
        old, state = states
        for u in range(many):
            later = advance(state)
            products(later, (sq0, sq1)[u % 2])
            cubes((sq1, sq0)[u % 2], (g1, g0)[u % 2])
            c, h, b = old
            acc[per_h * c + h] += gathered(wgt, b, (g0, g1)[u % 2])
            old, state = state, later
        return old, state

    states, left = (origin, second), units
    for many in BODIES[:-1]:
        turns = (left + BODIES[-1] - 1) // many
        states = lax.fori_loop(0, turns, functools.partial(body, many), states)
        left = left - turns * many
    few = BODIES[-1]
    lax.fori_loop(0, (left + few - 1) // few, functools.partial(body, few), states)
    for c in range(local):
        own = read_features(feat.at[RADIUS], c)
        for h in range(per_h):
            part = slice(h * wide, (h + 1) * wide)
            out[c : c + 1, part] = combine(own[:, part], acc[per_h * c + h])


def finish_kernel(
    roles,
    devs,
    live,
    glist,
    gkind,
    llist,
    lkind,
    momw,
    gmall,
    near,
    base,
    kry,
    maps_v,
    ups_v,
    fars_v,
    image_out,
    sums_out,
    red,
    send_sem,
    recv_sem,
):
    me, total = place(roles, devs)
    local, panels = near.shape
    coeffs = maps_v.shape[1]
    kinds = fars_v.shape[1]
    window = SIDES * local
    barrier = greet(me, roles, devs)

    groups = gmall[...].reshape(total, coeffs)
    g_rows = lax.broadcasted_iota(jnp.int32, (kinds, total), 0)
    g_lanes = lax.broadcasted_iota(jnp.int32, (kinds, total), 1)
    g_hot = jnp.zeros((kinds, total), F32)
    for n in range(glist.shape[1]):
        g_hot += jnp.where((g_rows == gkind[:, n : n + 1]) & (g_lanes == glist[:, n : n + 1]), 1.0, 0.0)
    g_hot = g_hot.astype(BF16)
    hi, mid, low = splits(groups)
    g_sum = mm(g_hot, hi.astype(BF16), NN) + mm(g_hot, mid.astype(BF16), NN)
    g_sum += mm(g_hot, low.astype(BF16), NN)
    g_both = halves(g_sum)

    lanes = lax.broadcasted_iota(jnp.int32, (local, window), 1)
    shift = (me - RADIUS) * local
    hots = [jnp.zeros((local, window), F32) for _ in range(kinds)]
    for n in range(llist.shape[1]):
        hit = lanes == (llist[:, n : n + 1] - shift)
        kind = jnp.broadcast_to(lkind[:, n : n + 1], (local, window))
        for o in range(kinds):
            hots[o] = hots[o] + jnp.where(hit & (kind == o), 1.0, 0.0)
    hot = jnp.concatenate(hots, axis=0).astype(BF16)
    held = jnp.concatenate([momw[side].astype(F32) for side in range(SIDES)], axis=0)
    summed = mm(hot, held.astype(BF16), NN)

    g_parts = jnp.zeros((kinds, coeffs), F32)
    for o in range(kinds):
        found = mm(g_both, fars_v[1, o], NT)
        found = found[:kinds] + found[kinds:]
        g_parts = jnp.where(row_is(found.shape, o), found, g_parts)
    g_local = jnp.sum(g_parts, axis=0, keepdims=True).astype(BF16)
    leaf = jnp.zeros((local, coeffs), F32)
    for o in range(kinds):
        found = mm(halves(summed[o * local : (o + 1) * local]), fars_v[0, o], NT)
        leaf = leaf + found[:local] + found[local:]
    g_wide = jnp.broadcast_to(g_local.astype(F32), (local, coeffs)).astype(BF16)
    down = jnp.zeros((local, coeffs), F32)
    for k in range(local):
        found = mm(g_wide, ups_v[k], NN)
        down = jnp.where(row_is(found.shape, k), found, down)
    leaf = (leaf + down).astype(BF16)
    far = jnp.zeros((local, panels), F32)
    for c in range(local):
        found = mm(leaf, maps_v[c], NN)
        far = jnp.where(row_is(found.shape, c), found, far)
    image = jnp.where(live[...] > 0.5, base[...] + near[...] + far, 0.0)

    lane = lax.broadcasted_iota(jnp.int32, (1, 128), 1)
    count = kry.shape[0]
    row = jnp.zeros((1, 128), F32)
    for k in range(count + 1):
        part = image * (kry[k] if k < count else image)
        value = jnp.sum(jnp.sum(part, axis=0, keepdims=True), axis=1, keepdims=True)
        row = jnp.where(lane == k, value, row)
    red[me] = row
    image_out[...] = image
    pl.semaphore_wait(barrier, total - 1)

    def row_copy(slot, other):
        return pltpu.make_async_remote_copy(
            src_ref=red.at[me],
            dst_ref=red.at[slot],
            send_sem=send_sem.at[other],
            recv_sem=recv_sem.at[slot],
            device_id=coords(other, devs),
            device_id_type=MESH,
        )

    far_first(me, roles, devs, lambda other: row_copy(me, other).start())
    far_first(me, roles, devs, lambda other: row_copy(other, other).wait())
    scale = 1.0 / (total * local * panels)
    sums_out[...] = jnp.sum(red[...], axis=0) * scale


def update_kernel(sums_ref, image, kry, nxt, hess):
    count = kry.shape[0]
    sums = sums_ref[...]
    lane = lax.broadcasted_iota(jnp.int32, sums.shape, 1)
    rest = image[...]
    energy = sums[:, count : count + 1]
    for k in range(count):
        c_k = sums[:, k : k + 1]
        rest = rest - c_k * kry[k]
        energy = energy - c_k * c_k
    height = jnp.sqrt(energy + EPSILON)
    nxt[...] = rest / height
    hess[...] = jnp.where(lane == count, height, sums)[:, : count + 1]


def shards(
    roles,
    devs,
    positions,
    normals,
    panel_areas,
    panel_counts,
    near_lists,
    near_counts,
    leaf_lists,
    leaf_kinds,
    group_lists,
    group_kinds,
    block_inverse,
    moment_maps,
    up_operators,
    far_operators,
    krylov_basis,
):
    local, _, panels = positions.shape
    coeffs = moment_maps.shape[1]
    total = roles * devs
    wide = 256
    vmem = pl.BlockSpec(memory_space=pltpu.VMEM)
    smem = pl.BlockSpec(memory_space=pltpu.SMEM)
    hbm = pl.BlockSpec(memory_space=pltpu.HBM)
    dma = pltpu.SemaphoreType.DMA
    posw, anw, denw, cntw, momw, gmall, base, live = pl.pallas_call(
        functools.partial(source_kernel, roles, devs),
        name="sources",
        out_shape=(
            jax.ShapeDtypeStruct((SPARE // (6 * local * panels), 3, local, panels), jnp.int16),
            jax.ShapeDtypeStruct((SPARE // (6 * local * panels), 3 * local, panels), BF16),
            jax.ShapeDtypeStruct((SPARE // (2 * local * panels), local, panels), BF16),
            jax.ShapeDtypeStruct((SPARE // 512, 1, 128), jnp.int32),
            jax.ShapeDtypeStruct((SIDES, local, coeffs), BF16),
            jax.ShapeDtypeStruct((total, 1, coeffs), F32),
            jax.ShapeDtypeStruct((local, panels), F32),
            jax.ShapeDtypeStruct((local, panels), F32),
        ),
        in_specs=[hbm] * 10,
        out_specs=(hbm,) * 8,
        scratch_shapes=[
            pltpu.SMEM(panel_counts.shape, jnp.int32),
            pltpu.SMEM(near_lists.shape, jnp.int32),
            pltpu.SMEM(near_counts.shape, jnp.int32),
            pltpu.VMEM((local, coeffs), BF16),
            pltpu.VMEM((1, coeffs), F32),
            pltpu.VMEM((local, panels), F32),
            pltpu.VMEM((local, panels), F32),
            pltpu.VMEM((3, local, panels), F32),
            pltpu.VMEM((3, local, panels), jnp.int16),
            pltpu.VMEM((3 * local, panels), BF16),
            pltpu.VMEM((local, panels), BF16),
            pltpu.VMEM((1, 128), jnp.int32),
            pltpu.VMEM((local, 1, 128), jnp.int32),
            pltpu.VMEM((3, local, panels), F32),
            pltpu.VMEM((local, panels), F32),
            pltpu.VMEM((local, panels), F32),
            pltpu.VMEM(block_inverse.shape, BF16),
            pltpu.VMEM(moment_maps.shape, BF16),
            pltpu.VMEM(up_operators.shape, BF16),
            dma((18,)),
            dma((local,)),
            dma((5, 6)),
            dma((5, 6)),
            dma((total,)),
            dma((total,)),
            pltpu.VMEM((panels // 128, 8 * local, 128), F32),
            pltpu.VMEM((local * (panels // wide), 48, wide), BF16),
            pltpu.VMEM((local * (panels // 128), 48, 128), BF16),
            pltpu.VMEM((local * (panels // 128), 16, 128), BF16),
            pltpu.VMEM((256, wide), F32),
            pltpu.VMEM((256, wide), F32),
            pltpu.VMEM((256, wide), BF16),
            pltpu.VMEM((256, wide), BF16),
            pltpu.VMEM((local * (panels // wide), 16, wide), F32),
        ],
        compiler_params=pltpu.CompilerParams(
            collective_id=0, has_side_effects=True, vmem_limit_bytes=62 << 20
        ),
    )(
        panel_counts,
        near_lists,
        near_counts,
        jnp.transpose(positions, (1, 0, 2)),
        jnp.transpose(normals, (1, 0, 2)),
        panel_areas,
        krylov_basis,
        block_inverse,
        moment_maps,
        up_operators,
    )
    room = local * (near_lists.shape[1] * (panels // 128) + 1) + 8
    goals = (local + 1) * (panels // wide)
    near = pl.pallas_call(
        near_kernel,
        name="near",
        cost_estimate=pl.CostEstimate(
            flops=40 * local * panels * panels * (near_lists.shape[1] + 1),
            bytes_accessed=48 * local * panels * SIDES,
            transcendentals=local * panels * panels * (near_lists.shape[1] + 1),
        ),
        out_shape=jax.ShapeDtypeStruct((local, panels), F32),
        in_specs=[hbm] * 4,
        out_specs=vmem,
        scratch_shapes=[
            pltpu.SMEM((SIDES + local, 1, 128), jnp.int32),
            pltpu.VMEM((SIDES, 3, local, panels), jnp.int16),
            pltpu.VMEM((SIDES, 3 * local, panels), BF16),
            pltpu.VMEM((SIDES, local, panels), BF16),
            dma((3, SIDES)),
            pltpu.VMEM((SIDES, panels // 128, 8 * local, 128), F32),
            pltpu.VMEM((goals, 48, wide), BF16),
            pltpu.VMEM((room, 48, 128), BF16),
            pltpu.VMEM((room, 16, 128), BF16),
            pltpu.VMEM((256, wide), F32),
            pltpu.VMEM((256, wide), F32),
            pltpu.VMEM((256, wide), BF16),
            pltpu.VMEM((256, wide), BF16),
            pltpu.VMEM((goals, 16, wide), F32),
            pltpu.SMEM((local + 2,), jnp.int32),
            pltpu.SMEM((local + 2,), jnp.int32),
        ],
        compiler_params=pltpu.CompilerParams(vmem_limit_bytes=52 << 20),
    )(cntw, posw, anw, denw)
    image, sums = pl.pallas_call(
        functools.partial(finish_kernel, roles, devs),
        name="finish",
        out_shape=(
            jax.ShapeDtypeStruct((local, panels), F32),
            jax.ShapeDtypeStruct((1, 128), F32),
        ),
        in_specs=[vmem] * 13,
        out_specs=(vmem, vmem),
        scratch_shapes=[
            pltpu.VMEM((total, 1, 128), F32),
            dma((total,)),
            dma((total,)),
        ],
        compiler_params=pltpu.CompilerParams(
            collective_id=1, has_side_effects=True, vmem_limit_bytes=14 << 20
        ),
    )(
        live,
        group_lists,
        group_kinds,
        leaf_lists,
        leaf_kinds,
        momw,
        gmall,
        near,
        base,
        krylov_basis,
        moment_maps,
        up_operators,
        far_operators,
    )
    nxt, hess = pl.pallas_call(
        update_kernel,
        name="update",
        out_shape=(
            jax.ShapeDtypeStruct((local, panels), F32),
            jax.ShapeDtypeStruct((1, krylov_basis.shape[0] + 1), F32),
        ),
        in_specs=[vmem] * 3,
        out_specs=(vmem, vmem),
        compiler_params=pltpu.CompilerParams(vmem_limit_bytes=8 << 20),
    )(sums, image, krylov_basis)
    return nxt, jnp.reshape(hess, (krylov_basis.shape[0] + 1,))


def solution(mesh):
    roles, devs = mesh.shape["role"], mesh.shape["dev"]
    return jax.shard_map(
        functools.partial(shards, roles, devs),
        mesh=mesh,
        in_specs=(
            P(AXES, None, None),
            P(AXES, None, None),
            P(AXES, None),
            P(AXES),
            P(AXES, None),
            P(AXES),
            P(AXES, None),
            P(AXES, None),
            P(AXES, None),
            P(AXES, None),
            P(AXES, None, None),
            P(AXES, None, None),
            P(),
            P(),
            P(None, AXES, None),
        ),
        out_specs=(P(AXES, None), P()),
        check_vma=False,
    )
```

```python
import functools

import jax
import jax.numpy as jnp
from jax import lax
from jax.experimental import pallas as pl
from jax.experimental.pallas import tpu as pltpu
from jax.sharding import PartitionSpec as P

RADIUS = 3
SIDES = 2 * RADIUS + 1
SOFTEN = 0.01
EPSILON = 1e-06
BODIES = (48, 16, 8)
SPARE = 12 << 20
FIXED = 32767.0
MESH = pl.DeviceIdType.MESH
NT = (((1,), (1,)), ((), ()))
NN = (((1,), (0,)), ((), ()))
TN = (((0,), (0,)), ((), ()))
F32 = jnp.float32
BF16 = jnp.bfloat16
AXES = ("role", "dev")


def mm(a, b, dims):
    return lax.dot_general(a, b, dims, preferred_element_type=F32)


def row_is(shape, k):
    return lax.broadcasted_iota(jnp.int32, shape, 0) == k


def place(roles, devs):
    me = lax.axis_index("role") * devs + lax.axis_index("dev")
    return me, roles * devs


def coords(linear, devs):
    return (linear // devs, lax.rem(linear, devs))


def far_first(me, roles, devs, visit):
    own = lax.rem(me, devs)

    def body(t, ends):
        low, high = ends
        left = own - low >= high - own
        other = jnp.where(left, low, high)
        for r in range(roles):
            visit(r * devs + other)
        return jnp.where(left, low + 1, low), jnp.where(left, high, high - 1)

    ends = (jnp.int32(0), jnp.int32(devs - 1))
    for t in range(devs - 1):
        ends = body(t, ends)
    for r in range(1, roles):
        visit(lax.rem(me + r * devs, roles * devs))


def greet(me, roles, devs):
    barrier = pltpu.get_barrier_semaphore()

    def visit(other):
        pl.semaphore_signal(barrier, inc=1, device_id=coords(other, devs), device_id_type=MESH)

    far_first(me, roles, devs, visit)
    return barrier


def live_mask(cnt_ref, shape):
    rows = lax.broadcasted_iota(jnp.int32, shape, 0)
    limit = jnp.zeros(shape, jnp.int32)
    for c in range(shape[0]):
        limit = jnp.where(rows == c, cnt_ref[c], limit)
    return lax.broadcasted_iota(jnp.int32, shape, 1) < limit


def halves(x):
    hi = x.astype(BF16).astype(F32)
    return jnp.concatenate([hi, x - hi], axis=0).astype(BF16)


def splits(x):
    hi = x.astype(BF16).astype(F32)
    rest = x - hi
    mid = rest.astype(BF16).astype(F32)
    return hi, mid, rest - mid


def pack(parts):
    return jnp.concatenate(parts, axis=0).astype(BF16)


def spread_all(feat, positions, weights):
    local, panels = positions[0].shape
    norm = jnp.zeros((local, panels), F32)
    inside = jnp.zeros((local, panels), F32)
    for y, w in zip(positions, weights):
        norm = norm + y * y
        inside = inside - y * w
    rows = list(positions) + [norm] + list(weights) + [inside]
    for k, value in enumerate(rows):
        for b in range(panels // 128):
            feat[b, k * local : (k + 1) * local, :] = value[:, b * 128 : (b + 1) * 128]


def read_features(feat, inner):
    at = pl.ds(inner, 8, stride=feat.shape[1] // 8)
    return jnp.concatenate([feat[b, at, :] for b in range(feat.shape[0])], axis=1)


def goal_rows(own):
    shape = own.shape
    rows = lax.broadcasted_iota(jnp.int32, shape, 0)
    x = jnp.where(rows < 3, -2.0 * own, jnp.where(rows == 3, own + SOFTEN, 0.0))
    hi, mid, low = splits(x)
    norms = [jnp.broadcast_to(part[3:4], shape) for part in (hi, mid, low)]
    firm = jnp.where(rows < 3, hi, jnp.where(rows == 3, 1.0, 0.0))
    soft = jnp.where(rows < 3, mid, 0.0)
    last = jnp.where(rows < 3, low, 0.0)
    tail = soft
    for k in range(3):
        tail = jnp.where(rows == 4 + k, norms[k], tail)
    return pack([firm, firm, firm, soft, last, tail])


def source_rows(own):
    rows = lax.broadcasted_iota(jnp.int32, own.shape, 0)
    hi, mid, low = splits(own)
    made = pack([hi, mid, low, hi, hi, jnp.where(rows < 4, mid, 1.0)])
    return made, pack([jnp.where(rows < 4, pltpu.roll(mid, 4, 0), hi), low])


def squares(src, block, target, ref):
    for k in range(2):
        ref[k * 128 : (k + 1) * 128, :] = mm(src[2 * block + k], target, TN)


def cubes(a, b):
    inverse = lax.rsqrt(a[...])
    b[...] = (inverse * inverse * inverse).astype(BF16)


def gathered(wgt, block, ref):
    both = jnp.concatenate([wgt[2 * block], wgt[2 * block + 1]], axis=1)
    return mm(both, ref[...], NN)


def combine(own, got):
    total = got[:8] + pltpu.roll(got[:8], 4, 0) + got[8:]
    rows = lax.broadcasted_iota(jnp.int32, total.shape, 0)
    part = total * pltpu.roll(own, 4, 0)
    value = jnp.where(rows < 4, 0.0, jnp.where(rows == 7, total, part))
    return jnp.sum(value, axis=0, keepdims=True)


def own_near(pos_v, nrm_parts, density, feat, goal, src, wgt, sqs, gs, acc, out):
    local, panels = density.shape
    wide = goal.shape[2]
    per_h = panels // wide
    blocks = panels // 256
    positions = [pos_v[a] for a in range(3)]
    spread_all(feat, positions, [part * density for part in nrm_parts])
    for c in range(local):
        own = read_features(feat, c)
        made = goal_rows(own)
        for h in range(per_h):
            goal[per_h * c + h] = made[:, h * wide : (h + 1) * wide]
        made, pulled = source_rows(own)
        for b in range(panels // 128):
            src[2 * blocks * c + b] = made[:, b * 128 : (b + 1) * 128]
            wgt[2 * blocks * c + b] = pulled[:, b * 128 : (b + 1) * 128]
    acc[...] = jnp.zeros(acc.shape, F32)
    units = local * per_h * blocks

    def place_of(n):
        n = lax.rem(n, units)
        c = n // (per_h * blocks)
        return n // blocks, c * blocks + lax.rem(n, blocks)

    def start(n, ref):
        g, b = place_of(n)
        squares(src, b, goal[g], ref)

    start(0, sqs[0])
    cubes(sqs[0], gs[0])
    start(1, sqs[1])
    steps = 16

    def body(t, carry):
        for u in range(steps):
            n = t * steps + u
            start(n + 2, sqs[u % 2])
            cubes(sqs[(u + 1) % 2], gs[(u + 1) % 2])
            g, b = place_of(n)
            acc[g] += gathered(wgt, b, gs[u % 2])
        return carry

    lax.fori_loop(0, units // steps, body, 0)
    for c in range(local):
        own = read_features(feat, c)
        for h in range(per_h):
            part = slice(h * wide, (h + 1) * wide)
            out[c : c + 1, part] = out[c : c + 1, part] + combine(own[:, part], acc[per_h * c + h])


def source_kernel(
    roles,
    devs,
    cnth,
    nearh,
    usedh,
    pos,
    nrm,
    area,
    kry,
    binv,
    maps,
    ups,
    posw,
    anw,
    denw,
    cntw,
    momw,
    gmall,
    base,
    mask,
    cnt,
    near,
    used,
    mom_v,
    grp_v,
    base_v,
    mask_v,
    pos_v,
    fix_v,
    an_v,
    den_v,
    cnt_v,
    info_v,
    nrm_v,
    area_v,
    kry_v,
    binv_v,
    maps_v,
    ups_v,
    local_sem,
    big_sem,
    send_sem,
    recv_sem,
    gsend,
    grecv,
    feat,
    goal,
    src,
    wgt,
    sq0,
    sq1,
    g0,
    g1,
    acc,
):
    me, total = place(roles, devs)
    local, panels = area.shape
    coeffs = maps_v.shape[1]
    barrier = greet(me, roles, devs)
    copies = []
    for c in range(local):
        copies.append(pltpu.make_async_copy(binv.at[c], binv_v.at[c], big_sem.at[c]))
    map_copy = pltpu.make_async_copy(maps, maps_v, local_sem.at[0])
    up_copy = pltpu.make_async_copy(ups, ups_v, local_sem.at[1])
    small = [
        pltpu.make_async_copy(cnth, cnt, local_sem.at[13]),
        pltpu.make_async_copy(nearh, near, local_sem.at[14]),
        pltpu.make_async_copy(usedh, used, local_sem.at[15]),
        pltpu.make_async_copy(pos, pos_v, local_sem.at[2]),
        pltpu.make_async_copy(nrm, nrm_v, local_sem.at[3]),
        pltpu.make_async_copy(area, area_v, local_sem.at[4]),
        pltpu.make_async_copy(kry.at[kry.shape[0] - 1], kry_v, local_sem.at[5]),
    ]
    for copy in small + copies:
        copy.start()
    home = [
        pltpu.make_async_copy(fix_v, posw.at[RADIUS], local_sem.at[6]),
        pltpu.make_async_copy(an_v, anw.at[RADIUS], local_sem.at[7]),
        pltpu.make_async_copy(cnt_v, cntw.at[RADIUS], local_sem.at[8]),
        pltpu.make_async_copy(info_v, cntw.at[pl.ds(SIDES, local)], local_sem.at[9]),
        pltpu.make_async_copy(mom_v, momw.at[RADIUS], local_sem.at[10]),
        pltpu.make_async_copy(grp_v, gmall.at[me], local_sem.at[11]),
        pltpu.make_async_copy(base_v, base, local_sem.at[12]),
        pltpu.make_async_copy(mask_v, mask, local_sem.at[16]),
        pltpu.make_async_copy(den_v, denw.at[RADIUS], local_sem.at[17]),
    ]
    map_copy.start()
    up_copy.start()
    for copy in small:
        copy.wait()
    fix_v[...] = jnp.floor(pos_v[...] * FIXED + 0.5).astype(jnp.int32).astype(jnp.int16)
    home[0].start()
    parts = [(nrm_v[a] * area_v[...]).astype(BF16).astype(F32) for a in range(3)]
    an_v[...] = jnp.concatenate(parts, axis=0).astype(BF16)
    home[1].start()
    lane = lax.broadcasted_iota(jnp.int32, (1, 128), 1)
    counts = jnp.zeros((1, 128), jnp.int32)
    for c in range(local):
        counts = jnp.where(lane == c, cnt[c], counts)
    cnt_v[...] = counts
    home[2].start()
    for c in range(local):
        row = jnp.where(lane == 6, used[c], (me - RADIUS) * local)
        for n in range(near.shape[1]):
            row = jnp.where(lane == 8 + n, near[c, n], row)
        info_v[c] = row
    home[3].start()
    pl.semaphore_wait(barrier, total - 1)

    def to_neighbours(own, ref, kind):
        made = []
        for n, d in enumerate([3, -3, 2, -2, 1, -1]):
            made.append(
                pltpu.make_async_remote_copy(
                    src_ref=own,
                    dst_ref=ref.at[RADIUS - d],
                    send_sem=send_sem.at[kind, n],
                    recv_sem=recv_sem.at[kind, n],
                    device_id=coords(lax.rem(me + d + total, total), devs),
                    device_id_type=MESH,
                )
            )
        for copy in made:
            copy.start()
        return made

    sent = to_neighbours(fix_v, posw, 0)
    sent += to_neighbours(an_v, anw, 4)
    sent += to_neighbours(cnt_v, cntw, 1)
    live = live_mask(cnt, (local, panels))
    current = kry_v[...].astype(BF16)
    density = jnp.zeros((local, panels), F32)
    for c in range(local):
        copies[c].wait()
        found = mm(current, binv_v[c], NT)
        density = jnp.where(row_is(found.shape, c), found, density)
    rounded = jnp.where(live, density, 0.0).astype(BF16)
    den_v[...] = rounded
    base_v[...] = 0.5 * rounded.astype(F32)
    mask_v[...] = jnp.where(live, 1.0, 0.0)
    home[7].start()
    home[8].start()
    sent += to_neighbours(den_v, denw, 2)
    map_copy.wait()
    moments = jnp.zeros((local, coeffs), F32)
    for c in range(local):
        found = mm(rounded, maps_v[c], NT)
        moments = jnp.where(row_is(found.shape, c), found, moments)
    moments = moments.astype(BF16)
    mom_v[...] = moments
    home[4].start()
    sent += to_neighbours(mom_v, momw, 3)
    up_copy.wait()
    merged = jnp.zeros((local, coeffs), F32)
    for k in range(local):
        found = mm(moments, ups_v[k], NT)
        merged = jnp.where(row_is(found.shape, k), found, merged)
    grp_v[...] = jnp.sum(merged, axis=0, keepdims=True)
    home[5].start()

    def group_copy(slot, other):
        return pltpu.make_async_remote_copy(
            src_ref=grp_v,
            dst_ref=gmall.at[slot],
            send_sem=gsend.at[other],
            recv_sem=grecv.at[slot],
            device_id=coords(other, devs),
            device_id_type=MESH,
        )

    far_first(me, roles, devs, lambda other: group_copy(me, other).start())
    own_near(
        pos_v, parts, rounded.astype(F32), feat, goal, src, wgt, (sq0, sq1), (g0, g1), acc, base_v
    )
    home[6].start()
    for copy in home + sent:
        copy.wait()
    far_first(me, roles, devs, lambda other: group_copy(other, other).wait())


def near_kernel(
    infoh,
    posh,
    anh,
    denh,
    out,
    info,
    posw,
    anw,
    denw,
    sems,
    feat,
    goal,
    src,
    wgt,
    sq0,
    sq1,
    g0,
    g1,
    acc,
    begin,
    spans,
):
    local, panels = out.shape
    wide = goal.shape[2]
    per_h = panels // wide
    tally = pltpu.make_async_copy(infoh.at[pl.ds(0, SIDES + local)], info, sems.at[2, 0])
    tally.start()
    thick = pltpu.make_async_copy(denh.at[pl.ds(0, SIDES)], denw, sems.at[2, 1])
    order = [RADIUS] + [k for k in range(SIDES) if k != RADIUS]
    loads = []
    for k in order:
        loads.append(pltpu.make_async_copy(posh.at[k], posw.at[k], sems.at[0, k]))
        loads.append(pltpu.make_async_copy(anh.at[k], anw.at[k], sems.at[1, k]))
    for copy in [thick] + loads:
        copy.start()
    thick.wait()
    for n, side in enumerate(order):
        loads[2 * n].wait()
        loads[2 * n + 1].wait()
        fields = anw[side].astype(F32)
        dens = denw[side].astype(F32)
        weights = [fields[a * local : (a + 1) * local] * dens for a in range(3)]
        centres = posw[side].astype(jnp.int32).astype(F32) * (1.0 / FIXED)
        spread_all(feat.at[side], [centres[a] for a in range(3)], weights)
    tally.wait()
    first = info[SIDES, 0, 7]

    def cluster_body(c, start):
        made = goal_rows(read_features(feat.at[RADIUS], c))
        for h in range(per_h):
            goal[per_h * c + h] = made[:, h * wide : (h + 1) * wide]

        def slot_body(s, offset):
            w = info[SIDES + c, 0, 8 + s] - first
            side = w // local
            inner = lax.rem(w, local)
            made, pulled = source_rows(read_features(feat.at[side], inner))
            for b in range(panels // 128):
                src[offset + b] = made[:, b * 128 : (b + 1) * 128]
                wgt[offset + b] = pulled[:, b * 128 : (b + 1) * 128]
            return offset + (info[side, 0, inner] + 127) // 128

        end = lax.fori_loop(0, info[SIDES + c, 0, 6], slot_body, start)
        pad_rows = lax.broadcasted_iota(jnp.int32, (48, 128), 0)
        src[end] = jnp.where(pad_rows >= 44, 1.0, 0.0).astype(BF16)
        wgt[end] = jnp.zeros((16, 128), BF16)
        stop = (end + 1) // 2 * 2
        begin[c] = start // 2
        spans[c] = (info[RADIUS, 0, c] + wide - 1) // wide
        return stop

    end = lax.fori_loop(0, local, cluster_body, 0)
    begin[local] = end // 2
    begin[local + 1] = end // 2
    spans[local] = 1
    acc[...] = jnp.zeros(acc.shape, F32)

    def advance(state):
        c, h, b = state
        over = b + 1 >= begin[jnp.minimum(c + 1, local)]
        h = jnp.where(over, h + 1, h)
        done = h >= spans[c]
        b = jnp.where(over, begin[c], b + 1)
        c_next = jnp.where(done, jnp.minimum(c + 1, local), c)
        b = jnp.where(done, begin[c_next], b)
        return c_next, jnp.where(done, 0, h), b

    def products(state, ref):
        c, h, b = state
        squares(src, b, goal[per_h * c + h], ref)

    def count_body(c, total):
        return total + spans[c] * (begin[c + 1] - begin[c])

    units = lax.fori_loop(0, local, count_body, 0)
    origin = (jnp.int32(0), jnp.int32(0), jnp.int32(0))
    products(origin, sq0)
    cubes(sq0, g0)
    second = advance(origin)
    products(second, sq1)

    def body(many, t, states):
        old, state = states
        for u in range(many):
            later = advance(state)
            products(later, (sq0, sq1)[u % 2])
            cubes((sq1, sq0)[u % 2], (g1, g0)[u % 2])
            c, h, b = old
            acc[per_h * c + h] += gathered(wgt, b, (g0, g1)[u % 2])
            old, state = state, later
        return old, state

    states, left = (origin, second), units
    for many in BODIES[:-1]:
        turns = (left + BODIES[-1] - 1) // many
        states = lax.fori_loop(0, turns, functools.partial(body, many), states)
        left = left - turns * many
    few = BODIES[-1]
    lax.fori_loop(0, (left + few - 1) // few, functools.partial(body, few), states)
    for c in range(local):
        own = read_features(feat.at[RADIUS], c)
        for h in range(per_h):
            part = slice(h * wide, (h + 1) * wide)
            out[c : c + 1, part] = combine(own[:, part], acc[per_h * c + h])


def finish_kernel(
    roles,
    devs,
    live,
    glist,
    gkind,
    llist,
    lkind,
    momw,
    gmall,
    near,
    base,
    kry,
    maps_v,
    ups_v,
    fars_v,
    image_out,
    sums_out,
    red,
    send_sem,
    recv_sem,
):
    me, total = place(roles, devs)
    local, panels = near.shape
    coeffs = maps_v.shape[1]
    kinds = fars_v.shape[1]
    window = SIDES * local
    barrier = greet(me, roles, devs)

    groups = gmall[...].reshape(total, coeffs)
    g_rows = lax.broadcasted_iota(jnp.int32, (kinds, total), 0)
    g_lanes = lax.broadcasted_iota(jnp.int32, (kinds, total), 1)
    g_hot = jnp.zeros((kinds, total), F32)
    for n in range(glist.shape[1]):
        g_hot += jnp.where((g_rows == gkind[:, n : n + 1]) & (g_lanes == glist[:, n : n + 1]), 1.0, 0.0)
    g_hot = g_hot.astype(BF16)
    hi, mid, low = splits(groups)
    g_sum = mm(g_hot, hi.astype(BF16), NN) + mm(g_hot, mid.astype(BF16), NN)
    g_sum += mm(g_hot, low.astype(BF16), NN)
    g_both = halves(g_sum)

    lanes = lax.broadcasted_iota(jnp.int32, (local, window), 1)
    shift = (me - RADIUS) * local
    hots = [jnp.zeros((local, window), F32) for _ in range(kinds)]
    for n in range(llist.shape[1]):
        hit = lanes == (llist[:, n : n + 1] - shift)
        kind = jnp.broadcast_to(lkind[:, n : n + 1], (local, window))
        for o in range(kinds):
            hots[o] = hots[o] + jnp.where(hit & (kind == o), 1.0, 0.0)
    hot = jnp.concatenate(hots, axis=0).astype(BF16)
    held = jnp.concatenate([momw[side].astype(F32) for side in range(SIDES)], axis=0)
    summed = mm(hot, held.astype(BF16), NN)

    g_parts = jnp.zeros((kinds, coeffs), F32)
    for o in range(kinds):
        found = mm(g_both, fars_v[1, o], NT)
        found = found[:kinds] + found[kinds:]
        g_parts = jnp.where(row_is(found.shape, o), found, g_parts)
    g_local = jnp.sum(g_parts, axis=0, keepdims=True).astype(BF16)
    leaf = jnp.zeros((local, coeffs), F32)
    for o in range(kinds):
        found = mm(halves(summed[o * local : (o + 1) * local]), fars_v[0, o], NT)
        leaf = leaf + found[:local] + found[local:]
    g_wide = jnp.broadcast_to(g_local.astype(F32), (local, coeffs)).astype(BF16)
    down = jnp.zeros((local, coeffs), F32)
    for k in range(local):
        found = mm(g_wide, ups_v[k], NN)
        down = jnp.where(row_is(found.shape, k), found, down)
    leaf = (leaf + down).astype(BF16)
    far = jnp.zeros((local, panels), F32)
    for c in range(local):
        found = mm(leaf, maps_v[c], NN)
        far = jnp.where(row_is(found.shape, c), found, far)
    image = jnp.where(live[...] > 0.5, base[...] + near[...] + far, 0.0)

    lane = lax.broadcasted_iota(jnp.int32, (1, 128), 1)
    count = kry.shape[0]
    row = jnp.zeros((1, 128), F32)
    for k in range(count + 1):
        part = image * (kry[k] if k < count else image)
        value = jnp.sum(jnp.sum(part, axis=0, keepdims=True), axis=1, keepdims=True)
        row = jnp.where(lane == k, value, row)
    red[me] = row
    image_out[...] = image
    pl.semaphore_wait(barrier, total - 1)

    def row_copy(slot, other):
        return pltpu.make_async_remote_copy(
            src_ref=red.at[me],
            dst_ref=red.at[slot],
            send_sem=send_sem.at[other],
            recv_sem=recv_sem.at[slot],
            device_id=coords(other, devs),
            device_id_type=MESH,
        )

    far_first(me, roles, devs, lambda other: row_copy(me, other).start())
    far_first(me, roles, devs, lambda other: row_copy(other, other).wait())
    scale = 1.0 / (total * local * panels)
    sums_out[...] = jnp.sum(red[...], axis=0) * scale


def update_kernel(sums_ref, image, kry, nxt, hess):
    count = kry.shape[0]
    sums = sums_ref[...]
    lane = lax.broadcasted_iota(jnp.int32, sums.shape, 1)
    rest = image[...]
    energy = sums[:, count : count + 1]
    for k in range(count):
        c_k = sums[:, k : k + 1]
        rest = rest - c_k * kry[k]
        energy = energy - c_k * c_k
    height = jnp.sqrt(energy + EPSILON)
    nxt[...] = rest / height
    hess[...] = jnp.where(lane == count, height, sums)[:, : count + 1]


def shards(
    roles,
    devs,
    positions,
    normals,
    panel_areas,
    panel_counts,
    near_lists,
    near_counts,
    leaf_lists,
    leaf_kinds,
    group_lists,
    group_kinds,
    block_inverse,
    moment_maps,
    up_operators,
    far_operators,
    krylov_basis,
):
    local, _, panels = positions.shape
    coeffs = moment_maps.shape[1]
    total = roles * devs
    wide = 256
    vmem = pl.BlockSpec(memory_space=pltpu.VMEM)
    smem = pl.BlockSpec(memory_space=pltpu.SMEM)
    hbm = pl.BlockSpec(memory_space=pltpu.HBM)
    dma = pltpu.SemaphoreType.DMA
    posw, anw, denw, cntw, momw, gmall, base, live = pl.pallas_call(
        functools.partial(source_kernel, roles, devs),
        name="sources",
        out_shape=(
            jax.ShapeDtypeStruct((SPARE // (6 * local * panels), 3, local, panels), jnp.int16),
            jax.ShapeDtypeStruct((SPARE // (6 * local * panels), 3 * local, panels), BF16),
            jax.ShapeDtypeStruct((SPARE // (2 * local * panels), local, panels), BF16),
            jax.ShapeDtypeStruct((SPARE // 512, 1, 128), jnp.int32),
            jax.ShapeDtypeStruct((SIDES, local, coeffs), BF16),
            jax.ShapeDtypeStruct((total, 1, coeffs), F32),
            jax.ShapeDtypeStruct((local, panels), F32),
            jax.ShapeDtypeStruct((local, panels), F32),
        ),
        in_specs=[hbm] * 10,
        out_specs=(hbm,) * 8,
        scratch_shapes=[
            pltpu.SMEM(panel_counts.shape, jnp.int32),
            pltpu.SMEM(near_lists.shape, jnp.int32),
            pltpu.SMEM(near_counts.shape, jnp.int32),
            pltpu.VMEM((local, coeffs), BF16),
            pltpu.VMEM((1, coeffs), F32),
            pltpu.VMEM((local, panels), F32),
            pltpu.VMEM((local, panels), F32),
            pltpu.VMEM((3, local, panels), F32),
            pltpu.VMEM((3, local, panels), jnp.int16),
            pltpu.VMEM((3 * local, panels), BF16),
            pltpu.VMEM((local, panels), BF16),
            pltpu.VMEM((1, 128), jnp.int32),
            pltpu.VMEM((local, 1, 128), jnp.int32),
            pltpu.VMEM((3, local, panels), F32),
            pltpu.VMEM((local, panels), F32),
            pltpu.VMEM((local, panels), F32),
            pltpu.VMEM(block_inverse.shape, BF16),
            pltpu.VMEM(moment_maps.shape, BF16),
            pltpu.VMEM(up_operators.shape, BF16),
            dma((18,)),
            dma((local,)),
            dma((5, 6)),
            dma((5, 6)),
            dma((total,)),
            dma((total,)),
            pltpu.VMEM((panels // 128, 8 * local, 128), F32),
            pltpu.VMEM((local * (panels // wide), 48, wide), BF16),
            pltpu.VMEM((local * (panels // 128), 48, 128), BF16),
            pltpu.VMEM((local * (panels // 128), 16, 128), BF16),
            pltpu.VMEM((256, wide), F32),
            pltpu.VMEM((256, wide), F32),
            pltpu.VMEM((256, wide), BF16),
            pltpu.VMEM((256, wide), BF16),
            pltpu.VMEM((local * (panels // wide), 16, wide), F32),
        ],
        compiler_params=pltpu.CompilerParams(
            collective_id=0, has_side_effects=True, vmem_limit_bytes=62 << 20
        ),
    )(
        panel_counts,
        near_lists,
        near_counts,
        jnp.transpose(positions, (1, 0, 2)),
        jnp.transpose(normals, (1, 0, 2)),
        panel_areas,
        krylov_basis,
        block_inverse,
        moment_maps,
        up_operators,
    )
    room = local * (near_lists.shape[1] * (panels // 128) + 1) + 8
    goals = (local + 1) * (panels // wide)
    near = pl.pallas_call(
        near_kernel,
        name="near",
        cost_estimate=pl.CostEstimate(
            flops=40 * local * panels * panels * (near_lists.shape[1] + 1),
            bytes_accessed=48 * local * panels * SIDES,
            transcendentals=local * panels * panels * (near_lists.shape[1] + 1),
        ),
        out_shape=jax.ShapeDtypeStruct((local, panels), F32),
        in_specs=[hbm] * 4,
        out_specs=vmem,
        scratch_shapes=[
            pltpu.SMEM((SIDES + local, 1, 128), jnp.int32),
            pltpu.VMEM((SIDES, 3, local, panels), jnp.int16),
            pltpu.VMEM((SIDES, 3 * local, panels), BF16),
            pltpu.VMEM((SIDES, local, panels), BF16),
            dma((3, SIDES)),
            pltpu.VMEM((SIDES, panels // 128, 8 * local, 128), F32),
            pltpu.VMEM((goals, 48, wide), BF16),
            pltpu.VMEM((room, 48, 128), BF16),
            pltpu.VMEM((room, 16, 128), BF16),
            pltpu.VMEM((256, wide), F32),
            pltpu.VMEM((256, wide), F32),
            pltpu.VMEM((256, wide), BF16),
            pltpu.VMEM((256, wide), BF16),
            pltpu.VMEM((goals, 16, wide), F32),
            pltpu.SMEM((local + 2,), jnp.int32),
            pltpu.SMEM((local + 2,), jnp.int32),
        ],
        compiler_params=pltpu.CompilerParams(vmem_limit_bytes=52 << 20),
    )(cntw, posw, anw, denw)
    image, sums = pl.pallas_call(
        functools.partial(finish_kernel, roles, devs),
        name="finish",
        out_shape=(
            jax.ShapeDtypeStruct((local, panels), F32),
            jax.ShapeDtypeStruct((1, 128), F32),
        ),
        in_specs=[vmem] * 13,
        out_specs=(vmem, vmem),
        scratch_shapes=[
            pltpu.VMEM((total, 1, 128), F32),
            dma((total,)),
            dma((total,)),
        ],
        compiler_params=pltpu.CompilerParams(
            collective_id=1, has_side_effects=True, vmem_limit_bytes=14 << 20
        ),
    )(
        live,
        group_lists,
        group_kinds,
        leaf_lists,
        leaf_kinds,
        momw,
        gmall,
        near,
        base,
        krylov_basis,
        moment_maps,
        up_operators,
        far_operators,
    )
    nxt, hess = pl.pallas_call(
        update_kernel,
        name="update",
        out_shape=(
            jax.ShapeDtypeStruct((local, panels), F32),
            jax.ShapeDtypeStruct((1, krylov_basis.shape[0] + 1), F32),
        ),
        in_specs=[vmem] * 3,
        out_specs=(vmem, vmem),
        compiler_params=pltpu.CompilerParams(vmem_limit_bytes=8 << 20),
    )(sums, image, krylov_basis)
    return nxt, jnp.reshape(hess, (krylov_basis.shape[0] + 1,))


def solution(mesh):
    roles, devs = mesh.shape["role"], mesh.shape["dev"]
    return jax.shard_map(
        functools.partial(shards, roles, devs),
        mesh=mesh,
        in_specs=(
            P(AXES, None, None),
            P(AXES, None, None),
            P(AXES, None),
            P(AXES),
            P(AXES, None),
            P(AXES),
            P(AXES, None),
            P(AXES, None),
            P(AXES, None),
            P(AXES, None),
            P(AXES, None, None),
            P(AXES, None, None),
            P(),
            P(),
            P(None, AXES, None),
        ),
        out_specs=(P(AXES, None), P()),
        check_vma=False,
    )
```
